512 devices in a mesh: box: 32 (over x, y, core), dir: 16 (over z).
Axes of the slice: x: 4, y: 4, z: 16, core: 2. Of those that a mesh axis runs over, the one named last changes fastest.
Arguments:
- outgoing: float32 [2048, 8, 2048], P(('box', 'dir')), may hold values from -6 to 6
- fine_slot: int32 [2048], P('box'), may hold values from 0 to 2047, as said below
- translator: float32 [316, 2, 8192], P(None, None, 'dir'), may hold values from -0.4 to 0.4
- list_partner: int32 [256, 189], replicated, may hold values from 0 to 255
- list_kind: int32 [256, 189], replicated, may hold values from 0 to 315
- list_count: int32 [256], replicated, may hold values from 63 to 189, as said below
Outputs:
- fine_incoming: float32 [2048, 8, 2048], P(('box', 'dir'))
The draws below stay inside these ranges and needn't reach their ends.
Inputs may be any that keep to these rules, and one draw needn't show every extreme that they name: `fine_slot`: the fine boxes 8 * 8 * g to 8 * 8 * (g + 1) - 1 carry each of the values 8 * 8 * g to 8 * 8 * (g + 1) - 1 exactly once, so every parent has its 8 children, one in each octant, within that group. Slots from list_count[p] on are ignored.
All inputs are finite; a program needn't handle non-finite values.
Results may differ from the reference program's by a relative error of at most 0.0003.
Values sent between devices are 32-bit elements; how exact they have to be, the bound alone decides.
No kernel may reach another device: no remote copies, remote signals or barrier semaphores. Data moves between devices by JAX's collectives and lax.ppermute only.
A program may use at most 64 MiB of HBM per device.

```python
import jax
import jax.numpy as jnp
from jax import lax

TF = 32
PF = 64
TP = 64
PP = 128
EXC = 4
LIST = 189
NKIND = 316
PB_DEV = 8
NP = 256
NF = 2048
KF = 2048
KP = 8192


def draw_fine_slot(key, part):
    group_width = 8 * PB_DEV
    groups = NF // group_width
    row_keys = jax.random.split(jax.random.fold_in(key, 7), groups)
    shuffled = jax.vmap(lambda row_key: jax.random.permutation(row_key, group_width))(row_keys)
    offsets = jnp.arange(groups, dtype=jnp.int32)[:, None] * group_width
    return (shuffled.astype(jnp.int32) + offsets).reshape(NF).astype(jnp.int32)


def draw_list_count(key, part):
    base_key = jax.random.fold_in(key, 11)
    count_key, first_key, second_key = jax.random.split(base_key, 3)
    counts = jax.random.randint(count_key, (NP,), LIST // 3, LIST + 1)
    longest = jax.random.randint(first_key, (), 0, NP)
    shortest = (longest + 1 + jax.random.randint(second_key, (), 0, NP - 1)) % NP
    counts = counts.at[longest].set(LIST)
    counts = counts.at[shortest].set(LIST // 3)
    return counts.astype(jnp.int32)


def touch_ends(entries, own_key, smallest, top_value):
    dims = entries.shape
    index_at = [jax.random.randint(jax.random.fold_in(own_key, axis), (), 0, dims[axis]) for axis in range(len(dims))]
    entries = entries.at[tuple(index_at)].set(smallest)
    longest = dims.index(max(dims))
    index_at[longest] = (index_at[longest] + 1) % dims[longest]
    return entries.at[tuple(index_at)].set(top_value)


def levels(key, dims, shards, low, high):
    level, own = 1.0, jax.random.fold_in(key, 6)
    for position, parts in shards:
        heights = jnp.exp(jax.random.uniform(jax.random.fold_in(own, position), (parts,), jnp.float32, low / len(shards), high / len(shards)))
        level = level * jnp.repeat(heights, dims[position] // parts).reshape([-1 if axis == position else 1 for axis in range(len(dims))])
    return level


def scatter_about(own_key, extent, scale, limit, shards=(), kind=jnp.bfloat16):
    level = levels(own_key, extent, shards, -0.22, 0.18) if shards else 1.0
    values = jax.random.normal(own_key, extent, jnp.float32) * scale * level
    return jnp.minimum(jnp.maximum(values, -limit), limit).astype(kind)


def setup_inputs(seed: int = 0) -> dict:
    streams_of = jax.random.split(jax.random.key(seed), 7)
    outgoing = scatter_about(streams_of[0], (NF, 2 * EXC, KF), 1.0, 6.0, ((0, 512),), jnp.float32)
    fine_slot = draw_fine_slot(jax.random.fold_in(streams_of[6], 71), 0)
    translator = scatter_about(streams_of[2], (NKIND, 2, KP), 0.06, 0.4, ((2, 16),), jnp.float32)
    list_partner = touch_ends(jax.random.randint(streams_of[3], (NP, LIST), 0, NP), jax.random.fold_in(streams_of[3], 1), 0, NP - 1).astype(jnp.int32)
    list_kind = touch_ends(jax.random.randint(streams_of[4], (NP, LIST), 0, NKIND), jax.random.fold_in(streams_of[4], 1), 0, NKIND - 1).astype(jnp.int32)
    list_count = draw_list_count(jax.random.fold_in(streams_of[6], 71), 0)
    return dict(outgoing=outgoing, fine_slot=fine_slot, translator=translator, list_partner=list_partner, list_kind=list_kind, list_count=list_count)


wave_shift = 5.0
highest = lax.Precision.HIGHEST


def theta_table(fine_count, coarse_count):
    fine_angle = (jnp.arange(fine_count, dtype=jnp.float32) + 0.5) * (jnp.pi / fine_count)
    coarse_angle = (jnp.arange(coarse_count, dtype=jnp.float32) + 0.5) * (jnp.pi / coarse_count)
    orders = jnp.arange(1, fine_count, dtype=jnp.float32)
    products = jnp.cos(coarse_angle[:, None, None] * orders) * jnp.cos(fine_angle[None, :, None] * orders)
    return (1.0 + 2.0 * jnp.sum(products, axis=2)) / fine_count


def phi_table(fine_count, coarse_count):
    fine_angle = jnp.arange(fine_count, dtype=jnp.float32) * (2.0 * jnp.pi / fine_count)
    coarse_angle = jnp.arange(coarse_count, dtype=jnp.float32) * (2.0 * jnp.pi / coarse_count)
    offset = coarse_angle[:, None] - fine_angle[None, :]
    orders = jnp.arange(1, fine_count // 2, dtype=jnp.float32)
    series = jnp.sum(jnp.cos(offset[:, :, None] * orders), axis=2)
    return (1.0 + 2.0 * series + jnp.cos(offset * (fine_count // 2))) / fine_count


def octant_phase(octant, first_theta, theta_count, coarse_theta, coarse_phi):
    theta_index = first_theta + jnp.arange(theta_count, dtype=jnp.int32)
    polar = (theta_index.astype(jnp.float32) + 0.5) * (jnp.pi / coarse_theta)
    azimuth = jnp.arange(coarse_phi, dtype=jnp.float32) * (2.0 * jnp.pi / coarse_phi)
    along_x = jnp.sin(polar)[:, None] * jnp.cos(azimuth)[None, :]
    along_y = jnp.sin(polar)[:, None] * jnp.sin(azimuth)[None, :]
    along_z = jnp.cos(polar)[:, None] + 0.0 * azimuth[None, :]
    sign_x = (2 * (octant % 2) - 1).astype(jnp.float32)
    sign_y = (2 * ((octant // 2) % 2) - 1).astype(jnp.float32)
    sign_z = (2 * (octant // 4) - 1).astype(jnp.float32)
    phase_angle = wave_shift * (sign_x[:, None, None] * along_x[None] + sign_y[:, None, None] * along_y[None] + sign_z[:, None, None] * along_z[None])
    return jnp.cos(phase_angle), jnp.sin(phase_angle)


def reference(outgoing, fine_slot, translator, list_partner, list_kind, list_count):
    channels = outgoing.shape[1]
    excite = channels // 2
    row_boxes = 8 * PB_DEV
    groups = NF // row_boxes
    up_theta = theta_table(TF, TP)
    up_phi = phi_table(PF, PP)
    parent_index = jnp.arange(PB_DEV, dtype=jnp.int32)

    def aggregate_group(inputs):
        group_data, group_slot = inputs
        pattern = group_data.reshape(row_boxes, channels, TF, PF)
        raised = jnp.einsum("ut,fctp->fcup", up_theta, pattern, precision=highest)
        raised = jnp.einsum("qp,fcup->fcuq", up_phi, raised, precision=highest)
        cos_table, sin_table = octant_phase(group_slot % 8, 0, TP, TP, PP)
        cos_table = cos_table[:, None]
        sin_table = sin_table[:, None]
        real_part = raised[:, :excite]
        imag_part = raised[:, excite:]
        shifted = jnp.concatenate([real_part * cos_table + imag_part * sin_table, imag_part * cos_table - real_part * sin_table], axis=1)
        onehot = (((group_slot // 8) % PB_DEV)[None, :] == parent_index[:, None]).astype(jnp.float32)
        summed = jnp.einsum("pf,fcuq->pcuq", onehot, shifted, precision=highest)
        return summed.reshape(PB_DEV, channels, TP * PP)

    parent_out = lax.map(aggregate_group, (outgoing.reshape(groups, row_boxes, channels, TF * PF), fine_slot.reshape(groups, row_boxes)))
    parent_out = parent_out.reshape(NP, channels, TP * PP)
    positions = jnp.arange(LIST, dtype=jnp.int32)

    def translate_parent(inputs):
        partner_row, kind_row, live_count = inputs
        picked = parent_out[partner_row]
        alive_mask = (positions < live_count).astype(jnp.float32)[:, None]
        kernel_rows = translator[kind_row]
        along_real = (kernel_rows[:, 0] * alive_mask)[:, None]
        along_imag = (kernel_rows[:, 1] * alive_mask)[:, None]
        real_part = picked[:, :excite]
        imag_part = picked[:, excite:]
        new_real = jnp.sum(along_real * real_part - along_imag * imag_part, axis=0)
        new_imag = jnp.sum(along_real * imag_part + along_imag * real_part, axis=0)
        return jnp.concatenate([new_real, new_imag], axis=0)

    incoming = lax.map(translate_parent, (list_partner, list_kind, list_count))

    def disaggregate_group(inputs):
        group_field, group_slot = inputs
        onehot = (((group_slot // 8) % PB_DEV)[None, :] == parent_index[:, None]).astype(jnp.float32)
        fields = group_field.reshape(PB_DEV, channels, TP, PP)
        spread = jnp.einsum("pf,pcuq->fcuq", onehot, fields, precision=highest)
        cos_table, sin_table = octant_phase(group_slot % 8, 0, TP, TP, PP)
        cos_table = cos_table[:, None]
        sin_table = sin_table[:, None]
        real_part = spread[:, :excite]
        imag_part = spread[:, excite:]
        shifted = jnp.concatenate([real_part * cos_table - imag_part * sin_table, imag_part * cos_table + real_part * sin_table], axis=1)
        lowered = jnp.einsum("qp,fcuq->fcup", up_phi, shifted, precision=highest) * (PF / PP)
        result = jnp.einsum("ut,fcup->fctp", up_theta, lowered, precision=highest) * (TF / TP)
        return result.reshape(row_boxes, channels, TF * PF)

    fine_incoming = lax.map(disaggregate_group, (incoming.reshape(groups, PB_DEV, channels, TP * PP), fine_slot.reshape(groups, row_boxes)))
    return fine_incoming.reshape(NF, channels, TF * PF)
```

```python
import numpy as np

import jax
import jax.numpy as jnp
from jax import lax
from jax.experimental import pallas as pl
from jax.experimental.pallas import tpu as pltpu
from jax.sharding import PartitionSpec as P

TF = 32
PF = 64
TP = 64
PP = 128
LANES = 128
SLOTS = 256
KINDS = 384
TARGETS = 64
SOURCES = 256
CHUNK = 64

wave_shift = 5.0
f32 = jnp.float32
bf16 = jnp.bfloat16


def theta_matrix():
    a = (np.arange(TP) + 0.5) * np.pi / TP
    b = (np.arange(TF) + 0.5) * np.pi / TF
    m = np.arange(1, TF)
    series = np.cos(a[:, None, None] * m) * np.cos(b[None, :, None] * m)
    return (1.0 + 2.0 * series.sum(2)) / TF


def phi_matrix():
    e = 2 * np.pi * (np.arange(PP)[:, None] / PP - np.arange(PF)[None, :] / PF)
    k = np.arange(1, PF // 2)
    series = np.cos(e[:, :, None] * k).sum(2)
    return (1.0 + 2.0 * series + np.cos(e * (PF // 2))) / PF


def pair_table(matrix):
    n_out, n_in = matrix.shape
    m = matrix.reshape(n_out // 2, 2, n_in // 2, 2).transpose(0, 2, 1, 3)
    same = np.stack([m[:, :, 0, 0], m[:, :, 1, 1]], -1)
    cross = np.stack([m[:, :, 1, 0], m[:, :, 0, 1]], -1)
    table = np.repeat(np.stack([same, cross], 2), PF, axis=3)
    return table.reshape(n_out // 2, n_in, LANES).astype(np.float32)


def split(x):
    high = x.astype(bf16)
    return high, (x - high.astype(f32)).astype(bf16)


def split_constant(x):
    high = np.asarray(x, np.float32).astype(jnp.bfloat16)
    low = (np.asarray(x, np.float32) - high.astype(np.float32)).astype(jnp.bfloat16)
    return np.stack([high, low])


def swap_halves(x):
    return pltpu.roll(x, PF, x.ndim - 1)


def theta_up_kernel(x_ref, c_ref, o_ref):
    def step(z, carry):
        for part in range(2):
            j = 2 * z + part
            same = [jnp.zeros((8, LANES), f32) for _ in range(4)]
            cross = [jnp.zeros((8, LANES), f32) for _ in range(4)]
            for i in range(TF // 2):
                cs = c_ref[j, pl.ds(2 * i, 1), :]
                cx = c_ref[j, pl.ds(2 * i + 1, 1), :]
                for f in range(4):
                    v = x_ref[f, :, pl.ds(i * LANES, LANES)]
                    same[f] = same[f] + cs * v
                    cross[f] = cross[f] + cx * v
            for f in range(4):
                o_ref[z, f, :, pl.ds(part * LANES, LANES)] = same[f] + swap_halves(cross[f])
        return carry

    lax.fori_loop(0, 16, step, 0)


def theta_down_kernel(y_ref, c_ref, o_ref):
    for j in range(TF // 2):
        zero = jnp.zeros((8, LANES), f32)

        def step(z, carry):
            same, cross = list(carry[:4]), list(carry[4:])
            for part in range(2):
                i = 2 * z + part
                cs = c_ref[j, pl.ds(2 * i, 1), :]
                cx = c_ref[j, pl.ds(2 * i + 1, 1), :]
                for f in range(4):
                    v = y_ref[z, f, :, pl.ds(part * LANES, LANES)]
                    same[f] = same[f] + cs * v
                    cross[f] = cross[f] + cx * v
            return (*same, *cross)

        done = lax.fori_loop(0, 16, step, (zero,) * 8, unroll=True)
        for f in range(4):
            o_ref[f, :, pl.ds(j * LANES, LANES)] = done[f] + swap_halves(done[4 + f])


def channel_sign():
    row = lax.broadcasted_iota(jnp.int32, (8, 4 * LANES), 0)
    return jnp.where(row < 4, 1.0, -1.0).astype(f32)


def gather_kernel(slot_ref, x_ref, w_ref, cos_ref, sin_ref, after_ref, o_ref, raised_ref, parent_ref, inv_ref):
    for i in range(64):
        inv_ref[slot_ref[i] % 64] = i
    for j in range(2):
        high, low = split(x_ref[:, :, :, pl.ds(j * LANES, LANES)].reshape(512, LANES))
        wh, wl = w_ref[0], w_ref[1]
        part = (
            jnp.dot(high, wh, preferred_element_type=f32)
            + jnp.dot(low, wh, preferred_element_type=f32)
            + jnp.dot(high, wl, preferred_element_type=f32)
        )
        raised_ref[:, :, pl.ds(j * 256, 256)] = part.reshape(64, 8, 256)
    sign = channel_sign()

    def step(p, carry):
        plain = jnp.zeros((8, 512), f32)
        turned = jnp.zeros((8, 512), f32)
        for o in range(8):
            v = raised_ref[inv_ref[p * 8 + o]]
            plain = plain + v * cos_ref[pl.ds(o, 1), :]
            turned = turned + v * sin_ref[pl.ds(o, 1), :]
        parent_ref[p] = plain + sign * pltpu.roll(turned, 4, 0)
        return carry

    lax.fori_loop(0, 8, step, 0)
    low_half = lax.broadcasted_iota(jnp.int32, (8, LANES), 1) < PF
    for j in range(4):
        for block in range(4):
            a = parent_ref[j, :, pl.ds(block * LANES, LANES)]
            b = parent_ref[j + 4, :, pl.ds(block * LANES, LANES)]
            even = jnp.where(low_half, a, swap_halves(b))
            odd = jnp.where(low_half, swap_halves(a), b)
            for group in range(4):
                o_ref[group * 8 + 2 * block, j] = even
                o_ref[group * 8 + 2 * block + 1, j] = odd


def matrix_kernel(partner_ref, kind_ref, table_ref, o_ref, both_ref):
    @pl.when(pl.program_id(0) == 0)
    def _():
        high, low = split(table_ref[...])
        both_ref[:LANES] = high
        both_ref[LANES:] = low

    slot_kind = lax.broadcasted_iota(jnp.int32, (KINDS, SLOTS), 0)
    slot_source = lax.broadcasted_iota(jnp.int32, (SOURCES, SLOTS), 0)
    table = both_ref[...]

    def step(p, carry):
        pick_kind = jnp.where(slot_kind == kind_ref[pl.ds(p, 1), :], 1.0, 0.0).astype(bf16)
        pick_source = jnp.where(slot_source == partner_ref[pl.ds(p, 1), :], 1.0, 0.0).astype(bf16)
        rows = jnp.dot(table, pick_kind, preferred_element_type=f32).astype(bf16)
        both = lax.dot_general(
            pick_source, rows, (((1,), (1,)), ((), ())), preferred_element_type=f32
        )
        o_ref[p] = both[:, :LANES] + both[:, LANES:]
        return carry

    lax.fori_loop(0, 8, step, 0)


def translate_kernel(s_ref, m_ref, o_ref, wide_ref):
    low_half = lax.broadcasted_iota(jnp.int32, (8, LANES), 1) < PF

    @pl.when(pl.program_id(0) == 0)
    def _():
        def spread(b, carry):
            for j in range(4):
                v = s_ref[b, j]
                r = swap_halves(v)
                wide_ref[b * 8 + j] = jnp.where(low_half, v, r)
                wide_ref[b * 8 + j + 4] = jnp.where(low_half, r, v)
            return carry

        lax.fori_loop(0, 32, spread, 0)

    def step(q, sums):
        sums = list(sums)
        for k in range(8):
            s = q * 8 + k
            v = wide_ref[s]
            for p in range(8):
                sums[p] = sums[p] + m_ref[p, pl.ds(s, 1), :] * v
        return tuple(sums)

    sums = lax.fori_loop(0, SOURCES // 8, step, (jnp.zeros((8, LANES), f32),) * 8)
    row = lax.broadcasted_iota(jnp.int32, (8, LANES), 0)
    sign = jnp.where(row < 4, -1.0, 1.0).astype(f32)
    whole = [a + sign * pltpu.roll(swap_halves(a), 4, 0) for a in sums]
    for j in range(4):
        o_ref[0, j] = jnp.where(low_half, whole[j], swap_halves(whole[j + 4]))


def scatter_kernel(slot_ref, x_ref, w_ref, cos_ref, sin_ref, o_ref, plain_ref, turned_ref, child_ref):
    low_half = lax.broadcasted_iota(jnp.int32, (8, LANES), 1) < PF
    for block in range(4):
        for j in range(4):
            a = x_ref[2 * block, j]
            b = x_ref[2 * block + 1, j]
            first = jnp.where(low_half, a, swap_halves(b))
            second = jnp.where(low_half, swap_halves(a), b)
            plain_ref[j, :, pl.ds(block * LANES, LANES)] = first
            plain_ref[j + 4, :, pl.ds(block * LANES, LANES)] = second
    sign = channel_sign()
    for p in range(8):
        turned_ref[p] = -sign * pltpu.roll(plain_ref[p], 4, 0)

    def step(f, carry):
        s = slot_ref[f] % 64
        p = s // 8
        o = s % 8
        child_ref[f] = (
            plain_ref[p] * cos_ref[pl.ds(o, 1), :] + turned_ref[p] * sin_ref[pl.ds(o, 1), :]
        )
        return carry

    lax.fori_loop(0, 64, step, 0, unroll=4)
    for j in range(2):
        high, low = split(child_ref[:, :, pl.ds(j * 256, 256)].reshape(512, 256))
        wh, wl = w_ref[0], w_ref[1]
        part = (
            jnp.dot(high, wh, preferred_element_type=f32)
            + jnp.dot(low, wh, preferred_element_type=f32)
            + jnp.dot(high, wl, preferred_element_type=f32)
        )
        o_ref[:, :, :, pl.ds(j * LANES, LANES)] = part.reshape(16, 4, 8, LANES)


def phase_tables(dir_index):
    theta_here = TP // 16
    theta_index = dir_index * theta_here + jnp.arange(theta_here, dtype=jnp.int32)
    polar = (theta_index.astype(f32) + 0.5) * (jnp.pi / TP)
    azimuth = jnp.arange(PP, dtype=f32) * (2.0 * jnp.pi / PP)
    along_x = (jnp.sin(polar)[:, None] * jnp.cos(azimuth)[None, :]).reshape(1, 512)
    along_y = (jnp.sin(polar)[:, None] * jnp.sin(azimuth)[None, :]).reshape(1, 512)
    along_z = (jnp.cos(polar)[:, None] + 0.0 * azimuth[None, :]).reshape(1, 512)
    octant = jnp.arange(8, dtype=jnp.int32)[:, None]
    sign_x = (2 * (octant % 2) - 1).astype(f32)
    sign_y = (2 * (octant // 2 % 2) - 1).astype(f32)
    sign_z = (2 * (octant // 4) - 1).astype(f32)
    angle = wave_shift * (sign_x * along_x + sign_y * along_y + sign_z * along_z)
    return jnp.cos(angle), jnp.sin(angle)


vmem = pl.BlockSpec(memory_space=pltpu.VMEM)
smem = pl.BlockSpec(memory_space=pltpu.SMEM)


def shape(*dims):
    return jax.ShapeDtypeStruct(dims, f32)


def body(outgoing, fine_slot, translator, list_partner, list_kind, list_count):
    box_index = lax.axis_index("box")
    dir_index = lax.axis_index("dir")
    chunk = box_index % 8
    group = box_index // 8

    theta = theta_matrix()
    up = jnp.asarray(pair_table(theta))
    down = jnp.asarray(pair_table(theta.T * (TF / TP)))
    phi = phi_matrix()
    phi_up = jnp.asarray(split_constant(np.kron(np.eye(2), phi.T)))
    phi_down = jnp.asarray(split_constant(np.kron(np.eye(2), phi) * (PF / PP)))

    sent = pl.pallas_call(
        theta_up_kernel, out_shape=shape(16, 4, 8, 256), in_specs=[vmem, vmem], out_specs=vmem
    )(outgoing, up)
    spread = lax.all_to_all(sent, "dir", split_axis=0, concat_axis=0, tiled=True)

    rows = lax.dynamic_slice_in_dim(list_partner, group * TARGETS, TARGETS, 0)
    kinds = lax.dynamic_slice_in_dim(list_kind, group * TARGETS, TARGETS, 0)
    count = lax.dynamic_slice_in_dim(list_count, group * TARGETS, TARGETS, 0)
    length = rows.shape[1]
    live = jnp.arange(length, dtype=jnp.int32)[None, :] < count[:, None]
    pad = ((0, 0), (0, SLOTS - length))
    rows = jnp.pad(jnp.where(live, rows, -1), pad, constant_values=-1)
    kinds = jnp.pad(kinds, pad, constant_values=-1)
    table = lax.dynamic_slice_in_dim(translator, chunk * CHUNK, CHUNK, 2)
    table = table.reshape(table.shape[0], LANES).T
    table = jnp.pad(table, ((0, 0), (0, KINDS - table.shape[1])))
    matrix = pl.pallas_call(
        matrix_kernel,
        grid=(TARGETS // 8,),
        in_specs=[
            pl.BlockSpec((8, SLOTS), lambda i: (i, 0)),
            pl.BlockSpec((8, SLOTS), lambda i: (i, 0)),
            pl.BlockSpec((LANES, KINDS), lambda i: (0, 0)),
        ],
        out_specs=pl.BlockSpec((8, SOURCES, LANES), lambda i: (i, 0, 0)),
        out_shape=shape(TARGETS, SOURCES, LANES),
        scratch_shapes=[pltpu.VMEM((256, KINDS), bf16)],
    )(rows, kinds, table)
    cos_table, sin_table = phase_tables(dir_index)

    packed = pl.pallas_call(
        gather_kernel,
        out_shape=shape(32, 4, 8, LANES),
        in_specs=[smem, vmem, vmem, vmem, vmem, pl.BlockSpec(memory_space=pl.ANY)],
        out_specs=vmem,
        scratch_shapes=[
            pltpu.VMEM((64, 8, 512), f32),
            pltpu.VMEM((8, 8, 512), f32),
            pltpu.SMEM((64,), jnp.int32),
        ],
    )(fine_slot, spread, phi_up, cos_table, sin_table, matrix)
    everyone = lax.all_to_all(packed, "box", split_axis=0, concat_axis=0, tiled=True)
    incoming = pl.pallas_call(
        translate_kernel,
        grid=(TARGETS // 8,),
        in_specs=[
            pl.BlockSpec((32, 4, 8, LANES), lambda i: (0, 0, 0, 0)),
            pl.BlockSpec((8, SOURCES, LANES), lambda i: (i, 0, 0)),
        ],
        out_specs=pl.BlockSpec((1, 4, 8, LANES), lambda i: (i, 0, 0, 0)),
        out_shape=shape(8, 4, 8, LANES),
        scratch_shapes=[pltpu.VMEM((SOURCES, 8, LANES), f32)],
    )(everyone, matrix)
    groups = [[8 * g + k for k in range(8)] for g in range(4)]
    fields = lax.all_to_all(
        incoming, "box", split_axis=0, concat_axis=0, axis_index_groups=groups, tiled=True
    )
    lowered = pl.pallas_call(
        scatter_kernel,
        out_shape=shape(16, 4, 8, 256),
        in_specs=[smem, vmem, vmem, vmem, vmem],
        out_specs=vmem,
        scratch_shapes=[
            pltpu.VMEM((8, 8, 512), f32),
            pltpu.VMEM((8, 8, 512), f32),
            pltpu.VMEM((64, 8, 512), f32),
        ],
    )(fine_slot, fields, phi_down, cos_table, sin_table)
    back = lax.all_to_all(lowered, "dir", split_axis=0, concat_axis=0, tiled=True)
    return pl.pallas_call(
        theta_down_kernel, out_shape=shape(4, 8, TF * PF), in_specs=[vmem, vmem], out_specs=vmem
    )(back, down)


def solution(mesh):
    placed = (P(("box", "dir"), None, None), P("box"), P(None, None, "dir"), P(), P(), P())
    return jax.shard_map(
        body, mesh=mesh, in_specs=placed, out_specs=P(("box", "dir"), None, None), check_vma=False
    )
```

```python
import numpy as np

import jax
import jax.numpy as jnp
from jax import lax
from jax.experimental import pallas as pl
from jax.experimental.pallas import tpu as pltpu
from jax.sharding import PartitionSpec as P

TF = 32
PF = 64
TP = 64
PP = 128
LANES = 128
SLOTS = 256
KINDS = 384
TARGETS = 64
SOURCES = 256
CHUNK = 64

wave_shift = 5.0
f32 = jnp.float32
bf16 = jnp.bfloat16


def theta_matrix():
    a = (np.arange(TP) + 0.5) * np.pi / TP
    b = (np.arange(TF) + 0.5) * np.pi / TF
    m = np.arange(1, TF)
    series = np.cos(a[:, None, None] * m) * np.cos(b[None, :, None] * m)
    return (1.0 + 2.0 * series.sum(2)) / TF


def phi_matrix():
    e = 2 * np.pi * (np.arange(PP)[:, None] / PP - np.arange(PF)[None, :] / PF)
    k = np.arange(1, PF // 2)
    series = np.cos(e[:, :, None] * k).sum(2)
    return (1.0 + 2.0 * series + np.cos(e * (PF // 2))) / PF


def pair_table(matrix):
    n_out, n_in = matrix.shape
    m = matrix.reshape(n_out // 2, 2, n_in // 2, 2).transpose(0, 2, 1, 3)
    same = np.stack([m[:, :, 0, 0], m[:, :, 1, 1]], -1)
    cross = np.stack([m[:, :, 1, 0], m[:, :, 0, 1]], -1)
    table = np.repeat(np.stack([same, cross], 2), PF, axis=3)
    return table.reshape(n_out // 2, n_in, LANES).astype(np.float32)


def split(x):
    high = x.astype(bf16)
    return high, (x - high.astype(f32)).astype(bf16)


def split_constant(x):
    high = np.asarray(x, np.float32).astype(jnp.bfloat16)
    low = (np.asarray(x, np.float32) - high.astype(np.float32)).astype(jnp.bfloat16)
    return np.stack([high, low])


def swap_halves(x):
    return pltpu.roll(x, PF, x.ndim - 1)


def theta_up_kernel(x_ref, c_ref, o_ref):
    def step(z, carry):
        for part in range(2):
            j = 2 * z + part
            same = [jnp.zeros((8, LANES), f32) for _ in range(4)]
            cross = [jnp.zeros((8, LANES), f32) for _ in range(4)]
            for i in range(TF // 2):
                cs = c_ref[j, pl.ds(2 * i, 1), :]
                cx = c_ref[j, pl.ds(2 * i + 1, 1), :]
                for f in range(4):
                    v = x_ref[f, :, pl.ds(i * LANES, LANES)]
                    same[f] = same[f] + cs * v
                    cross[f] = cross[f] + cx * v
            for f in range(4):
                o_ref[z, f, :, pl.ds(part * LANES, LANES)] = same[f] + swap_halves(cross[f])
        return carry

    lax.fori_loop(0, 16, step, 0)


def theta_down_kernel(y_ref, c_ref, o_ref):
    for j in range(TF // 2):
        zero = jnp.zeros((8, LANES), f32)

        def step(z, carry):
            same, cross = list(carry[:4]), list(carry[4:])
            for part in range(2):
                i = 2 * z + part
                cs = c_ref[j, pl.ds(2 * i, 1), :]
                cx = c_ref[j, pl.ds(2 * i + 1, 1), :]
                for f in range(4):
                    v = y_ref[z, f, :, pl.ds(part * LANES, LANES)]
                    same[f] = same[f] + cs * v
                    cross[f] = cross[f] + cx * v
            return (*same, *cross)

        done = lax.fori_loop(0, 16, step, (zero,) * 8, unroll=True)
        for f in range(4):
            o_ref[f, :, pl.ds(j * LANES, LANES)] = done[f] + swap_halves(done[4 + f])


def channel_sign():
    row = lax.broadcasted_iota(jnp.int32, (8, 4 * LANES), 0)
    return jnp.where(row < 4, 1.0, -1.0).astype(f32)


def gather_kernel(slot_ref, x_ref, w_ref, cos_ref, sin_ref, after_ref, o_ref, raised_ref, parent_ref, inv_ref):
    for i in range(64):
        inv_ref[slot_ref[i] % 64] = i
    for j in range(2):
        high, low = split(x_ref[:, :, :, pl.ds(j * LANES, LANES)].reshape(512, LANES))
        wh, wl = w_ref[0], w_ref[1]
        part = (
            jnp.dot(high, wh, preferred_element_type=f32)
            + jnp.dot(low, wh, preferred_element_type=f32)
            + jnp.dot(high, wl, preferred_element_type=f32)
        )
        raised_ref[:, :, pl.ds(j * 256, 256)] = part.reshape(64, 8, 256)
    sign = channel_sign()

    def step(p, carry):
        plain = jnp.zeros((8, 512), f32)
        turned = jnp.zeros((8, 512), f32)
        for o in range(8):
            v = raised_ref[inv_ref[p * 8 + o]]
            plain = plain + v * cos_ref[pl.ds(o, 1), :]
            turned = turned + v * sin_ref[pl.ds(o, 1), :]
        parent_ref[p] = plain + sign * pltpu.roll(turned, 4, 0)
        return carry

    lax.fori_loop(0, 8, step, 0)
    low_half = lax.broadcasted_iota(jnp.int32, (8, LANES), 1) < PF
    for j in range(4):
        for block in range(4):
            a = parent_ref[j, :, pl.ds(block * LANES, LANES)]
            b = parent_ref[j + 4, :, pl.ds(block * LANES, LANES)]
            even = jnp.where(low_half, a, swap_halves(b))
            odd = jnp.where(low_half, swap_halves(a), b)
            for group in range(4):
                o_ref[group * 8 + 2 * block, j] = even
                o_ref[group * 8 + 2 * block + 1, j] = odd


def matrix_kernel(partner_ref, kind_ref, table_ref, o_ref, both_ref):
    @pl.when(pl.program_id(0) == 0)
    def _():
        high, low = split(table_ref[...])
        both_ref[:LANES] = high
        both_ref[LANES:] = low

    slot_kind = lax.broadcasted_iota(jnp.int32, (KINDS, SLOTS), 0)
    slot_source = lax.broadcasted_iota(jnp.int32, (SOURCES, SLOTS), 0)
    table = both_ref[...]

    def step(p, carry):
        pick_kind = jnp.where(slot_kind == kind_ref[pl.ds(p, 1), :], 1.0, 0.0).astype(bf16)
        pick_source = jnp.where(slot_source == partner_ref[pl.ds(p, 1), :], 1.0, 0.0).astype(bf16)
        rows = jnp.dot(table, pick_kind, preferred_element_type=f32).astype(bf16)
        both = lax.dot_general(
            pick_source, rows, (((1,), (1,)), ((), ())), preferred_element_type=f32
        )
        o_ref[p] = both[:, :LANES] + both[:, LANES:]
        return carry

    lax.fori_loop(0, 8, step, 0)


def translate_kernel(s_ref, m_ref, o_ref, wide_ref):
    low_half = lax.broadcasted_iota(jnp.int32, (8, LANES), 1) < PF

    @pl.when(pl.program_id(0) == 0)
    def _():
        def spread(b, carry):
            for j in range(4):
                v = s_ref[b, j]
                r = swap_halves(v)
                wide_ref[b * 8 + j] = jnp.where(low_half, v, r)
                wide_ref[b * 8 + j + 4] = jnp.where(low_half, r, v)
            return carry

        lax.fori_loop(0, 32, spread, 0)

    def step(q, sums):
        sums = list(sums)
        for k in range(8):
            s = q * 8 + k
            v = wide_ref[s]
            for p in range(8):
                sums[p] = sums[p] + m_ref[p, pl.ds(s, 1), :] * v
        return tuple(sums)

    sums = lax.fori_loop(0, SOURCES // 8, step, (jnp.zeros((8, LANES), f32),) * 8)
    row = lax.broadcasted_iota(jnp.int32, (8, LANES), 0)
    sign = jnp.where(row < 4, -1.0, 1.0).astype(f32)
    whole = [a + sign * pltpu.roll(swap_halves(a), 4, 0) for a in sums]
    for j in range(4):
        o_ref[pl.program_id(0), j] = jnp.where(low_half, whole[j], swap_halves(whole[j + 4]))


def scatter_kernel(slot_ref, x_ref, w_ref, cos_ref, sin_ref, o_ref, plain_ref, turned_ref, child_ref):
    low_half = lax.broadcasted_iota(jnp.int32, (8, LANES), 1) < PF
    for block in range(4):
        for j in range(4):
            a = x_ref[2 * block, j]
            b = x_ref[2 * block + 1, j]
            first = jnp.where(low_half, a, swap_halves(b))
            second = jnp.where(low_half, swap_halves(a), b)
            plain_ref[j, :, pl.ds(block * LANES, LANES)] = first
            plain_ref[j + 4, :, pl.ds(block * LANES, LANES)] = second
    sign = channel_sign()
    for p in range(8):
        turned_ref[p] = -sign * pltpu.roll(plain_ref[p], 4, 0)

    def step(f, carry):
        s = slot_ref[f] % 64
        p = s // 8
        o = s % 8
        child_ref[f] = (
            plain_ref[p] * cos_ref[pl.ds(o, 1), :] + turned_ref[p] * sin_ref[pl.ds(o, 1), :]
        )
        return carry

    lax.fori_loop(0, 64, step, 0, unroll=4)
    for j in range(2):
        high, low = split(child_ref[:, :, pl.ds(j * 256, 256)].reshape(512, 256))
        wh, wl = w_ref[0], w_ref[1]
        part = (
            jnp.dot(high, wh, preferred_element_type=f32)
            + jnp.dot(low, wh, preferred_element_type=f32)
            + jnp.dot(high, wl, preferred_element_type=f32)
        )
        o_ref[:, :, :, pl.ds(j * LANES, LANES)] = part.reshape(16, 4, 8, LANES)


def phase_tables(dir_index):
    theta_here = TP // 16
    theta_index = dir_index * theta_here + jnp.arange(theta_here, dtype=jnp.int32)
    polar = (theta_index.astype(f32) + 0.5) * (jnp.pi / TP)
    azimuth = jnp.arange(PP, dtype=f32) * (2.0 * jnp.pi / PP)
    along_x = (jnp.sin(polar)[:, None] * jnp.cos(azimuth)[None, :]).reshape(1, 512)
    along_y = (jnp.sin(polar)[:, None] * jnp.sin(azimuth)[None, :]).reshape(1, 512)
    along_z = (jnp.cos(polar)[:, None] + 0.0 * azimuth[None, :]).reshape(1, 512)
    octant = jnp.arange(8, dtype=jnp.int32)[:, None]
    sign_x = (2 * (octant % 2) - 1).astype(f32)
    sign_y = (2 * (octant // 2 % 2) - 1).astype(f32)
    sign_z = (2 * (octant // 4) - 1).astype(f32)
    angle = wave_shift * (sign_x * along_x + sign_y * along_y + sign_z * along_z)
    return jnp.cos(angle), jnp.sin(angle)


vmem = pl.BlockSpec(memory_space=pltpu.VMEM)
smem = pl.BlockSpec(memory_space=pltpu.SMEM)


def shape(*dims):
    return jax.ShapeDtypeStruct(dims, f32)


def near(*dims):
    return pltpu.VMEM(dims, f32)


def hold(x):
    return pltpu.with_memory_space_constraint(x, pltpu.VMEM)


def body(outgoing, fine_slot, translator, list_partner, list_kind, list_count):
    box_index = lax.axis_index("box")
    dir_index = lax.axis_index("dir")
    chunk = box_index % 8
    group = box_index // 8

    theta = theta_matrix()
    up = jnp.asarray(pair_table(theta))
    down = jnp.asarray(pair_table(theta.T * (TF / TP)))
    phi = phi_matrix()
    phi_up = jnp.asarray(split_constant(np.kron(np.eye(2), phi.T)))
    phi_down = jnp.asarray(split_constant(np.kron(np.eye(2), phi) * (PF / PP)))

    sent = pl.pallas_call(
        theta_up_kernel, out_shape=near(16, 4, 8, 256), in_specs=[vmem, vmem], out_specs=vmem
    )(outgoing, up)
    spread = lax.all_to_all(sent, "dir", split_axis=0, concat_axis=0, tiled=True)

    rows = lax.dynamic_slice_in_dim(list_partner, group * TARGETS, TARGETS, 0)
    kinds = lax.dynamic_slice_in_dim(list_kind, group * TARGETS, TARGETS, 0)
    count = lax.dynamic_slice_in_dim(list_count, group * TARGETS, TARGETS, 0)
    length = rows.shape[1]
    live = jnp.arange(length, dtype=jnp.int32)[None, :] < count[:, None]
    pad = ((0, 0), (0, SLOTS - length))
    rows = jnp.pad(jnp.where(live, rows, -1), pad, constant_values=-1)
    kinds = jnp.pad(kinds, pad, constant_values=-1)
    table = lax.dynamic_slice_in_dim(translator, chunk * CHUNK, CHUNK, 2)
    table = table.reshape(table.shape[0], LANES).T
    table = jnp.pad(table, ((0, 0), (0, KINDS - table.shape[1])))
    matrix = pl.pallas_call(
        matrix_kernel,
        grid=(TARGETS // 8,),
        in_specs=[
            pl.BlockSpec((8, SLOTS), lambda i: (i, 0)),
            pl.BlockSpec((8, SLOTS), lambda i: (i, 0)),
            pl.BlockSpec((LANES, KINDS), lambda i: (0, 0)),
        ],
        out_specs=pl.BlockSpec((8, SOURCES, LANES), lambda i: (i, 0, 0)),
        out_shape=shape(TARGETS, SOURCES, LANES),
        scratch_shapes=[pltpu.VMEM((256, KINDS), bf16)],
    )(rows, kinds, table)
    cos_table, sin_table = phase_tables(dir_index)

    packed = pl.pallas_call(
        gather_kernel,
        out_shape=near(32, 4, 8, LANES),
        in_specs=[smem, vmem, vmem, vmem, vmem, pl.BlockSpec(memory_space=pl.ANY)],
        out_specs=vmem,
        scratch_shapes=[
            pltpu.VMEM((64, 8, 512), f32),
            pltpu.VMEM((8, 8, 512), f32),
            pltpu.SMEM((64,), jnp.int32),
        ],
    )(fine_slot, hold(spread), phi_up, cos_table, sin_table, matrix)
    everyone = lax.all_to_all(packed, "box", split_axis=0, concat_axis=0, tiled=True)
    incoming = pl.pallas_call(
        translate_kernel,
        grid=(TARGETS // 8,),
        in_specs=[
            vmem,
            pl.BlockSpec((8, SOURCES, LANES), lambda i: (i, 0, 0)),
        ],
        out_specs=vmem,
        out_shape=near(8, 4, 8, LANES),
        scratch_shapes=[pltpu.VMEM((SOURCES, 8, LANES), f32)],
    )(hold(everyone), matrix)
    groups = [[8 * g + k for k in range(8)] for g in range(4)]
    fields = lax.all_to_all(
        incoming, "box", split_axis=0, concat_axis=0, axis_index_groups=groups, tiled=True
    )
    lowered = pl.pallas_call(
        scatter_kernel,
        out_shape=near(16, 4, 8, 256),
        in_specs=[smem, vmem, vmem, vmem, vmem],
        out_specs=vmem,
        scratch_shapes=[
            pltpu.VMEM((8, 8, 512), f32),
            pltpu.VMEM((8, 8, 512), f32),
            pltpu.VMEM((64, 8, 512), f32),
        ],
    )(fine_slot, hold(fields), phi_down, cos_table, sin_table)
    back = lax.all_to_all(lowered, "dir", split_axis=0, concat_axis=0, tiled=True)
    return pl.pallas_call(
        theta_down_kernel, out_shape=shape(4, 8, TF * PF), in_specs=[vmem, vmem], out_specs=vmem
    )(hold(back), down)


def solution(mesh):
    placed = (P(("box", "dir"), None, None), P("box"), P(None, None, "dir"), P(), P(), P())
    return jax.shard_map(
        body, mesh=mesh, in_specs=placed, out_specs=P(("box", "dir"), None, None), check_vma=False
    )
```

```python
import numpy as np

import jax
import jax.numpy as jnp
from jax import lax
from jax.experimental import pallas as pl
from jax.experimental.pallas import tpu as pltpu
from jax.sharding import PartitionSpec as P

TF = 32
PF = 64
TP = 64
PP = 128
LANES = 128
SLOTS = 192
KINDS = 384
TARGETS = 64
SOURCES = 256
CHUNK = 64

wave_shift = 5.0
f32 = jnp.float32
bf16 = jnp.bfloat16


def theta_matrix():
    a = (np.arange(TP) + 0.5) * np.pi / TP
    b = (np.arange(TF) + 0.5) * np.pi / TF
    m = np.arange(1, TF)
    series = np.cos(a[:, None, None] * m) * np.cos(b[None, :, None] * m)
    return (1.0 + 2.0 * series.sum(2)) / TF


def phi_matrix():
    e = 2 * np.pi * (np.arange(PP)[:, None] / PP - np.arange(PF)[None, :] / PF)
    k = np.arange(1, PF // 2)
    series = np.cos(e[:, :, None] * k).sum(2)
    return (1.0 + 2.0 * series + np.cos(e * (PF // 2))) / PF


def pair_table(matrix):
    n_out, n_in = matrix.shape
    m = matrix.reshape(n_out // 2, 2, n_in // 2, 2).transpose(0, 2, 1, 3)
    same = np.stack([m[:, :, 0, 0], m[:, :, 1, 1]], -1)
    cross = np.stack([m[:, :, 1, 0], m[:, :, 0, 1]], -1)
    table = np.repeat(np.stack([same, cross], 2), PF, axis=3)
    return table.reshape(n_out // 2, n_in, LANES).astype(np.float32)


def split(x):
    high = x.astype(bf16)
    return high, (x - high.astype(f32)).astype(bf16)


def split_constant(x):
    high = np.asarray(x, np.float32).astype(jnp.bfloat16)
    low = (np.asarray(x, np.float32) - high.astype(np.float32)).astype(jnp.bfloat16)
    return np.stack([high, low])


def swap_halves(x):
    return pltpu.roll(x, PF, x.ndim - 1)


def parity_table(matrix):
    n_out, n_in = matrix.shape
    top = matrix[: n_out // 2]
    near, far = top[:, : n_in // 2], top[:, ::-1][:, : n_in // 2]
    return np.concatenate([pair_table((near + far) / 2), pair_table((near - far) / 2)], 1)


def theta_step(parity_ref, c_ref, j, count):
    zero = jnp.zeros((8, LANES), f32)
    sums = [[zero] * 4 for _ in range(4)]
    for i in range(count):
        for odd in range(2):
            base = odd * 2 * count + 2 * i
            cs = c_ref[j, pl.ds(base, 1), :]
            cx = c_ref[j, pl.ds(base + 1, 1), :]
            for f in range(4):
                v = parity_ref[f, i, odd]
                sums[2 * odd][f] = sums[2 * odd][f] + cs * v
                sums[2 * odd + 1][f] = sums[2 * odd + 1][f] + cx * v
    out = []
    for f in range(4):
        es, ex, os, ox = (sums[k][f] for k in range(4))
        out.append(((es + os) + swap_halves(ex + ox), swap_halves(es - os) + (ex - ox)))
    return out


def theta_up_kernel(x_ref, c_ref, o_ref, parity_ref):
    for f in range(4):
        for i in range(8):
            v = x_ref[f, :, pl.ds(i * LANES, LANES)]
            w = swap_halves(x_ref[f, :, pl.ds((15 - i) * LANES, LANES)])
            parity_ref[f, i, 0] = v + w
            parity_ref[f, i, 1] = v - w

    def step(z, carry):
        for part in range(2):
            out = theta_step(parity_ref, c_ref, 2 * z + part, 8)
            for f in range(4):
                o_ref[z, f, :, pl.ds(part * LANES, LANES)] = out[f][0]
                o_ref[15 - z, f, :, pl.ds((1 - part) * LANES, LANES)] = out[f][1]
        return carry

    lax.fori_loop(0, 8, step, 0)


def theta_down_kernel(y_ref, c_ref, o_ref, parity_ref):
    for f in range(4):
        for i in range(16):
            v = y_ref[i // 2, f, :, pl.ds(i % 2 * LANES, LANES)]
            w = swap_halves(y_ref[15 - i // 2, f, :, pl.ds((1 - i % 2) * LANES, LANES)])
            parity_ref[f, i, 0] = v + w
            parity_ref[f, i, 1] = v - w
    for j in range(8):
        out = theta_step(parity_ref, c_ref, j, 16)
        for f in range(4):
            o_ref[f, :, pl.ds(j * LANES, LANES)] = out[f][0]
            o_ref[f, :, pl.ds((15 - j) * LANES, LANES)] = out[f][1]


def channel_sign():
    row = lax.broadcasted_iota(jnp.int32, (8, 4 * LANES), 0)
    return jnp.where(row < 4, 1.0, -1.0).astype(f32)


def gather_kernel(slot_ref, x_ref, w_ref, cos_ref, sin_ref, after_ref, o_ref, raised_ref, parent_ref, inv_ref):
    for i in range(64):
        inv_ref[slot_ref[i] % 64] = i
    for j in range(2):
        high, low = split(x_ref[:, :, :, pl.ds(j * LANES, LANES)].reshape(512, LANES))
        wh, wl = w_ref[0], w_ref[1]
        part = (
            jnp.dot(high, wh, preferred_element_type=f32)
            + jnp.dot(low, wh, preferred_element_type=f32)
            + jnp.dot(high, wl, preferred_element_type=f32)
        )
        raised_ref[:, :, pl.ds(j * 256, 256)] = part.reshape(64, 8, 256)
    sign = channel_sign()

    def step(p, carry):
        plain = jnp.zeros((8, 512), f32)
        turned = jnp.zeros((8, 512), f32)
        for o in range(8):
            v = raised_ref[inv_ref[p * 8 + o]]
            plain = plain + v * cos_ref[pl.ds(o, 1), :]
            turned = turned + v * sin_ref[pl.ds(o, 1), :]
        parent_ref[p] = plain + sign * pltpu.roll(turned, 4, 0)
        return carry

    lax.fori_loop(0, 8, step, 0)
    low_half = lax.broadcasted_iota(jnp.int32, (8, LANES), 1) < PF
    for j in range(4):
        for block in range(4):
            a = parent_ref[2 * j, :, pl.ds(block * LANES, LANES)]
            b = parent_ref[2 * j + 1, :, pl.ds(block * LANES, LANES)]
            even = jnp.where(low_half, a, swap_halves(b))
            odd = jnp.where(low_half, swap_halves(a), b)
            for group in range(4):
                o_ref[group * 8 + 2 * block, j] = even
                o_ref[group * 8 + 2 * block + 1, j] = odd


def matrix_kernel(partner_ref, kind_ref, table_ref, o_ref, both_ref, picked_ref):
    @pl.when(pl.program_id(0) == 0)
    def _():
        high, low = split(table_ref[...])
        both_ref[:, :LANES] = high
        both_ref[:, LANES:] = low

    lane_kind = lax.broadcasted_iota(jnp.int32, (SLOTS, KINDS), 1)
    row_source = lax.broadcasted_iota(jnp.int32, (SOURCES, SLOTS), 0)
    pick_kind = jnp.concatenate(
        [
            jnp.where(lane_kind == kind_ref[0, :, p : p + 1], 1.0, 0.0).astype(bf16)
            for p in range(8)
        ],
        0,
    )
    picked_ref[...] = jnp.dot(pick_kind, both_ref[...], preferred_element_type=f32).astype(bf16)
    for p in range(8):
        pick_source = jnp.where(row_source == partner_ref[pl.ds(p, 1), :], 1.0, 0.0).astype(bf16)
        rows = picked_ref[pl.ds(p * SLOTS, SLOTS), :]
        both = jnp.dot(pick_source, rows, preferred_element_type=f32)
        o_ref[p] = both[:, :LANES] + both[:, LANES:]


def fold_rows(parts):
    row = lax.broadcasted_iota(jnp.int32, (8, LANES), 0)
    shift = 1
    while len(parts) > 1:
        first = (row & shift) == 0
        parts = [
            jnp.where(first, a, b) + pltpu.roll(jnp.where(first, b, a), shift, 0)
            for a, b in zip(parts[0::2], parts[1::2])
        ]
        shift *= 2
    return parts[0]


def translate_kernel(s_ref, m_ref, o_ref, rows_ref, wide_ref):
    low_half = lax.broadcasted_iota(jnp.int32, (8, LANES), 1) < PF
    top = lax.broadcasted_iota(jnp.int32, (8, LANES), 0) < 4

    @pl.when(pl.program_id(0) == 0)
    def _():
        def pair(b, carry):
            for j in range(4):
                v = s_ref[b, j]
                w = swap_halves(pltpu.roll(v, 4, 0))
                rows_ref[pl.ds(b * 32 + j * 8, 8), :] = jnp.where(low_half == top, v, w)
            return carry

        lax.fori_loop(0, 32, pair, 0)

        def spread(b, carry):
            plain = [rows_ref[pl.ds(b * 32 + e, 8, stride=4), :] for e in range(4)]
            both = [v + swap_halves(v) for v in plain]
            for e in range(4):
                wide_ref[b, e] = plain[e]
            for h in range(2):
                wide_ref[b, 4 + h] = jnp.where(low_half, both[2 * h], both[2 * h + 1])
            return carry

        lax.fori_loop(0, 32, spread, 0)

    for q in range(2):

        def step(b, sums):
            sums = list(sums)
            source = [wide_ref[b, k] for k in range(6)]
            for p in range(4):
                m = m_ref[4 * q + p, pl.ds(pl.multiple_of(b * 8, 8), 8), :]
                t = m + swap_halves(m)
                for k in range(6):
                    sums[6 * p + k] = sums[6 * p + k] + source[k] * (m if k < 4 else t)
            return tuple(sums)

        sums = lax.fori_loop(0, SOURCES // 8, step, (jnp.zeros((8, LANES), f32),) * 24, unroll=True)
        real, imag = [], []
        for p in range(4):
            part = sums[6 * p : 6 * p + 6]
            turned = [swap_halves(v) for v in part[:4]]
            real.append([a - b for a, b in zip(part[:4], turned)])
            total = [a + b for a, b in zip(part[:4], turned)]
            imag.append(
                [part[4 + h] - jnp.where(low_half, total[2 * h], total[2 * h + 1]) for h in range(2)]
            )
        for j in range(2):
            a, b = 2 * j, 2 * j + 1
            parts = [jnp.where(low_half, x, -y) for x, y in zip(real[a], real[b])]
            for h in range(2):
                x, y = imag[a][h], imag[b][h]
                parts.append(jnp.where(low_half, x, swap_halves(y)))
                parts.append(jnp.where(low_half, swap_halves(x), y))
            o_ref[pl.program_id(0), 2 * q + j] = fold_rows(parts)


def scatter_kernel(slot_ref, x_ref, w_ref, cos_ref, sin_ref, o_ref, plain_ref, turned_ref, child_ref):
    low_half = lax.broadcasted_iota(jnp.int32, (8, LANES), 1) < PF
    for block in range(4):
        for j in range(4):
            a = x_ref[2 * block, j]
            b = x_ref[2 * block + 1, j]
            first = jnp.where(low_half, a, swap_halves(b))
            second = jnp.where(low_half, swap_halves(a), b)
            plain_ref[2 * j, :, pl.ds(block * LANES, LANES)] = first
            plain_ref[2 * j + 1, :, pl.ds(block * LANES, LANES)] = second
    sign = channel_sign()
    for p in range(8):
        turned_ref[p] = -sign * pltpu.roll(plain_ref[p], 4, 0)

    def step(f, carry):
        s = slot_ref[f] % 64
        p = s // 8
        o = s % 8
        child_ref[f] = (
            plain_ref[p] * cos_ref[pl.ds(o, 1), :] + turned_ref[p] * sin_ref[pl.ds(o, 1), :]
        )
        return carry

    lax.fori_loop(0, 64, step, 0, unroll=4)
    for j in range(2):
        high, low = split(child_ref[:, :, pl.ds(j * 256, 256)].reshape(512, 256))
        wh, wl = w_ref[0], w_ref[1]
        part = (
            jnp.dot(high, wh, preferred_element_type=f32)
            + jnp.dot(low, wh, preferred_element_type=f32)
            + jnp.dot(high, wl, preferred_element_type=f32)
        )
        o_ref[:, :, :, pl.ds(j * LANES, LANES)] = part.reshape(16, 4, 8, LANES)


def phase_tables(dir_index):
    theta_here = TP // 16
    theta_index = dir_index * theta_here + jnp.arange(theta_here, dtype=jnp.int32)
    polar = (theta_index.astype(f32) + 0.5) * (jnp.pi / TP)
    azimuth = jnp.arange(PP, dtype=f32) * (2.0 * jnp.pi / PP)
    along_x = (jnp.sin(polar)[:, None] * jnp.cos(azimuth)[None, :]).reshape(1, 512)
    along_y = (jnp.sin(polar)[:, None] * jnp.sin(azimuth)[None, :]).reshape(1, 512)
    along_z = (jnp.cos(polar)[:, None] + 0.0 * azimuth[None, :]).reshape(1, 512)
    octant = jnp.arange(8, dtype=jnp.int32)[:, None]
    sign_x = (2 * (octant % 2) - 1).astype(f32)
    sign_y = (2 * (octant // 2 % 2) - 1).astype(f32)
    sign_z = (2 * (octant // 4) - 1).astype(f32)
    angle = wave_shift * (sign_x * along_x + sign_y * along_y + sign_z * along_z)
    return jnp.cos(angle), jnp.sin(angle)


vmem = pl.BlockSpec(memory_space=pltpu.VMEM)
smem = pl.BlockSpec(memory_space=pltpu.SMEM)


def shape(*dims):
    return jax.ShapeDtypeStruct(dims, f32)


def near(*dims):
    return pltpu.VMEM(dims, f32)


def hold(x):
    return pltpu.with_memory_space_constraint(x, pltpu.VMEM)


def body(outgoing, fine_slot, translator, list_partner, list_kind, list_count):
    box_index = lax.axis_index("box")
    dir_index = lax.axis_index("dir")
    chunk = box_index % 8
    group = box_index // 8

    theta = theta_matrix()
    up = jnp.asarray(parity_table(theta))
    down = jnp.asarray(parity_table(theta.T * (TF / TP)))
    phi = phi_matrix()
    phi_up = jnp.asarray(split_constant(np.kron(np.eye(2), phi.T)))
    phi_down = jnp.asarray(split_constant(np.kron(np.eye(2), phi) * (PF / PP)))

    sent = pl.pallas_call(
        theta_up_kernel,
        out_shape=near(16, 4, 8, 256),
        in_specs=[vmem, vmem],
        out_specs=vmem,
        scratch_shapes=[pltpu.VMEM((4, 8, 2, 8, LANES), f32)],
    )(outgoing, up)
    spread = lax.all_to_all(sent, "dir", split_axis=0, concat_axis=0, tiled=True)

    rows = lax.dynamic_slice_in_dim(list_partner, group * TARGETS, TARGETS, 0)
    kinds = lax.dynamic_slice_in_dim(list_kind, group * TARGETS, TARGETS, 0)
    count = lax.dynamic_slice_in_dim(list_count, group * TARGETS, TARGETS, 0)
    length = rows.shape[1]
    live = jnp.arange(length, dtype=jnp.int32)[None, :] < count[:, None]
    pad = ((0, 0), (0, SLOTS - length))
    rows = jnp.pad(jnp.where(live, rows, -1), pad, constant_values=-1)
    kinds = jnp.pad(kinds, pad, constant_values=-1)
    kinds = kinds.reshape(TARGETS // 8, 8, SLOTS).transpose(0, 2, 1)
    table = lax.dynamic_slice_in_dim(translator, chunk * CHUNK, CHUNK, 2)
    table = table.reshape(table.shape[0], LANES)
    table = jnp.pad(table, ((0, KINDS - table.shape[0]), (0, 0)))
    matrix = pl.pallas_call(
        matrix_kernel,
        grid=(TARGETS // 8,),
        in_specs=[
            pl.BlockSpec((8, SLOTS), lambda i: (i, 0)),
            pl.BlockSpec((1, SLOTS, 8), lambda i: (i, 0, 0)),
            pl.BlockSpec((KINDS, LANES), lambda i: (0, 0)),
        ],
        out_specs=pl.BlockSpec((8, SOURCES, LANES), lambda i: (i, 0, 0)),
        out_shape=shape(TARGETS, SOURCES, LANES),
        scratch_shapes=[pltpu.VMEM((KINDS, 256), bf16), pltpu.VMEM((8 * SLOTS, 256), bf16)],
    )(rows, kinds, table)
    cos_table, sin_table = phase_tables(dir_index)

    packed = pl.pallas_call(
        gather_kernel,
        out_shape=near(32, 4, 8, LANES),
        in_specs=[smem, vmem, vmem, vmem, vmem, pl.BlockSpec(memory_space=pl.ANY)],
        out_specs=vmem,
        scratch_shapes=[
            pltpu.VMEM((64, 8, 512), f32),
            pltpu.VMEM((8, 8, 512), f32),
            pltpu.SMEM((64,), jnp.int32),
        ],
    )(fine_slot, hold(spread), hold(phi_up), cos_table, sin_table, matrix)
    everyone = lax.all_to_all(packed, "box", split_axis=0, concat_axis=0, tiled=True)
    incoming = pl.pallas_call(
        translate_kernel,
        grid=(TARGETS // 8,),
        in_specs=[
            vmem,
            pl.BlockSpec((8, SOURCES, LANES), lambda i: (i, 0, 0)),
        ],
        out_specs=vmem,
        out_shape=near(8, 4, 8, LANES),
        scratch_shapes=[
            pltpu.VMEM((SOURCES * 4, LANES), f32),
            pltpu.VMEM((SOURCES // 8, 6, 8, LANES), f32),
        ],
    )(hold(everyone), matrix)
    groups = [[8 * g + k for k in range(8)] for g in range(4)]
    fields = lax.all_to_all(
        incoming, "box", split_axis=0, concat_axis=0, axis_index_groups=groups, tiled=True
    )
    lowered = pl.pallas_call(
        scatter_kernel,
        out_shape=near(16, 4, 8, 256),
        in_specs=[smem, vmem, vmem, vmem, vmem],
        out_specs=vmem,
        scratch_shapes=[
            pltpu.VMEM((8, 8, 512), f32),
            pltpu.VMEM((8, 8, 512), f32),
            pltpu.VMEM((64, 8, 512), f32),
        ],
    )(fine_slot, hold(fields), hold(phi_down), cos_table, sin_table)
    back = lax.all_to_all(lowered, "dir", split_axis=0, concat_axis=0, tiled=True)
    return pl.pallas_call(
        theta_down_kernel,
        out_shape=shape(4, 8, TF * PF),
        in_specs=[vmem, vmem],
        out_specs=vmem,
        scratch_shapes=[pltpu.VMEM((4, 16, 2, 8, LANES), f32)],
    )(hold(back), hold(down))


def solution(mesh):
    placed = (P(("box", "dir"), None, None), P("box"), P(None, None, "dir"), P(), P(), P())
    return jax.shard_map(
        body, mesh=mesh, in_specs=placed, out_specs=P(("box", "dir"), None, None), check_vma=False
    )
```

```python
import numpy as np

import jax
import jax.numpy as jnp
from jax import lax
from jax.experimental import pallas as pl
from jax.experimental.pallas import tpu as pltpu
from jax.sharding import PartitionSpec as P

TF = 32
PF = 64
TP = 64
PP = 128
LANES = 128
SLOTS = 192
KINDS = 384
TARGETS = 64
SOURCES = 256
CHUNK = 64

wave_shift = 5.0
f32 = jnp.float32
bf16 = jnp.bfloat16


def theta_matrix():
    a = (np.arange(TP) + 0.5) * np.pi / TP
    b = (np.arange(TF) + 0.5) * np.pi / TF
    m = np.arange(1, TF)
    series = np.cos(a[:, None, None] * m) * np.cos(b[None, :, None] * m)
    return (1.0 + 2.0 * series.sum(2)) / TF


def phi_matrix():
    e = 2 * np.pi * (np.arange(PP)[:, None] / PP - np.arange(PF)[None, :] / PF)
    k = np.arange(1, PF // 2)
    series = np.cos(e[:, :, None] * k).sum(2)
    return (1.0 + 2.0 * series + np.cos(e * (PF // 2))) / PF


def pair_table(matrix):
    n_out, n_in = matrix.shape
    m = matrix.reshape(n_out // 2, 2, n_in // 2, 2).transpose(0, 2, 1, 3)
    same = np.stack([m[:, :, 0, 0], m[:, :, 1, 1]], -1)
    cross = np.stack([m[:, :, 1, 0], m[:, :, 0, 1]], -1)
    table = np.repeat(np.stack([same, cross], 2), PF, axis=3)
    return table.reshape(n_out // 2, n_in, LANES).astype(np.float32)


def split(x):
    high = x.astype(bf16)
    return high, (x - high.astype(f32)).astype(bf16)


def split_constant(x):
    high = np.asarray(x, np.float32).astype(jnp.bfloat16)
    low = (np.asarray(x, np.float32) - high.astype(np.float32)).astype(jnp.bfloat16)
    return np.stack([high, low])


def swap_halves(x):
    return pltpu.roll(x, PF, x.ndim - 1)


def parity_table(matrix):
    n_out, n_in = matrix.shape
    top = matrix[: n_out // 2]
    near, far = top[:, : n_in // 2], top[:, ::-1][:, : n_in // 2]
    return np.concatenate([pair_table((near + far) / 2), pair_table((near - far) / 2)], 1)


def theta_step(parity_ref, c_ref, j, count):
    zero = jnp.zeros((8, LANES), f32)
    sums = [[zero] * 4 for _ in range(4)]
    for i in range(count):
        for odd in range(2):
            base = odd * 2 * count + 2 * i
            cs = c_ref[j, pl.ds(base, 1), :]
            cx = c_ref[j, pl.ds(base + 1, 1), :]
            for f in range(4):
                v = parity_ref[f, i, odd]
                sums[2 * odd][f] = sums[2 * odd][f] + cs * v
                sums[2 * odd + 1][f] = sums[2 * odd + 1][f] + cx * v
    out = []
    for f in range(4):
        es, ex, os, ox = (sums[k][f] for k in range(4))
        out.append(((es + os) + swap_halves(ex + ox), swap_halves(es - os) + (ex - ox)))
    return out


def theta_up_kernel(x_ref, c_ref, o_ref, parity_ref):
    for f in range(4):
        for i in range(8):
            v = x_ref[f, :, pl.ds(i * LANES, LANES)]
            w = swap_halves(x_ref[f, :, pl.ds((15 - i) * LANES, LANES)])
            parity_ref[f, i, 0] = v + w
            parity_ref[f, i, 1] = v - w

    def step(z, carry):
        for part in range(2):
            out = theta_step(parity_ref, c_ref, 2 * z + part, 8)
            for f in range(4):
                o_ref[z, f, :, pl.ds(part * LANES, LANES)] = out[f][0]
                o_ref[15 - z, f, :, pl.ds((1 - part) * LANES, LANES)] = out[f][1]
        return carry

    lax.fori_loop(0, 8, step, 0)


def theta_down_kernel(y_ref, c_ref, o_ref, parity_ref):
    for f in range(4):
        for i in range(16):
            v = y_ref[i // 2, f, :, pl.ds(i % 2 * LANES, LANES)]
            w = swap_halves(y_ref[15 - i // 2, f, :, pl.ds((1 - i % 2) * LANES, LANES)])
            parity_ref[f, i, 0] = v + w
            parity_ref[f, i, 1] = v - w
    for j in range(8):
        out = theta_step(parity_ref, c_ref, j, 16)
        for f in range(4):
            o_ref[f, :, pl.ds(j * LANES, LANES)] = out[f][0]
            o_ref[f, :, pl.ds((15 - j) * LANES, LANES)] = out[f][1]


def channel_sign():
    row = lax.broadcasted_iota(jnp.int32, (8, 4 * LANES), 0)
    return jnp.where(row < 4, 1.0, -1.0).astype(f32)


def gather_kernel(slot_ref, x_ref, w_ref, cos_ref, sin_ref, after_ref, o_ref, raised_ref, parent_ref, inv_ref):
    for i in range(64):
        inv_ref[slot_ref[i] % 64] = i
    for j in range(2):
        high, low = split(x_ref[:, :, :, pl.ds(j * LANES, LANES)].reshape(512, LANES))
        wh, wl = w_ref[0], w_ref[1]
        part = (
            jnp.dot(high, wh, preferred_element_type=f32)
            + jnp.dot(low, wh, preferred_element_type=f32)
            + jnp.dot(high, wl, preferred_element_type=f32)
        )
        raised_ref[:, :, pl.ds(j * 256, 256)] = part.reshape(64, 8, 256)
    sign = channel_sign()

    def step(p, carry):
        plain = jnp.zeros((8, 512), f32)
        turned = jnp.zeros((8, 512), f32)
        for o in range(8):
            v = raised_ref[inv_ref[p * 8 + o]]
            plain = plain + v * cos_ref[pl.ds(o, 1), :]
            turned = turned + v * sin_ref[pl.ds(o, 1), :]
        parent_ref[p] = plain + sign * pltpu.roll(turned, 4, 0)
        return carry

    lax.fori_loop(0, 8, step, 0)
    low_half = lax.broadcasted_iota(jnp.int32, (8, LANES), 1) < PF
    for j in range(4):
        for block in range(4):
            a = parent_ref[2 * j, :, pl.ds(block * LANES, LANES)]
            b = parent_ref[2 * j + 1, :, pl.ds(block * LANES, LANES)]
            even = jnp.where(low_half, a, swap_halves(b))
            odd = jnp.where(low_half, swap_halves(a), b)
            for group in range(4):
                o_ref[group * 8 + 2 * block, j] = even
                o_ref[group * 8 + 2 * block + 1, j] = odd


def matrix_kernel(partner_ref, kind_ref, table_ref, cos_ref, sin_ref, o_ref, token_ref, both_ref, picked_ref):
    @pl.when(pl.program_id(0) == 0)
    def _():
        high, low = split(table_ref[...])
        both_ref[:, :LANES] = high
        both_ref[:, LANES:] = low
        token_ref[...] = jnp.zeros((8, LANES), f32)

    lane_kind = lax.broadcasted_iota(jnp.int32, (SLOTS, KINDS), 1)
    row_source = lax.broadcasted_iota(jnp.int32, (SOURCES, SLOTS), 0)
    pick_kind = jnp.concatenate(
        [
            jnp.where(lane_kind == kind_ref[0, :, p : p + 1], 1.0, 0.0).astype(bf16)
            for p in range(8)
        ],
        0,
    )
    picked_ref[...] = jnp.dot(pick_kind, both_ref[...], preferred_element_type=f32).astype(bf16)
    for p in range(8):
        pick_source = jnp.where(row_source == partner_ref[pl.ds(p, 1), :], 1.0, 0.0).astype(bf16)
        rows = picked_ref[pl.ds(p * SLOTS, SLOTS), :]
        both = jnp.dot(pick_source, rows, preferred_element_type=f32)
        o_ref[p] = both[:, :LANES] + both[:, LANES:]


def fold_rows(parts):
    row = lax.broadcasted_iota(jnp.int32, (8, LANES), 0)
    shift = 1
    while len(parts) > 1:
        first = (row & shift) == 0
        parts = [
            jnp.where(first, a, b) + pltpu.roll(jnp.where(first, b, a), shift, 0)
            for a, b in zip(parts[0::2], parts[1::2])
        ]
        shift *= 2
    return parts[0]


def translate_kernel(s_ref, m_far, o_ref, rows_ref, wide_ref, m_ref, arrived):
    low_half = lax.broadcasted_iota(jnp.int32, (8, LANES), 1) < PF
    top = lax.broadcasted_iota(jnp.int32, (8, LANES), 0) < 4

    def fetch(g):
        four = pl.ds(g * 4, 4)
        return pltpu.make_async_copy(m_far.at[four], m_ref.at[four], arrived.at[g])

    for g in range(TARGETS // 4):
        fetch(g).start()

    def pair(b, carry):
        for j in range(4):
            v = s_ref[b, j]
            w = swap_halves(pltpu.roll(v, 4, 0))
            rows_ref[pl.ds(b * 32 + j * 8, 8), :] = jnp.where(low_half == top, v, w)
        return carry

    lax.fori_loop(0, 32, pair, 0, unroll=4)

    def spread(b, carry):
        plain = [rows_ref[pl.ds(b * 32 + e, 8, stride=4), :] for e in range(4)]
        both = [v + swap_halves(v) for v in plain]
        for e in range(4):
            wide_ref[b, e] = plain[e]
        for h in range(2):
            wide_ref[b, 4 + h] = jnp.where(low_half, both[2 * h], both[2 * h + 1])
        return carry

    lax.fori_loop(0, 32, spread, 0, unroll=4)

    def four_targets(g, carry):
        fetch(g).wait()
        sums = [[jnp.zeros((8, LANES), f32) for _ in range(6)] for _ in range(4)]
        for b in range(SOURCES // 8):
            source = [wide_ref[b, k] for k in range(6)]
            for p in range(4):
                m = m_ref[g * 4 + p, pl.ds(b * 8, 8), :]
                t = m + swap_halves(m)
                for k in range(6):
                    sums[p][k] = sums[p][k] + source[k] * (m if k < 4 else t)
        real, imag = [], []
        for p in range(4):
            turned = [swap_halves(v) for v in sums[p][:4]]
            real.append([x - y for x, y in zip(sums[p], turned)])
            total = [x + y for x, y in zip(sums[p], turned)]
            imag.append(
                [sums[p][4 + h] - jnp.where(low_half, total[2 * h], total[2 * h + 1]) for h in range(2)]
            )
        for j in range(2):
            a, b = 2 * j, 2 * j + 1
            parts = [jnp.where(low_half, x, -y) for x, y in zip(real[a], real[b])]
            for h in range(2):
                x, y = imag[a][h], imag[b][h]
                parts.append(jnp.where(low_half, x, swap_halves(y)))
                parts.append(jnp.where(low_half, swap_halves(x), y))
            o_ref[g // 2, (g % 2) * 2 + j] = fold_rows(parts)
        return carry

    lax.fori_loop(0, TARGETS // 4, four_targets, 0)


def scatter_kernel(slot_ref, x_ref, w_ref, cos_ref, sin_ref, o_ref, plain_ref, turned_ref, child_ref):
    low_half = lax.broadcasted_iota(jnp.int32, (8, LANES), 1) < PF
    for block in range(4):
        for j in range(4):
            a = x_ref[2 * block, j]
            b = x_ref[2 * block + 1, j]
            first = jnp.where(low_half, a, swap_halves(b))
            second = jnp.where(low_half, swap_halves(a), b)
            plain_ref[2 * j, :, pl.ds(block * LANES, LANES)] = first
            plain_ref[2 * j + 1, :, pl.ds(block * LANES, LANES)] = second
    sign = channel_sign()
    for p in range(8):
        turned_ref[p] = -sign * pltpu.roll(plain_ref[p], 4, 0)

    def step(f, carry):
        s = slot_ref[f] % 64
        p = s // 8
        o = s % 8
        child_ref[f] = (
            plain_ref[p] * cos_ref[pl.ds(o, 1), :] + turned_ref[p] * sin_ref[pl.ds(o, 1), :]
        )
        return carry

    lax.fori_loop(0, 64, step, 0, unroll=4)
    for j in range(2):
        high, low = split(child_ref[:, :, pl.ds(j * 256, 256)].reshape(512, 256))
        wh, wl = w_ref[0], w_ref[1]
        part = (
            jnp.dot(high, wh, preferred_element_type=f32)
            + jnp.dot(low, wh, preferred_element_type=f32)
            + jnp.dot(high, wl, preferred_element_type=f32)
        )
        o_ref[:, :, :, pl.ds(j * LANES, LANES)] = part.reshape(16, 4, 8, LANES)


def phase_tables(dir_index):
    theta_here = TP // 16
    theta_index = dir_index * theta_here + jnp.arange(theta_here, dtype=jnp.int32)
    polar = (theta_index.astype(f32) + 0.5) * (jnp.pi / TP)
    azimuth = jnp.arange(PP, dtype=f32) * (2.0 * jnp.pi / PP)
    along_x = (jnp.sin(polar)[:, None] * jnp.cos(azimuth)[None, :]).reshape(1, 512)
    along_y = (jnp.sin(polar)[:, None] * jnp.sin(azimuth)[None, :]).reshape(1, 512)
    along_z = (jnp.cos(polar)[:, None] + 0.0 * azimuth[None, :]).reshape(1, 512)
    octant = jnp.arange(8, dtype=jnp.int32)[:, None]
    sign_x = (2 * (octant % 2) - 1).astype(f32)
    sign_y = (2 * (octant // 2 % 2) - 1).astype(f32)
    sign_z = (2 * (octant // 4) - 1).astype(f32)
    angle = wave_shift * (sign_x * along_x + sign_y * along_y + sign_z * along_z)
    return jnp.cos(angle), jnp.sin(angle)


vmem = pl.BlockSpec(memory_space=pltpu.VMEM)
smem = pl.BlockSpec(memory_space=pltpu.SMEM)


def shape(*dims):
    return jax.ShapeDtypeStruct(dims, f32)


def near(*dims):
    return pltpu.VMEM(dims, f32)


def grant(mib):
    return pltpu.CompilerParams(vmem_limit_bytes=mib << 20)


def hold(x):
    return pltpu.with_memory_space_constraint(x, pltpu.VMEM)


def body(outgoing, fine_slot, translator, list_partner, list_kind, list_count):
    box_index = lax.axis_index("box")
    dir_index = lax.axis_index("dir")
    chunk = box_index % 8
    group = box_index // 8

    theta = theta_matrix()
    up = jnp.asarray(parity_table(theta))
    down = jnp.asarray(parity_table(theta.T * (TF / TP)))
    phi = phi_matrix()
    phi_up = jnp.asarray(split_constant(np.kron(np.eye(2), phi.T)))
    phi_down = jnp.asarray(split_constant(np.kron(np.eye(2), phi) * (PF / PP)))

    sent = pl.pallas_call(
        theta_up_kernel,
        out_shape=near(16, 4, 8, 256),
        in_specs=[vmem, vmem],
        out_specs=vmem,
        scratch_shapes=[pltpu.VMEM((4, 8, 2, 8, LANES), f32)],
        compiler_params=grant(8),
    )(outgoing, up)
    spread = lax.all_to_all(sent, "dir", split_axis=0, concat_axis=0, tiled=True)

    rows = lax.dynamic_slice_in_dim(list_partner, group * TARGETS, TARGETS, 0)
    kinds = lax.dynamic_slice_in_dim(list_kind, group * TARGETS, TARGETS, 0)
    count = lax.dynamic_slice_in_dim(list_count, group * TARGETS, TARGETS, 0)
    length = rows.shape[1]
    live = jnp.arange(length, dtype=jnp.int32)[None, :] < count[:, None]
    pad = ((0, 0), (0, SLOTS - length))
    rows = jnp.pad(jnp.where(live, rows, -1), pad, constant_values=-1)
    kinds = jnp.pad(kinds, pad, constant_values=-1)
    kinds = kinds.reshape(TARGETS // 8, 8, SLOTS).transpose(0, 2, 1)
    table = lax.dynamic_slice_in_dim(translator, chunk * CHUNK, CHUNK, 2)
    table = table.reshape(table.shape[0], LANES)
    table = jnp.pad(table, ((0, KINDS - table.shape[0]), (0, 0)))
    cos_table, sin_table = phase_tables(dir_index)
    matrix, token = pl.pallas_call(
        matrix_kernel,
        grid=(TARGETS // 8,),
        in_specs=[
            pl.BlockSpec((8, SLOTS), lambda i: (i, 0)),
            pl.BlockSpec((1, SLOTS, 8), lambda i: (i, 0, 0)),
            pl.BlockSpec((KINDS, LANES), lambda i: (0, 0)),
            vmem,
            vmem,
        ],
        out_specs=[pl.BlockSpec((8, SOURCES, LANES), lambda i: (i, 0, 0)), vmem],
        out_shape=[pltpu.HBM((TARGETS, SOURCES, LANES), f32), near(8, LANES)],
        scratch_shapes=[pltpu.VMEM((KINDS, 256), bf16), pltpu.VMEM((8 * SLOTS, 256), bf16)],
        compiler_params=grant(16),
    )(rows, kinds, table, hold(cos_table), hold(sin_table))

    packed = pl.pallas_call(
        gather_kernel,
        out_shape=near(32, 4, 8, LANES),
        in_specs=[smem, vmem, vmem, vmem, vmem, vmem],
        out_specs=vmem,
        scratch_shapes=[
            pltpu.VMEM((64, 8, 512), f32),
            pltpu.VMEM((8, 8, 512), f32),
            pltpu.SMEM((64,), jnp.int32),
        ],
        compiler_params=grant(16),
    )(fine_slot, hold(spread), hold(phi_up), hold(cos_table), hold(sin_table), hold(token))
    everyone = lax.all_to_all(packed, "box", split_axis=0, concat_axis=0, tiled=True)
    incoming = pl.pallas_call(
        translate_kernel,
        in_specs=[vmem, pl.BlockSpec(memory_space=pltpu.HBM)],
        out_specs=vmem,
        out_shape=near(8, 4, 8, LANES),
        scratch_shapes=[
            pltpu.VMEM((SOURCES * 4, LANES), f32),
            pltpu.VMEM((SOURCES // 8, 6, 8, LANES), f32),
            pltpu.VMEM((TARGETS, SOURCES, LANES), f32),
            pltpu.SemaphoreType.DMA((TARGETS // 4,)),
        ],
        compiler_params=grant(16),
    )(hold(everyone), pltpu.with_memory_space_constraint(matrix, pltpu.HBM))
    groups = [[8 * g + k for k in range(8)] for g in range(4)]
    fields = lax.all_to_all(
        incoming, "box", split_axis=0, concat_axis=0, axis_index_groups=groups, tiled=True
    )
    lowered = pl.pallas_call(
        scatter_kernel,
        out_shape=near(16, 4, 8, 256),
        in_specs=[smem, vmem, vmem, vmem, vmem],
        out_specs=vmem,
        scratch_shapes=[
            pltpu.VMEM((8, 8, 512), f32),
            pltpu.VMEM((8, 8, 512), f32),
            pltpu.VMEM((64, 8, 512), f32),
        ],
        compiler_params=grant(16),
    )(fine_slot, hold(fields), hold(phi_down), hold(cos_table), hold(sin_table))
    back = lax.all_to_all(lowered, "dir", split_axis=0, concat_axis=0, tiled=True)
    return pl.pallas_call(
        theta_down_kernel,
        out_shape=shape(4, 8, TF * PF),
        in_specs=[vmem, vmem],
        out_specs=vmem,
        scratch_shapes=[pltpu.VMEM((4, 16, 2, 8, LANES), f32)],
        compiler_params=grant(8),
    )(hold(back), hold(down))


def solution(mesh):
    placed = (P(("box", "dir"), None, None), P("box"), P(None, None, "dir"), P(), P(), P())
    return jax.shard_map(
        body, mesh=mesh, in_specs=placed, out_specs=P(("box", "dir"), None, None), check_vma=False
    )
```

```python
import numpy as np

import jax
import jax.numpy as jnp
from jax import lax
from jax.experimental import pallas as pl
from jax.experimental.pallas import tpu as pltpu
from jax.sharding import PartitionSpec as P

TF = 32
PF = 64
TP = 64
PP = 128
LANES = 128
SLOTS = 192
KINDS = 384
TARGETS = 64
SOURCES = 256
CHUNK = 64

wave_shift = 5.0
f32 = jnp.float32
bf16 = jnp.bfloat16


def theta_matrix():
    a = (np.arange(TP) + 0.5) * np.pi / TP
    b = (np.arange(TF) + 0.5) * np.pi / TF
    m = np.arange(1, TF)
    series = np.cos(a[:, None, None] * m) * np.cos(b[None, :, None] * m)
    return (1.0 + 2.0 * series.sum(2)) / TF


def phi_matrix():
    e = 2 * np.pi * (np.arange(PP)[:, None] / PP - np.arange(PF)[None, :] / PF)
    k = np.arange(1, PF // 2)
    series = np.cos(e[:, :, None] * k).sum(2)
    return (1.0 + 2.0 * series + np.cos(e * (PF // 2))) / PF


def pair_table(matrix):
    n_out, n_in = matrix.shape
    m = matrix.reshape(n_out // 2, 2, n_in // 2, 2).transpose(0, 2, 1, 3)
    same = np.stack([m[:, :, 0, 0], m[:, :, 1, 1]], -1)
    cross = np.stack([m[:, :, 1, 0], m[:, :, 0, 1]], -1)
    table = np.repeat(np.stack([same, cross], 2), PF, axis=3)
    return table.reshape(n_out // 2, n_in, LANES).astype(np.float32)


def split(x):
    high = x.astype(bf16)
    return high, (x - high.astype(f32)).astype(bf16)


def split_constant(x):
    high = np.asarray(x, np.float32).astype(jnp.bfloat16)
    low = (np.asarray(x, np.float32) - high.astype(np.float32)).astype(jnp.bfloat16)
    return high, low


def swap_halves(x):
    return pltpu.roll(x, PF, x.ndim - 1)


def parity_table(matrix):
    n_out, n_in = matrix.shape
    top = matrix[: n_out // 2]
    near, far = top[:, : n_in // 2], top[:, ::-1][:, : n_in // 2]
    return np.concatenate([pair_table((near + far) / 2), pair_table((near - far) / 2)], 1)


def theta_step(parity_ref, c_ref, j, count):
    zero = jnp.zeros((8, LANES), f32)
    sums = [[zero] * 4 for _ in range(4)]
    for i in range(count):
        for odd in range(2):
            base = odd * 2 * count + 2 * i
            cs = c_ref[j, pl.ds(base, 1), :]
            cx = c_ref[j, pl.ds(base + 1, 1), :]
            for f in range(4):
                v = parity_ref[f, i, odd]
                sums[2 * odd][f] = sums[2 * odd][f] + cs * v
                sums[2 * odd + 1][f] = sums[2 * odd + 1][f] + cx * v
    out = []
    for f in range(4):
        es, ex, os, ox = (sums[k][f] for k in range(4))
        out.append(((es + os) + swap_halves(ex + ox), swap_halves(es - os) + (ex - ox)))
    return out


def theta_up_kernel(x_far, c_far, o_far, x_ref, c_ref, o_ref, parity_ref, x_in, c_in, o_out):
    def get_x(f):
        return pltpu.make_async_copy(x_far.at[f], x_ref.at[f], x_in.at[f])

    def get_c(z):
        two = pl.ds(2 * z, 2)
        return pltpu.make_async_copy(c_far.at[two], c_ref.at[two], c_in.at[z])

    def put(z):
        return pltpu.make_async_copy(o_ref.at[z], o_far.at[z], o_out.at[z])

    for f in range(4):
        get_x(f).start()
    for z in range(8):
        get_c(z).start()
    for f in range(4):
        get_x(f).wait()
        for i in range(8):
            v = x_ref[f, :, pl.ds(i * LANES, LANES)]
            w = swap_halves(x_ref[f, :, pl.ds((15 - i) * LANES, LANES)])
            parity_ref[f, i, 0] = v + w
            parity_ref[f, i, 1] = v - w

    def step(z, carry):
        get_c(z).wait()
        for part in range(2):
            out = theta_step(parity_ref, c_ref, 2 * z + part, 8)
            for f in range(4):
                o_ref[z, f, :, pl.ds(part * LANES, LANES)] = out[f][0]
                o_ref[15 - z, f, :, pl.ds((1 - part) * LANES, LANES)] = out[f][1]
        put(z).start()
        put(15 - z).start()
        return carry

    lax.fori_loop(0, 8, step, 0)
    for z in range(16):
        put(z).wait()


def theta_down_kernel(y_ref, c_ref, o_far, o_ref, parity_ref, o_out):
    def put(j):
        block = pl.ds(j * LANES, LANES)
        return pltpu.make_async_copy(o_ref.at[:, :, block], o_far.at[:, :, block], o_out.at[j])

    for f in range(4):
        for i in range(16):
            v = y_ref[i // 2, f, :, pl.ds(i % 2 * LANES, LANES)]
            w = swap_halves(y_ref[15 - i // 2, f, :, pl.ds((1 - i % 2) * LANES, LANES)])
            parity_ref[f, i, 0] = v + w
            parity_ref[f, i, 1] = v - w
    for j in range(8):
        out = theta_step(parity_ref, c_ref, j, 16)
        for f in range(4):
            o_ref[f, :, pl.ds(j * LANES, LANES)] = out[f][0]
            o_ref[f, :, pl.ds((15 - j) * LANES, LANES)] = out[f][1]
        put(j).start()
        put(15 - j).start()
    for j in range(16):
        put(j).wait()


def channel_sign():
    row = lax.broadcasted_iota(jnp.int32, (8, 4 * LANES), 0)
    return jnp.where(row < 4, 1.0, -1.0).astype(f32)


def gather_kernel(slot_ref, x_ref, w_ref, cos_ref, sin_ref, after_ref, o_ref, raised_ref, parent_ref, inv_ref):
    for i in range(64):
        inv_ref[slot_ref[i] % 64] = i
    for j in range(2):
        high, low = split(x_ref[:, :, :, pl.ds(j * LANES, LANES)].reshape(512, LANES))
        both = jnp.concatenate([high, low], 1)
        part = jnp.dot(both, w_ref[:256], preferred_element_type=f32)
        part = part + jnp.dot(high, w_ref[256:], preferred_element_type=f32)
        raised_ref[:, :, pl.ds(j * 256, 256)] = part.reshape(64, 8, 256)
    sign = channel_sign()

    def step(p, carry):
        plain = jnp.zeros((8, 512), f32)
        turned = jnp.zeros((8, 512), f32)
        for o in range(8):
            v = raised_ref[inv_ref[p * 8 + o]]
            plain = plain + v * cos_ref[pl.ds(o, 1), :]
            turned = turned + v * sin_ref[pl.ds(o, 1), :]
        parent_ref[p] = plain + sign * pltpu.roll(turned, 4, 0)
        return carry

    lax.fori_loop(0, 8, step, 0)
    low_half = lax.broadcasted_iota(jnp.int32, (8, LANES), 1) < PF
    for j in range(4):
        for block in range(4):
            a = parent_ref[2 * j, :, pl.ds(block * LANES, LANES)]
            b = parent_ref[2 * j + 1, :, pl.ds(block * LANES, LANES)]
            even = jnp.where(low_half, a, swap_halves(b))
            odd = jnp.where(low_half, swap_halves(a), b)
            for group in range(4):
                o_ref[group * 8 + 2 * block, j] = even
                o_ref[group * 8 + 2 * block + 1, j] = odd


def matrix_kernel(partner_ref, kind_ref, table_ref, cos_ref, sin_ref, o_ref, token_ref, both_ref, picked_ref):
    @pl.when(pl.program_id(0) == 0)
    def _():
        high, low = split(table_ref[...])
        both_ref[:, :LANES] = high
        both_ref[:, LANES:] = low
        token_ref[...] = jnp.zeros((8, LANES), f32)

    lane_kind = lax.broadcasted_iota(jnp.int32, (SLOTS, KINDS), 1)
    row_source = lax.broadcasted_iota(jnp.int32, (SOURCES, SLOTS), 0)
    pick_kind = jnp.concatenate(
        [
            jnp.where(lane_kind == kind_ref[0, :, p : p + 1], 1.0, 0.0).astype(bf16)
            for p in range(8)
        ],
        0,
    )
    picked_ref[...] = jnp.dot(pick_kind, both_ref[...], preferred_element_type=f32).astype(bf16)
    for p in range(8):
        pick_source = jnp.where(row_source == partner_ref[pl.ds(p, 1), :], 1.0, 0.0).astype(bf16)
        rows = picked_ref[pl.ds(p * SLOTS, SLOTS), :]
        both = jnp.dot(pick_source, rows, preferred_element_type=f32)
        o_ref[p] = both[:, :LANES] + both[:, LANES:]


def fold_rows(parts):
    row = lax.broadcasted_iota(jnp.int32, (8, LANES), 0)
    shift = 1
    while len(parts) > 1:
        first = (row & shift) == 0
        parts = [
            jnp.where(first, a, b) + pltpu.roll(jnp.where(first, b, a), shift, 0)
            for a, b in zip(parts[0::2], parts[1::2])
        ]
        shift *= 2
    return parts[0]


def translate_kernel(s_ref, m_far, o_ref, rows_ref, wide_ref, m_ref, arrived):
    low_half = lax.broadcasted_iota(jnp.int32, (8, LANES), 1) < PF
    top = lax.broadcasted_iota(jnp.int32, (8, LANES), 0) < 4

    def fetch(g):
        four = pl.ds(g * 4, 4)
        return pltpu.make_async_copy(m_far.at[four], m_ref.at[four], arrived.at[g])

    for g in range(TARGETS // 4):
        fetch(g).start()

    def pair(b, carry):
        for j in range(4):
            v = s_ref[b, j]
            w = swap_halves(pltpu.roll(v, 4, 0))
            rows_ref[pl.ds(b * 32 + j * 8, 8), :] = jnp.where(low_half == top, v, w)
        return carry

    lax.fori_loop(0, 32, pair, 0, unroll=4)

    def spread(b, carry):
        plain = [rows_ref[pl.ds(b * 32 + e, 8, stride=4), :] for e in range(4)]
        both = [v + swap_halves(v) for v in plain]
        for e in range(4):
            wide_ref[b, e] = plain[e]
        for h in range(2):
            wide_ref[b, 4 + h] = jnp.where(low_half, both[2 * h], both[2 * h + 1])
        return carry

    lax.fori_loop(0, 32, spread, 0, unroll=4)

    def four_targets(g, carry):
        fetch(g).wait()
        sums = [[jnp.zeros((8, LANES), f32) for _ in range(6)] for _ in range(4)]
        for b in range(SOURCES // 8):
            source = [wide_ref[b, k] for k in range(6)]
            for p in range(4):
                m = m_ref[g * 4 + p, pl.ds(b * 8, 8), :]
                t = m + swap_halves(m)
                for k in range(6):
                    sums[p][k] = sums[p][k] + source[k] * (m if k < 4 else t)
        real, imag = [], []
        for p in range(4):
            turned = [swap_halves(v) for v in sums[p][:4]]
            real.append([x - y for x, y in zip(sums[p], turned)])
            total = [x + y for x, y in zip(sums[p], turned)]
            imag.append(
                [sums[p][4 + h] - jnp.where(low_half, total[2 * h], total[2 * h + 1]) for h in range(2)]
            )
        for j in range(2):
            a, b = 2 * j, 2 * j + 1
            parts = [jnp.where(low_half, x, -y) for x, y in zip(real[a], real[b])]
            for h in range(2):
                x, y = imag[a][h], imag[b][h]
                parts.append(jnp.where(low_half, x, swap_halves(y)))
                parts.append(jnp.where(low_half, swap_halves(x), y))
            o_ref[g // 2, (g % 2) * 2 + j] = fold_rows(parts)
        return carry

    lax.fori_loop(0, TARGETS // 4, four_targets, 0)


def scatter_kernel(slot_ref, x_ref, w_ref, cos_ref, sin_ref, o_ref, plain_ref, turned_ref, child_ref):
    low_half = lax.broadcasted_iota(jnp.int32, (8, LANES), 1) < PF
    for block in range(4):
        for j in range(4):
            a = x_ref[2 * block, j]
            b = x_ref[2 * block + 1, j]
            first = jnp.where(low_half, a, swap_halves(b))
            second = jnp.where(low_half, swap_halves(a), b)
            plain_ref[2 * j, :, pl.ds(block * LANES, LANES)] = first
            plain_ref[2 * j + 1, :, pl.ds(block * LANES, LANES)] = second
    sign = channel_sign()
    for p in range(8):
        turned_ref[p] = -sign * pltpu.roll(plain_ref[p], 4, 0)

    def step(f, carry):
        s = slot_ref[f] % 64
        p = s // 8
        o = s % 8
        child_ref[f] = (
            plain_ref[p] * cos_ref[pl.ds(o, 1), :] + turned_ref[p] * sin_ref[pl.ds(o, 1), :]
        )
        return carry

    lax.fori_loop(0, 64, step, 0, unroll=4)
    for j in range(2):
        high, low = split(child_ref[:, :, pl.ds(j * 256, 256)].reshape(512, 256))
        part = jnp.dot(high, w_ref[...], preferred_element_type=f32)
        part = part[:, :LANES] + part[:, LANES:]
        part = part + jnp.dot(low, w_ref[:, :LANES], preferred_element_type=f32)
        o_ref[:, :, :, pl.ds(j * LANES, LANES)] = part.reshape(16, 4, 8, LANES)


def phase_tables(dir_index):
    theta_here = TP // 16
    theta_index = dir_index * theta_here + jnp.arange(theta_here, dtype=jnp.int32)
    polar = (theta_index.astype(f32) + 0.5) * (jnp.pi / TP)
    azimuth = jnp.arange(PP, dtype=f32) * (2.0 * jnp.pi / PP)
    along_x = (jnp.sin(polar)[:, None] * jnp.cos(azimuth)[None, :]).reshape(1, 512)
    along_y = (jnp.sin(polar)[:, None] * jnp.sin(azimuth)[None, :]).reshape(1, 512)
    along_z = (jnp.cos(polar)[:, None] + 0.0 * azimuth[None, :]).reshape(1, 512)
    octant = jnp.arange(8, dtype=jnp.int32)[:, None]
    sign_x = (2 * (octant % 2) - 1).astype(f32)
    sign_y = (2 * (octant // 2 % 2) - 1).astype(f32)
    sign_z = (2 * (octant // 4) - 1).astype(f32)
    angle = wave_shift * (sign_x * along_x + sign_y * along_y + sign_z * along_z)
    return jnp.cos(angle), jnp.sin(angle)


vmem = pl.BlockSpec(memory_space=pltpu.VMEM)
smem = pl.BlockSpec(memory_space=pltpu.SMEM)
hbm = pl.BlockSpec(memory_space=pltpu.HBM)


def shape(*dims):
    return jax.ShapeDtypeStruct(dims, f32)


def near(*dims):
    return pltpu.VMEM(dims, f32)


def grant(mib):
    return pltpu.CompilerParams(vmem_limit_bytes=mib << 20)


def far(x):
    return pltpu.with_memory_space_constraint(x, pltpu.HBM)


def hold(x):
    return pltpu.with_memory_space_constraint(x, pltpu.VMEM)


def body(outgoing, fine_slot, translator, list_partner, list_kind, list_count):
    box_index = lax.axis_index("box")
    dir_index = lax.axis_index("dir")
    chunk = box_index % 8
    group = box_index // 8

    theta = theta_matrix()
    up = jnp.asarray(parity_table(theta))
    down = jnp.asarray(parity_table(theta.T * (TF / TP)))
    phi = phi_matrix()
    high, low = split_constant(np.kron(np.eye(2), phi.T))
    phi_up = jnp.asarray(np.concatenate([high, high, low], 0))
    high, low = split_constant(np.kron(np.eye(2), phi) * (PF / PP))
    phi_down = jnp.asarray(np.concatenate([high, low], 1))

    sent = pl.pallas_call(
        theta_up_kernel,
        out_shape=pltpu.HBM((16, 4, 8, 256), f32),
        in_specs=[hbm, hbm],
        out_specs=hbm,
        scratch_shapes=[
            pltpu.VMEM((4, 8, TF * PF), f32),
            pltpu.VMEM((16, 32, LANES), f32),
            pltpu.VMEM((16, 4, 8, 256), f32),
            pltpu.VMEM((4, 8, 2, 8, LANES), f32),
            pltpu.SemaphoreType.DMA((4,)),
            pltpu.SemaphoreType.DMA((8,)),
            pltpu.SemaphoreType.DMA((16,)),
        ],
        compiler_params=grant(8),
    )(far(outgoing), far(up))
    spread = lax.all_to_all(sent, "dir", split_axis=0, concat_axis=0, tiled=True)

    rows = lax.dynamic_slice_in_dim(list_partner, group * TARGETS, TARGETS, 0)
    kinds = lax.dynamic_slice_in_dim(list_kind, group * TARGETS, TARGETS, 0)
    count = lax.dynamic_slice_in_dim(list_count, group * TARGETS, TARGETS, 0)
    length = rows.shape[1]
    live = jnp.arange(length, dtype=jnp.int32)[None, :] < count[:, None]
    pad = ((0, 0), (0, SLOTS - length))
    rows = jnp.pad(jnp.where(live, rows, -1), pad, constant_values=-1)
    kinds = jnp.pad(kinds, pad, constant_values=-1)
    kinds = kinds.reshape(TARGETS // 8, 8, SLOTS).transpose(0, 2, 1)
    table = lax.dynamic_slice_in_dim(translator, chunk * CHUNK, CHUNK, 2)
    table = table.reshape(table.shape[0], LANES)
    table = jnp.pad(table, ((0, KINDS - table.shape[0]), (0, 0)))
    cos_table, sin_table = phase_tables(dir_index)
    matrix, token = pl.pallas_call(
        matrix_kernel,
        grid=(TARGETS // 8,),
        in_specs=[
            pl.BlockSpec((8, SLOTS), lambda i: (i, 0)),
            pl.BlockSpec((1, SLOTS, 8), lambda i: (i, 0, 0)),
            pl.BlockSpec((KINDS, LANES), lambda i: (0, 0)),
            vmem,
            vmem,
        ],
        out_specs=[pl.BlockSpec((8, SOURCES, LANES), lambda i: (i, 0, 0)), vmem],
        out_shape=[pltpu.HBM((TARGETS, SOURCES, LANES), f32), near(8, LANES)],
        scratch_shapes=[pltpu.VMEM((KINDS, 256), bf16), pltpu.VMEM((8 * SLOTS, 256), bf16)],
        compiler_params=grant(16),
    )(rows, kinds, table, hold(cos_table), hold(sin_table))

    packed = pl.pallas_call(
        gather_kernel,
        out_shape=near(32, 4, 8, LANES),
        in_specs=[smem, vmem, vmem, vmem, vmem, vmem],
        out_specs=vmem,
        scratch_shapes=[
            pltpu.VMEM((64, 8, 512), f32),
            pltpu.VMEM((8, 8, 512), f32),
            pltpu.SMEM((64,), jnp.int32),
        ],
        compiler_params=grant(16),
    )(fine_slot, hold(spread), hold(phi_up), hold(cos_table), hold(sin_table), hold(token))
    everyone = lax.all_to_all(packed, "box", split_axis=0, concat_axis=0, tiled=True)
    incoming = pl.pallas_call(
        translate_kernel,
        in_specs=[vmem, hbm],
        out_specs=vmem,
        out_shape=near(8, 4, 8, LANES),
        scratch_shapes=[
            pltpu.VMEM((SOURCES * 4, LANES), f32),
            pltpu.VMEM((SOURCES // 8, 6, 8, LANES), f32),
            pltpu.VMEM((TARGETS, SOURCES, LANES), f32),
            pltpu.SemaphoreType.DMA((TARGETS // 4,)),
        ],
        compiler_params=grant(16),
    )(hold(everyone), far(matrix))
    groups = [[8 * g + k for k in range(8)] for g in range(4)]
    fields = lax.all_to_all(
        incoming, "box", split_axis=0, concat_axis=0, axis_index_groups=groups, tiled=True
    )
    lowered = pl.pallas_call(
        scatter_kernel,
        out_shape=near(16, 4, 8, 256),
        in_specs=[smem, vmem, vmem, vmem, vmem],
        out_specs=vmem,
        scratch_shapes=[
            pltpu.VMEM((8, 8, 512), f32),
            pltpu.VMEM((8, 8, 512), f32),
            pltpu.VMEM((64, 8, 512), f32),
        ],
        compiler_params=grant(16),
    )(fine_slot, hold(fields), hold(phi_down), hold(cos_table), hold(sin_table))
    back = lax.all_to_all(lowered, "dir", split_axis=0, concat_axis=0, tiled=True)
    return pl.pallas_call(
        theta_down_kernel,
        out_shape=shape(4, 8, TF * PF),
        in_specs=[vmem, vmem],
        out_specs=hbm,
        scratch_shapes=[
            pltpu.VMEM((4, 8, TF * PF), f32),
            pltpu.VMEM((4, 16, 2, 8, LANES), f32),
            pltpu.SemaphoreType.DMA((16,)),
        ],
        compiler_params=grant(8),
    )(hold(back), hold(down))


def solution(mesh):
    placed = (P(("box", "dir"), None, None), P("box"), P(None, None, "dir"), P(), P(), P())
    return jax.shard_map(
        body, mesh=mesh, in_specs=placed, out_specs=P(("box", "dir"), None, None), check_vma=False
    )
```

```python
import numpy as np

import jax
import jax.numpy as jnp
from jax import lax
from jax.experimental import pallas as pl
from jax.experimental.pallas import tpu as pltpu
from jax.sharding import PartitionSpec as P

TF = 32
PF = 64
TP = 64
PP = 128
LANES = 128
SLOTS = 192
KINDS = 384
TARGETS = 64
SOURCES = 256
CHUNK = 64

wave_shift = 5.0
f32 = jnp.float32
bf16 = jnp.bfloat16


def theta_matrix():
    a = (np.arange(TP) + 0.5) * np.pi / TP
    b = (np.arange(TF) + 0.5) * np.pi / TF
    m = np.arange(1, TF)
    series = np.cos(a[:, None, None] * m) * np.cos(b[None, :, None] * m)
    return (1.0 + 2.0 * series.sum(2)) / TF


def phi_matrix():
    e = 2 * np.pi * (np.arange(PP)[:, None] / PP - np.arange(PF)[None, :] / PF)
    k = np.arange(1, PF // 2)
    series = np.cos(e[:, :, None] * k).sum(2)
    return (1.0 + 2.0 * series + np.cos(e * (PF // 2))) / PF


def pair_table(matrix):
    n_out, n_in = matrix.shape
    m = matrix.reshape(n_out // 2, 2, n_in // 2, 2).transpose(0, 2, 1, 3)
    same = np.stack([m[:, :, 0, 0], m[:, :, 1, 1]], -1)
    cross = np.stack([m[:, :, 1, 0], m[:, :, 0, 1]], -1)
    table = np.repeat(np.stack([same, cross], 2), PF, axis=3)
    return table.reshape(n_out // 2, n_in, LANES).astype(np.float32)


def split(x):
    high = x.astype(bf16)
    return high, (x - high.astype(f32)).astype(bf16)


def split_constant(x):
    high = np.asarray(x, np.float32).astype(jnp.bfloat16)
    low = (np.asarray(x, np.float32) - high.astype(np.float32)).astype(jnp.bfloat16)
    return high, low


def swap_halves(x):
    return pltpu.roll(x, PF, x.ndim - 1)


def parity_table(matrix):
    n_out, n_in = matrix.shape
    top = matrix[: n_out // 2]
    near, far = top[:, : n_in // 2], top[:, ::-1][:, : n_in // 2]
    return np.concatenate([pair_table((near + far) / 2), pair_table((near - far) / 2)], 1)


def theta_step(parity_ref, c_ref, j, count):
    zero = jnp.zeros((8, LANES), f32)
    sums = [[[zero] * 4 for _ in range(4)] for _ in range(2)]
    for i in range(count):
        for odd in range(2):
            base = odd * 2 * count + 2 * i
            scales = [
                [c_ref[j + part, pl.ds(base + k, 1), :] for k in range(2)] for part in range(2)
            ]
            for f in range(4):
                v = parity_ref[f, i, odd]
                for part in range(2):
                    for k in range(2):
                        old = sums[part][2 * odd + k][f]
                        sums[part][2 * odd + k][f] = old + scales[part][k] * v
    out = []
    for part in range(2):
        for f in range(4):
            es, ex, os, ox = (sums[part][k][f] for k in range(4))
            out.append(((es + os) + swap_halves(ex + ox), swap_halves(es - os) + (ex - ox)))
    return out[:4], out[4:]


def theta_up_kernel(x_far, c_far, o_far, x_ref, c_ref, o_ref, parity_ref, x_in, c_in, o_out):
    def get_x(f):
        return pltpu.make_async_copy(x_far.at[f], x_ref.at[f], x_in.at[f])

    def get_c(z):
        two = pl.ds(2 * z, 2)
        return pltpu.make_async_copy(c_far.at[two], c_ref.at[two], c_in.at[z])

    def put(z):
        return pltpu.make_async_copy(o_ref.at[z], o_far.at[z], o_out.at[z])

    for f in range(4):
        get_x(f).start()
    for z in range(8):
        get_c(z).start()
    for f in range(4):
        get_x(f).wait()
        for i in range(8):
            v = x_ref[f, :, pl.ds(i * LANES, LANES)]
            w = swap_halves(x_ref[f, :, pl.ds((15 - i) * LANES, LANES)])
            parity_ref[f, i, 0] = v + w
            parity_ref[f, i, 1] = v - w

    def step(z, carry):
        get_c(z).wait()
        both = theta_step(parity_ref, c_ref, 2 * z, 8)
        for part, out in enumerate(both):
            for f in range(4):
                o_ref[z, f, :, pl.ds(part * LANES, LANES)] = out[f][0]
                o_ref[15 - z, f, :, pl.ds((1 - part) * LANES, LANES)] = out[f][1]
        put(z).start()
        put(15 - z).start()
        return carry

    lax.fori_loop(0, 8, step, 0)
    for z in range(16):
        put(z).wait()


def theta_down_kernel(y_ref, c_ref, o_far, o_ref, parity_ref, o_out):
    def put(j):
        block = pl.ds(pl.multiple_of(j * LANES, LANES), LANES)
        return pltpu.make_async_copy(o_ref.at[:, :, block], o_far.at[:, :, block], o_out.at[j])

    for f in range(4):
        for i in range(16):
            v = y_ref[i // 2, f, :, pl.ds(i % 2 * LANES, LANES)]
            w = swap_halves(y_ref[15 - i // 2, f, :, pl.ds((1 - i % 2) * LANES, LANES)])
            parity_ref[f, i, 0] = v + w
            parity_ref[f, i, 1] = v - w

    def step(q, carry):
        both = theta_step(parity_ref, c_ref, 2 * q, 16)
        for part, out in enumerate(both):
            j = 2 * q + part
            for f in range(4):
                o_ref[f, :, pl.ds(pl.multiple_of(j * LANES, LANES), LANES)] = out[f][0]
                o_ref[f, :, pl.ds(pl.multiple_of((15 - j) * LANES, LANES), LANES)] = out[f][1]
            put(j).start()
            put(15 - j).start()
        return carry

    for q in range(4):
        step(q, 0)
    for j in range(16):
        put(j).wait()


def channel_sign():
    row = lax.broadcasted_iota(jnp.int32, (8, 4 * LANES), 0)
    return jnp.where(row < 4, 1.0, -1.0).astype(f32)


def gather_kernel(inv_ref, x_ref, w_ref, cos_ref, sin_ref, after_ref, o_ref, raised_ref, parent_ref):
    for j in range(2):
        high, low = split(x_ref[:, :, :, pl.ds(j * LANES, LANES)].reshape(512, LANES))
        both = jnp.concatenate([high, low], 1)
        part = jnp.dot(both, w_ref[:256], preferred_element_type=f32)
        part = part + jnp.dot(high, w_ref[256:], preferred_element_type=f32)
        raised_ref[:, :, pl.ds(j * 256, 256)] = part.reshape(64, 8, 256)
    sign = channel_sign()

    def step(p, carry):
        plain = jnp.zeros((8, 512), f32)
        turned = jnp.zeros((8, 512), f32)
        for o in range(8):
            v = raised_ref[inv_ref[p * 8 + o]]
            plain = plain + v * cos_ref[pl.ds(o, 1), :]
            turned = turned + v * sin_ref[pl.ds(o, 1), :]
        parent_ref[p] = plain + sign * pltpu.roll(turned, 4, 0)
        return carry

    lax.fori_loop(0, 8, step, 0, unroll=4)
    low_half = lax.broadcasted_iota(jnp.int32, (8, LANES), 1) < PF
    for j in range(4):
        for block in range(4):
            a = parent_ref[2 * j, :, pl.ds(block * LANES, LANES)]
            b = parent_ref[2 * j + 1, :, pl.ds(block * LANES, LANES)]
            even = jnp.where(low_half, a, swap_halves(b))
            odd = jnp.where(low_half, swap_halves(a), b)
            for group in range(4):
                o_ref[group * 8 + 2 * block, j] = even
                o_ref[group * 8 + 2 * block + 1, j] = odd


def matrix_kernel(partner_ref, kind_ref, table_ref, cos_ref, sin_ref, o_ref, token_ref, both_ref, picked_ref):
    @pl.when(pl.program_id(0) == 0)
    def _():
        high, low = split(table_ref[...])
        both_ref[:, :LANES] = high
        both_ref[:, LANES:] = low
        token_ref[...] = jnp.zeros((8, LANES), f32)

    lane_kind = lax.broadcasted_iota(jnp.int32, (SLOTS, KINDS), 1)
    row_source = lax.broadcasted_iota(jnp.int32, (SOURCES, SLOTS), 0)
    pick_kind = jnp.concatenate(
        [
            jnp.where(lane_kind == kind_ref[0, :, p : p + 1], 1.0, 0.0).astype(bf16)
            for p in range(8)
        ],
        0,
    )
    picked_ref[...] = jnp.dot(pick_kind, both_ref[...], preferred_element_type=f32).astype(bf16)
    for p in range(8):
        pick_source = jnp.where(row_source == partner_ref[pl.ds(p, 1), :], 1.0, 0.0).astype(bf16)
        rows = picked_ref[pl.ds(p * SLOTS, SLOTS), :]
        both = jnp.dot(pick_source, rows, preferred_element_type=f32)
        o_ref[p] = both[:, :LANES] + both[:, LANES:]


def fold_rows(parts):
    row = lax.broadcasted_iota(jnp.int32, (8, LANES), 0)
    shift = 1
    while len(parts) > 1:
        first = (row & shift) == 0
        parts = [
            jnp.where(first, a, b) + pltpu.roll(jnp.where(first, b, a), shift, 0)
            for a, b in zip(parts[0::2], parts[1::2])
        ]
        shift *= 2
    return parts[0]


def translate_kernel(s_ref, m_far, o_ref, rows_ref, wide_ref, m_ref, arrived):
    low_half = lax.broadcasted_iota(jnp.int32, (8, LANES), 1) < PF
    top = lax.broadcasted_iota(jnp.int32, (8, LANES), 0) < 4

    def fetch(g):
        four = pl.ds(g * 4, 4)
        return pltpu.make_async_copy(m_far.at[four], m_ref.at[four], arrived.at[g])

    for g in range(TARGETS // 4):
        fetch(g).start()

    def pair(b, carry):
        for j in range(4):
            v = s_ref[b, j]
            w = swap_halves(pltpu.roll(v, 4, 0))
            rows_ref[pl.ds(b * 32 + j * 8, 8), :] = jnp.where(low_half == top, v, w)
        return carry

    lax.fori_loop(0, 32, pair, 0, unroll=4)

    def spread(b, carry):
        plain = [rows_ref[pl.ds(b * 32 + e, 8, stride=4), :] for e in range(4)]
        both = [v + swap_halves(v) for v in plain]
        for e in range(4):
            wide_ref[b, e] = plain[e]
        for h in range(2):
            wide_ref[b, 4 + h] = jnp.where(low_half, both[2 * h], both[2 * h + 1])
        return carry

    lax.fori_loop(0, 32, spread, 0, unroll=4)

    def four_targets(g, carry):
        fetch(g).wait()
        sums = [[jnp.zeros((8, LANES), f32) for _ in range(6)] for _ in range(4)]
        for b in range(SOURCES // 8):
            source = [wide_ref[b, k] for k in range(6)]
            for p in range(4):
                m = m_ref[g * 4 + p, pl.ds(b * 8, 8), :]
                t = m + swap_halves(m)
                for k in range(6):
                    sums[p][k] = sums[p][k] + source[k] * (m if k < 4 else t)
        real, imag = [], []
        for p in range(4):
            turned = [swap_halves(v) for v in sums[p][:4]]
            real.append([x - y for x, y in zip(sums[p], turned)])
            total = [x + y for x, y in zip(sums[p], turned)]
            imag.append(
                [sums[p][4 + h] - jnp.where(low_half, total[2 * h], total[2 * h + 1]) for h in range(2)]
            )
        for j in range(2):
            a, b = 2 * j, 2 * j + 1
            parts = [jnp.where(low_half, x, -y) for x, y in zip(real[a], real[b])]
            for h in range(2):
                x, y = imag[a][h], imag[b][h]
                parts.append(jnp.where(low_half, x, swap_halves(y)))
                parts.append(jnp.where(low_half, swap_halves(x), y))
            o_ref[g // 2, (g % 2) * 2 + j] = fold_rows(parts)
        return carry

    lax.fori_loop(0, TARGETS // 4, four_targets, 0)


def scatter_kernel(inv_ref, x_ref, w_ref, cos_ref, sin_ref, o_ref, plain_ref, child_ref):
    low_half = lax.broadcasted_iota(jnp.int32, (8, LANES), 1) < PF
    for block in range(4):
        for j in range(4):
            a = x_ref[2 * block, j]
            b = x_ref[2 * block + 1, j]
            first = jnp.where(low_half, a, swap_halves(b))
            second = jnp.where(low_half, swap_halves(a), b)
            plain_ref[2 * j, :, pl.ds(block * LANES, LANES)] = first
            plain_ref[2 * j + 1, :, pl.ds(block * LANES, LANES)] = second
    sign = channel_sign()

    def step(p, carry):
        plain = plain_ref[p]
        turned = -sign * pltpu.roll(plain, 4, 0)
        for o in range(8):
            child_ref[inv_ref[p * 8 + o]] = (
                plain * cos_ref[pl.ds(o, 1), :] + turned * sin_ref[pl.ds(o, 1), :]
            )
        return carry

    lax.fori_loop(0, 8, step, 0, unroll=4)
    for j in range(2):
        high, low = split(child_ref[:, :, pl.ds(j * 256, 256)].reshape(512, 256))
        part = jnp.dot(high, w_ref[...], preferred_element_type=f32)
        part = part[:, :LANES] + part[:, LANES:]
        part = part + jnp.dot(low, w_ref[:, :LANES], preferred_element_type=f32)
        o_ref[:, :, :, pl.ds(j * LANES, LANES)] = part.reshape(16, 4, 8, LANES)


def phase_tables(dir_index):
    theta_here = TP // 16
    theta_index = dir_index * theta_here + jnp.arange(theta_here, dtype=jnp.int32)
    polar = (theta_index.astype(f32) + 0.5) * (jnp.pi / TP)
    azimuth = jnp.arange(PP, dtype=f32) * (2.0 * jnp.pi / PP)
    along_x = (jnp.sin(polar)[:, None] * jnp.cos(azimuth)[None, :]).reshape(1, 512)
    along_y = (jnp.sin(polar)[:, None] * jnp.sin(azimuth)[None, :]).reshape(1, 512)
    along_z = (jnp.cos(polar)[:, None] + 0.0 * azimuth[None, :]).reshape(1, 512)
    octant = jnp.arange(8, dtype=jnp.int32)[:, None]
    sign_x = (2 * (octant % 2) - 1).astype(f32)
    sign_y = (2 * (octant // 2 % 2) - 1).astype(f32)
    sign_z = (2 * (octant // 4) - 1).astype(f32)
    angle = wave_shift * (sign_x * along_x + sign_y * along_y + sign_z * along_z)
    return jnp.cos(angle), jnp.sin(angle)


vmem = pl.BlockSpec(memory_space=pltpu.VMEM)
smem = pl.BlockSpec(memory_space=pltpu.SMEM)
hbm = pl.BlockSpec(memory_space=pltpu.HBM)


def shape(*dims):
    return jax.ShapeDtypeStruct(dims, f32)


def near(*dims):
    return pltpu.VMEM(dims, f32)


def grant(mib):
    return pltpu.CompilerParams(vmem_limit_bytes=mib << 20)


def far(x):
    return pltpu.with_memory_space_constraint(x, pltpu.HBM)


def hold(x):
    return pltpu.with_memory_space_constraint(x, pltpu.VMEM)


def body(outgoing, fine_slot, translator, list_partner, list_kind, list_count):
    box_index = lax.axis_index("box")
    dir_index = lax.axis_index("dir")
    chunk = box_index % 8
    group = box_index // 8

    theta = theta_matrix()
    up = jnp.asarray(parity_table(theta))
    down = jnp.asarray(parity_table(theta.T * (TF / TP)))
    phi = phi_matrix()
    high, low = split_constant(np.kron(np.eye(2), phi.T))
    phi_up = jnp.asarray(np.concatenate([high, high, low], 0))
    high, low = split_constant(np.kron(np.eye(2), phi) * (PF / PP))
    phi_down = jnp.asarray(np.concatenate([high, low], 1))

    sent = pl.pallas_call(
        theta_up_kernel,
        out_shape=pltpu.HBM((16, 4, 8, 256), f32),
        in_specs=[hbm, hbm],
        out_specs=hbm,
        scratch_shapes=[
            pltpu.VMEM((4, 8, TF * PF), f32),
            pltpu.VMEM((16, 32, LANES), f32),
            pltpu.VMEM((16, 4, 8, 256), f32),
            pltpu.VMEM((4, 8, 2, 8, LANES), f32),
            pltpu.SemaphoreType.DMA((4,)),
            pltpu.SemaphoreType.DMA((8,)),
            pltpu.SemaphoreType.DMA((16,)),
        ],
        compiler_params=grant(8),
    )(far(outgoing), far(up))
    spread = lax.all_to_all(sent, "dir", split_axis=0, concat_axis=0, tiled=True)

    rows = lax.dynamic_slice_in_dim(list_partner, group * TARGETS, TARGETS, 0)
    kinds = lax.dynamic_slice_in_dim(list_kind, group * TARGETS, TARGETS, 0)
    count = lax.dynamic_slice_in_dim(list_count, group * TARGETS, TARGETS, 0)
    length = rows.shape[1]
    live = jnp.arange(length, dtype=jnp.int32)[None, :] < count[:, None]
    pad = ((0, 0), (0, SLOTS - length))
    rows = jnp.pad(jnp.where(live, rows, -1), pad, constant_values=-1)
    kinds = jnp.pad(kinds, pad, constant_values=-1)
    kinds = kinds.reshape(TARGETS // 8, 8, SLOTS).transpose(0, 2, 1)
    table = lax.dynamic_slice_in_dim(translator, chunk * CHUNK, CHUNK, 2)
    table = table.reshape(table.shape[0], LANES)
    table = jnp.pad(table, ((0, KINDS - table.shape[0]), (0, 0)))
    cos_table, sin_table = phase_tables(dir_index)
    place = jnp.arange(64, dtype=jnp.int32)
    found = fine_slot[None, :] % 64 == place[:, None]
    inverse = jnp.sum(jnp.where(found, place[None, :], 0), 1)
    matrix, token = pl.pallas_call(
        matrix_kernel,
        grid=(TARGETS // 8,),
        in_specs=[
            pl.BlockSpec((8, SLOTS), lambda i: (i, 0)),
            pl.BlockSpec((1, SLOTS, 8), lambda i: (i, 0, 0)),
            pl.BlockSpec((KINDS, LANES), lambda i: (0, 0)),
            vmem,
            vmem,
        ],
        out_specs=[pl.BlockSpec((8, SOURCES, LANES), lambda i: (i, 0, 0)), vmem],
        out_shape=[pltpu.HBM((TARGETS, SOURCES, LANES), f32), near(8, LANES)],
        scratch_shapes=[pltpu.VMEM((KINDS, 256), bf16), pltpu.VMEM((8 * SLOTS, 256), bf16)],
        compiler_params=grant(16),
    )(rows, kinds, table, hold(cos_table), hold(sin_table))

    packed = pl.pallas_call(
        gather_kernel,
        out_shape=near(32, 4, 8, LANES),
        in_specs=[smem, vmem, vmem, vmem, vmem, vmem],
        out_specs=vmem,
        scratch_shapes=[
            pltpu.VMEM((64, 8, 512), f32),
            pltpu.VMEM((8, 8, 512), f32),
        ],
        compiler_params=grant(16),
    )(inverse, hold(spread), hold(phi_up), hold(cos_table), hold(sin_table), hold(token))
    everyone = lax.all_to_all(packed, "box", split_axis=0, concat_axis=0, tiled=True)
    incoming = pl.pallas_call(
        translate_kernel,
        in_specs=[vmem, hbm],
        out_specs=vmem,
        out_shape=near(8, 4, 8, LANES),
        scratch_shapes=[
            pltpu.VMEM((SOURCES * 4, LANES), f32),
            pltpu.VMEM((SOURCES // 8, 6, 8, LANES), f32),
            pltpu.VMEM((TARGETS, SOURCES, LANES), f32),
            pltpu.SemaphoreType.DMA((TARGETS // 4,)),
        ],
        compiler_params=grant(16),
    )(hold(everyone), far(matrix))
    groups = [[8 * g + k for k in range(8)] for g in range(4)]
    fields = lax.all_to_all(
        incoming, "box", split_axis=0, concat_axis=0, axis_index_groups=groups, tiled=True
    )
    lowered = pl.pallas_call(
        scatter_kernel,
        out_shape=near(16, 4, 8, 256),
        in_specs=[smem, vmem, vmem, vmem, vmem],
        out_specs=vmem,
        scratch_shapes=[
            pltpu.VMEM((8, 8, 512), f32),
            pltpu.VMEM((64, 8, 512), f32),
        ],
        compiler_params=grant(16),
    )(inverse, hold(fields), hold(phi_down), hold(cos_table), hold(sin_table))
    back = lax.all_to_all(lowered, "dir", split_axis=0, concat_axis=0, tiled=True)
    return pl.pallas_call(
        theta_down_kernel,
        out_shape=shape(4, 8, TF * PF),
        in_specs=[vmem, vmem],
        out_specs=hbm,
        scratch_shapes=[
            pltpu.VMEM((4, 8, TF * PF), f32),
            pltpu.VMEM((4, 16, 2, 8, LANES), f32),
            pltpu.SemaphoreType.DMA((16,)),
        ],
        compiler_params=grant(8),
    )(hold(back), hold(down))


def solution(mesh):
    placed = (P(("box", "dir"), None, None), P("box"), P(None, None, "dir"), P(), P(), P())
    return jax.shard_map(
        body, mesh=mesh, in_specs=placed, out_specs=P(("box", "dir"), None, None), check_vma=False
    )
```

```python
import numpy as np

import jax
import jax.numpy as jnp
from jax import lax
from jax.experimental import pallas as pl
from jax.experimental.pallas import tpu as pltpu
from jax.sharding import PartitionSpec as P

TF = 32
PF = 64
TP = 64
PP = 128
LANES = 128
SLOTS = 192
KINDS = 384
TARGETS = 64
SOURCES = 256
CHUNK = 64

wave_shift = 5.0
f32 = jnp.float32
bf16 = jnp.bfloat16


def theta_matrix():
    a = (np.arange(TP) + 0.5) * np.pi / TP
    b = (np.arange(TF) + 0.5) * np.pi / TF
    m = np.arange(1, TF)
    series = np.cos(a[:, None, None] * m) * np.cos(b[None, :, None] * m)
    return (1.0 + 2.0 * series.sum(2)) / TF


def phi_matrix():
    e = 2 * np.pi * (np.arange(PP)[:, None] / PP - np.arange(PF)[None, :] / PF)
    k = np.arange(1, PF // 2)
    series = np.cos(e[:, :, None] * k).sum(2)
    return (1.0 + 2.0 * series + np.cos(e * (PF // 2))) / PF


def pair_table(matrix):
    n_out, n_in = matrix.shape
    m = matrix.reshape(n_out // 2, 2, n_in // 2, 2).transpose(0, 2, 1, 3)
    same = np.stack([m[:, :, 0, 0], m[:, :, 1, 1]], -1)
    cross = np.stack([m[:, :, 1, 0], m[:, :, 0, 1]], -1)
    table = np.repeat(np.stack([same, cross], 2), PF, axis=3)
    return table.reshape(n_out // 2, n_in, LANES).astype(np.float32)


def split(x):
    high = x.astype(bf16)
    return high, (x - high.astype(f32)).astype(bf16)


def split_constant(x):
    high = np.asarray(x, np.float32).astype(jnp.bfloat16)
    low = (np.asarray(x, np.float32) - high.astype(np.float32)).astype(jnp.bfloat16)
    return high, low


def swap_halves(x):
    return pltpu.roll(x, PF, x.ndim - 1)


def parity_table(matrix):
    n_out, n_in = matrix.shape
    top = matrix[: n_out // 2]
    near, far = top[:, : n_in // 2], top[:, ::-1][:, : n_in // 2]
    return np.concatenate([pair_table((near + far) / 2), pair_table((near - far) / 2)], 1)


def theta_step(parity_ref, c_ref, j, count):
    zero = jnp.zeros((8, LANES), f32)
    sums = [[[zero] * 4 for _ in range(4)] for _ in range(2)]
    for i in range(count):
        for odd in range(2):
            base = odd * 2 * count + 2 * i
            scales = [
                [c_ref[j + part, pl.ds(base + k, 1), :] for k in range(2)] for part in range(2)
            ]
            for f in range(4):
                v = parity_ref[f, i, odd]
                for part in range(2):
                    for k in range(2):
                        old = sums[part][2 * odd + k][f]
                        sums[part][2 * odd + k][f] = old + scales[part][k] * v
    out = []
    for part in range(2):
        for f in range(4):
            es, ex, os, ox = (sums[part][k][f] for k in range(4))
            out.append(((es + os) + swap_halves(ex + ox), swap_halves(es - os) + (ex - ox)))
    return out[:4], out[4:]


def theta_up_kernel(x_far, c_far, o_far, x_ref, c_ref, o_ref, parity_ref, x_in, c_in, o_out):
    def get_x(f):
        return pltpu.make_async_copy(x_far.at[f], x_ref.at[f], x_in.at[f])

    def get_c(z):
        two = pl.ds(2 * z, 2)
        return pltpu.make_async_copy(c_far.at[two], c_ref.at[two], c_in.at[z])

    def put(z):
        return pltpu.make_async_copy(o_ref.at[z], o_far.at[z], o_out.at[z])

    for f in range(4):
        get_x(f).start()
    for z in range(8):
        get_c(z).start()
    for f in range(4):
        get_x(f).wait()
        for i in range(8):
            v = x_ref[f, :, pl.ds(i * LANES, LANES)]
            w = swap_halves(x_ref[f, :, pl.ds((15 - i) * LANES, LANES)])
            parity_ref[f, i, 0] = v + w
            parity_ref[f, i, 1] = v - w

    def step(z, carry):
        get_c(z).wait()
        both = theta_step(parity_ref, c_ref, 2 * z, 8)
        for part, out in enumerate(both):
            for f in range(4):
                o_ref[z, f, :, pl.ds(part * LANES, LANES)] = out[f][0]
                o_ref[15 - z, f, :, pl.ds((1 - part) * LANES, LANES)] = out[f][1]
        put(z).start()
        put(15 - z).start()
        return carry

    lax.fori_loop(0, 8, step, 0)
    for z in range(16):
        put(z).wait()


def theta_down_kernel(y_ref, c_ref, o_far, o_ref, parity_ref, o_out):
    def put(j):
        block = pl.ds(pl.multiple_of(j * LANES, LANES), LANES)
        return pltpu.make_async_copy(o_ref.at[:, :, block], o_far.at[:, :, block], o_out.at[j])

    for f in range(4):
        for i in range(16):
            v = y_ref[i // 2, f, :, pl.ds(i % 2 * LANES, LANES)]
            w = swap_halves(y_ref[15 - i // 2, f, :, pl.ds((1 - i % 2) * LANES, LANES)])
            parity_ref[f, i, 0] = v + w
            parity_ref[f, i, 1] = v - w

    def step(q, carry):
        both = theta_step(parity_ref, c_ref, 2 * q, 16)
        for part, out in enumerate(both):
            j = 2 * q + part
            for f in range(4):
                o_ref[f, :, pl.ds(pl.multiple_of(j * LANES, LANES), LANES)] = out[f][0]
                o_ref[f, :, pl.ds(pl.multiple_of((15 - j) * LANES, LANES), LANES)] = out[f][1]
            put(j).start()
            put(15 - j).start()
        return carry

    for q in range(4):
        step(q, 0)
    for j in range(16):
        put(j).wait()


def channel_sign():
    row = lax.broadcasted_iota(jnp.int32, (8, 4 * LANES), 0)
    return jnp.where(row < 4, 1.0, -1.0).astype(f32)


def gather_kernel(inv_ref, x_ref, w_ref, cos_ref, sin_ref, after_ref, o_ref, raised_ref, parent_ref):
    for j in range(2):
        high, low = split(x_ref[:, :, :, pl.ds(j * LANES, LANES)].reshape(512, LANES))
        both = jnp.concatenate([high, low], 1)
        part = jnp.dot(both, w_ref[:256], preferred_element_type=f32)
        part = part + jnp.dot(high, w_ref[256:], preferred_element_type=f32)
        raised_ref[:, :, pl.ds(j * 256, 256)] = part.reshape(64, 8, 256)
    sign = channel_sign()

    def step(p, carry):
        plain = jnp.zeros((8, 512), f32)
        turned = jnp.zeros((8, 512), f32)
        for o in range(8):
            v = raised_ref[inv_ref[p * 8 + o]]
            plain = plain + v * cos_ref[pl.ds(o, 1), :]
            turned = turned + v * sin_ref[pl.ds(o, 1), :]
        parent_ref[p] = plain + sign * pltpu.roll(turned, 4, 0)
        return carry

    lax.fori_loop(0, 8, step, 0, unroll=4)
    low_half = lax.broadcasted_iota(jnp.int32, (8, LANES), 1) < PF
    top = lax.broadcasted_iota(jnp.int32, (8, LANES), 0) < 4
    for j in range(4):
        for block in range(4):
            a = parent_ref[2 * j, :, pl.ds(block * LANES, LANES)]
            b = parent_ref[2 * j + 1, :, pl.ds(block * LANES, LANES)]
            real = jnp.where(top, a, pltpu.roll(b, 4, 0))
            imag = jnp.where(top, pltpu.roll(a, 4, 0), b)
            even = jnp.where(low_half, real, swap_halves(imag))
            odd = jnp.where(low_half, swap_halves(real), imag)
            for group in range(4):
                dest = group * 8 + 2 * block
                o_ref[pl.ds(dest * 32 + j * 8, 8), :] = even
                o_ref[pl.ds(dest * 32 + 32 + j * 8, 8), :] = odd


def matrix_kernel(partner_ref, kind_ref, table_ref, cos_ref, sin_ref, o_ref, token_ref, both_ref, picked_ref):
    @pl.when(pl.program_id(0) == 0)
    def _():
        high, low = split(table_ref[...])
        both_ref[:, :LANES] = high
        both_ref[:, LANES:] = low
        token_ref[...] = jnp.zeros((8, LANES), f32)

    lane_kind = lax.broadcasted_iota(jnp.int32, (SLOTS, KINDS), 1)
    row_source = lax.broadcasted_iota(jnp.int32, (SOURCES, SLOTS), 0)
    pick_kind = jnp.concatenate(
        [
            jnp.where(lane_kind == kind_ref[0, :, p : p + 1], 1.0, 0.0).astype(bf16)
            for p in range(8)
        ],
        0,
    )
    picked_ref[...] = jnp.dot(pick_kind, both_ref[...], preferred_element_type=f32).astype(bf16)
    for p in range(8):
        pick_source = jnp.where(row_source == partner_ref[pl.ds(p, 1), :], 1.0, 0.0).astype(bf16)
        rows = picked_ref[pl.ds(p * SLOTS, SLOTS), :]
        both = jnp.dot(pick_source, rows, preferred_element_type=f32)
        o_ref[p] = both[:, :LANES] + both[:, LANES:]


def fold_rows(parts):
    row = lax.broadcasted_iota(jnp.int32, (8, LANES), 0)
    shift = 1
    while len(parts) > 1:
        first = (row & shift) == 0
        parts = [
            jnp.where(first, a, b) + pltpu.roll(jnp.where(first, b, a), shift, 0)
            for a, b in zip(parts[0::2], parts[1::2])
        ]
        shift *= 2
    return parts[0]


def translate_kernel(s_ref, m_far, o_ref, wide_ref, m_ref, arrived):
    low_half = lax.broadcasted_iota(jnp.int32, (8, LANES), 1) < PF

    def fetch(g):
        four = pl.ds(g * 4, 4)
        return pltpu.make_async_copy(m_far.at[four], m_ref.at[four], arrived.at[g])

    for g in range(TARGETS // 4):
        fetch(g).start()

    def spread(b, carry):
        plain = [s_ref[pl.ds(b * 32 + e, 8, stride=4), :] for e in range(4)]
        both = [v + swap_halves(v) for v in plain]
        for e in range(4):
            wide_ref[b, e] = plain[e]
        for h in range(2):
            wide_ref[b, 4 + h] = jnp.where(low_half, both[2 * h], both[2 * h + 1])
        return carry

    lax.fori_loop(0, 32, spread, 0, unroll=4)

    def four_targets(g):
        sums = [[jnp.zeros((8, LANES), f32) for _ in range(6)] for _ in range(4)]
        for b in range(SOURCES // 8):
            source = [wide_ref[b, k] for k in range(6)]
            for p in range(4):
                m = m_ref[g * 4 + p, pl.ds(b * 8, 8), :]
                t = m + swap_halves(m)
                for k in range(6):
                    sums[p][k] = sums[p][k] + source[k] * (m if k < 4 else t)
        real, imag = [], []
        for p in range(4):
            turned = [swap_halves(v) for v in sums[p][:4]]
            real.append([x - y for x, y in zip(sums[p], turned)])
            total = [x + y for x, y in zip(sums[p], turned)]
            imag.append(
                [sums[p][4 + h] - jnp.where(low_half, total[2 * h], total[2 * h + 1]) for h in range(2)]
            )
        for j in range(2):
            a, b = 2 * j, 2 * j + 1
            parts = [jnp.where(low_half, x, -y) for x, y in zip(real[a], real[b])]
            for h in range(2):
                x, y = imag[a][h], imag[b][h]
                parts.append(jnp.where(low_half, x, swap_halves(y)))
                parts.append(jnp.where(low_half, swap_halves(x), y))
            o_ref[g // 2, (g % 2) * 2 + j] = fold_rows(parts)

    def step(q, carry):
        fetch(2 * q).wait()
        fetch(2 * q + 1).wait()
        four_targets(2 * q)
        four_targets(2 * q + 1)
        return carry

    lax.fori_loop(0, TARGETS // 8, step, 0)


def scatter_kernel(inv_ref, x_ref, w_ref, cos_ref, sin_ref, o_ref, plain_ref, child_ref):
    low_half = lax.broadcasted_iota(jnp.int32, (8, LANES), 1) < PF
    for block in range(4):
        for j in range(4):
            a = x_ref[2 * block, j]
            b = x_ref[2 * block + 1, j]
            first = jnp.where(low_half, a, swap_halves(b))
            second = jnp.where(low_half, swap_halves(a), b)
            plain_ref[2 * j, :, pl.ds(block * LANES, LANES)] = first
            plain_ref[2 * j + 1, :, pl.ds(block * LANES, LANES)] = second
    sign = channel_sign()

    def step(p, carry):
        plain = plain_ref[p]
        turned = -sign * pltpu.roll(plain, 4, 0)
        for o in range(8):
            child_ref[inv_ref[p * 8 + o]] = (
                plain * cos_ref[pl.ds(o, 1), :] + turned * sin_ref[pl.ds(o, 1), :]
            )
        return carry

    lax.fori_loop(0, 8, step, 0, unroll=4)
    for j in range(2):
        high, low = split(child_ref[:, :, pl.ds(j * 256, 256)].reshape(512, 256))
        part = jnp.dot(high, w_ref[...], preferred_element_type=f32)
        part = part[:, :LANES] + part[:, LANES:]
        part = part + jnp.dot(low, w_ref[:, :LANES], preferred_element_type=f32)
        o_ref[:, :, :, pl.ds(j * LANES, LANES)] = part.reshape(16, 4, 8, LANES)


def phase_tables(dir_index):
    theta_here = TP // 16
    theta_index = dir_index * theta_here + jnp.arange(theta_here, dtype=jnp.int32)
    polar = (theta_index.astype(f32) + 0.5) * (jnp.pi / TP)
    azimuth = jnp.arange(PP, dtype=f32) * (2.0 * jnp.pi / PP)
    along_x = (jnp.sin(polar)[:, None] * jnp.cos(azimuth)[None, :]).reshape(1, 512)
    along_y = (jnp.sin(polar)[:, None] * jnp.sin(azimuth)[None, :]).reshape(1, 512)
    along_z = (jnp.cos(polar)[:, None] + 0.0 * azimuth[None, :]).reshape(1, 512)
    octant = jnp.arange(8, dtype=jnp.int32)[:, None]
    sign_x = (2 * (octant % 2) - 1).astype(f32)
    sign_y = (2 * (octant // 2 % 2) - 1).astype(f32)
    sign_z = (2 * (octant // 4) - 1).astype(f32)
    angle = wave_shift * (sign_x * along_x + sign_y * along_y + sign_z * along_z)
    return jnp.cos(angle), jnp.sin(angle)


vmem = pl.BlockSpec(memory_space=pltpu.VMEM)
smem = pl.BlockSpec(memory_space=pltpu.SMEM)
hbm = pl.BlockSpec(memory_space=pltpu.HBM)


def shape(*dims):
    return jax.ShapeDtypeStruct(dims, f32)


def near(*dims):
    return pltpu.VMEM(dims, f32)


def grant(mib):
    return pltpu.CompilerParams(vmem_limit_bytes=mib << 20)


def far(x):
    return pltpu.with_memory_space_constraint(x, pltpu.HBM)


def hold(x):
    return pltpu.with_memory_space_constraint(x, pltpu.VMEM)


def body(outgoing, fine_slot, translator, list_partner, list_kind, list_count):
    box_index = lax.axis_index("box")
    dir_index = lax.axis_index("dir")
    chunk = box_index % 8
    group = box_index // 8

    theta = theta_matrix()
    up = jnp.asarray(parity_table(theta))
    down = jnp.asarray(parity_table(theta.T * (TF / TP)))
    phi = phi_matrix()
    high, low = split_constant(np.kron(np.eye(2), phi.T))
    phi_up = jnp.asarray(np.concatenate([high, high, low], 0))
    high, low = split_constant(np.kron(np.eye(2), phi) * (PF / PP))
    phi_down = jnp.asarray(np.concatenate([high, low], 1))

    sent = pl.pallas_call(
        theta_up_kernel,
        out_shape=pltpu.HBM((16, 4, 8, 256), f32),
        in_specs=[hbm, hbm],
        out_specs=hbm,
        scratch_shapes=[
            pltpu.VMEM((4, 8, TF * PF), f32),
            pltpu.VMEM((16, 32, LANES), f32),
            pltpu.VMEM((16, 4, 8, 256), f32),
            pltpu.VMEM((4, 8, 2, 8, LANES), f32),
            pltpu.SemaphoreType.DMA((4,)),
            pltpu.SemaphoreType.DMA((8,)),
            pltpu.SemaphoreType.DMA((16,)),
        ],
        compiler_params=grant(8),
    )(far(outgoing), far(up))
    spread = lax.all_to_all(sent, "dir", split_axis=0, concat_axis=0, tiled=True)

    rows = lax.dynamic_slice_in_dim(list_partner, group * TARGETS, TARGETS, 0)
    kinds = lax.dynamic_slice_in_dim(list_kind, group * TARGETS, TARGETS, 0)
    count = lax.dynamic_slice_in_dim(list_count, group * TARGETS, TARGETS, 0)
    length = rows.shape[1]
    live = jnp.arange(length, dtype=jnp.int32)[None, :] < count[:, None]
    pad = ((0, 0), (0, SLOTS - length))
    rows = jnp.pad(jnp.where(live, rows, -1), pad, constant_values=-1)
    kinds = jnp.pad(kinds, pad, constant_values=-1)
    kinds = kinds.reshape(TARGETS // 8, 8, SLOTS).transpose(0, 2, 1)
    table = lax.dynamic_slice_in_dim(translator, chunk * CHUNK, CHUNK, 2)
    table = table.reshape(table.shape[0], LANES)
    table = jnp.pad(table, ((0, KINDS - table.shape[0]), (0, 0)))
    cos_table, sin_table = phase_tables(dir_index)
    place = jnp.arange(64, dtype=jnp.int32)
    found = fine_slot[None, :] % 64 == place[:, None]
    inverse = jnp.sum(jnp.where(found, place[None, :], 0), 1)
    matrix, token = pl.pallas_call(
        matrix_kernel,
        grid=(TARGETS // 8,),
        in_specs=[
            pl.BlockSpec((8, SLOTS), lambda i: (i, 0)),
            pl.BlockSpec((1, SLOTS, 8), lambda i: (i, 0, 0)),
            pl.BlockSpec((KINDS, LANES), lambda i: (0, 0)),
            vmem,
            vmem,
        ],
        out_specs=[pl.BlockSpec((8, SOURCES, LANES), lambda i: (i, 0, 0)), vmem],
        out_shape=[pltpu.HBM((TARGETS, SOURCES, LANES), f32), near(8, LANES)],
        scratch_shapes=[pltpu.VMEM((KINDS, 256), bf16), pltpu.VMEM((8 * SLOTS, 256), bf16)],
        compiler_params=grant(16),
    )(rows, kinds, table, hold(cos_table), hold(sin_table))

    packed = pl.pallas_call(
        gather_kernel,
        out_shape=near(32 * 32, LANES),
        in_specs=[smem, vmem, vmem, vmem, vmem, vmem],
        out_specs=vmem,
        scratch_shapes=[
            pltpu.VMEM((64, 8, 512), f32),
            pltpu.VMEM((8, 8, 512), f32),
        ],
        compiler_params=grant(16),
    )(inverse, hold(spread), hold(phi_up), hold(cos_table), hold(sin_table), hold(token))
    everyone = lax.all_to_all(packed, "box", split_axis=0, concat_axis=0, tiled=True)
    incoming = pl.pallas_call(
        translate_kernel,
        in_specs=[vmem, hbm],
        out_specs=vmem,
        out_shape=near(8, 4, 8, LANES),
        scratch_shapes=[
            pltpu.VMEM((SOURCES // 8, 6, 8, LANES), f32),
            pltpu.VMEM((TARGETS, SOURCES, LANES), f32),
            pltpu.SemaphoreType.DMA((TARGETS // 4,)),
        ],
        compiler_params=grant(16),
    )(hold(everyone), far(matrix))
    groups = [[8 * g + k for k in range(8)] for g in range(4)]
    fields = lax.all_to_all(
        incoming, "box", split_axis=0, concat_axis=0, axis_index_groups=groups, tiled=True
    )
    lowered = pl.pallas_call(
        scatter_kernel,
        out_shape=near(16, 4, 8, 256),
        in_specs=[smem, vmem, vmem, vmem, vmem],
        out_specs=vmem,
        scratch_shapes=[
            pltpu.VMEM((8, 8, 512), f32),
            pltpu.VMEM((64, 8, 512), f32),
        ],
        compiler_params=grant(16),
    )(inverse, hold(fields), hold(phi_down), hold(cos_table), hold(sin_table))
    back = lax.all_to_all(lowered, "dir", split_axis=0, concat_axis=0, tiled=True)
    return pl.pallas_call(
        theta_down_kernel,
        out_shape=shape(4, 8, TF * PF),
        in_specs=[vmem, vmem],
        out_specs=hbm,
        scratch_shapes=[
            pltpu.VMEM((4, 8, TF * PF), f32),
            pltpu.VMEM((4, 16, 2, 8, LANES), f32),
            pltpu.SemaphoreType.DMA((16,)),
        ],
        compiler_params=grant(8),
    )(hold(back), hold(down))


def solution(mesh):
    placed = (P(("box", "dir"), None, None), P("box"), P(None, None, "dir"), P(), P(), P())
    return jax.shard_map(
        body, mesh=mesh, in_specs=placed, out_specs=P(("box", "dir"), None, None), check_vma=False
    )
```

```python
import numpy as np

import jax
import jax.numpy as jnp
from jax import lax
from jax.experimental import pallas as pl
from jax.experimental.pallas import tpu as pltpu
from jax.sharding import PartitionSpec as P

TF = 32
PF = 64
TP = 64
PP = 128
LANES = 128
SLOTS = 192
KINDS = 256
TARGETS = 128
SOURCES = 256
CHUNK = 32

wave_shift = 5.0
f32 = jnp.float32
bf16 = jnp.bfloat16


def theta_matrix():
    a = (np.arange(TP) + 0.5) * np.pi / TP
    b = (np.arange(TF) + 0.5) * np.pi / TF
    m = np.arange(1, TF)
    series = np.cos(a[:, None, None] * m) * np.cos(b[None, :, None] * m)
    return (1.0 + 2.0 * series.sum(2)) / TF


def phi_matrix():
    e = 2 * np.pi * (np.arange(PP)[:, None] / PP - np.arange(PF)[None, :] / PF)
    k = np.arange(1, PF // 2)
    series = np.cos(e[:, :, None] * k).sum(2)
    return (1.0 + 2.0 * series + np.cos(e * (PF // 2))) / PF


def pair_table(matrix):
    n_out, n_in = matrix.shape
    m = matrix.reshape(n_out // 2, 2, n_in // 2, 2).transpose(0, 2, 1, 3)
    same = np.stack([m[:, :, 0, 0], m[:, :, 1, 1]], -1)
    cross = np.stack([m[:, :, 1, 0], m[:, :, 0, 1]], -1)
    table = np.repeat(np.stack([same, cross], 2), PF, axis=3)
    return table.reshape(n_out // 2, n_in, LANES).astype(np.float32)


def split(x):
    high = x.astype(bf16)
    return high, (x - high.astype(f32)).astype(bf16)


def split_constant(x):
    high = np.asarray(x, np.float32).astype(jnp.bfloat16)
    low = (np.asarray(x, np.float32) - high.astype(np.float32)).astype(jnp.bfloat16)
    return high, low


def swap_halves(x):
    return pltpu.roll(x, PF, x.ndim - 1)


def parity_table(matrix):
    n_out, n_in = matrix.shape
    top = matrix[: n_out // 2]
    near, far = top[:, : n_in // 2], top[:, ::-1][:, : n_in // 2]
    return np.concatenate([pair_table((near + far) / 2), pair_table((near - far) / 2)], 1)


def lane_quarter():
    return lax.broadcasted_iota(jnp.int32, (8, LANES), 1) // 32


def transpose_quarters(x):
    low_half = lane_quarter() < 2
    even = lane_quarter() % 2 == 0
    half = [
        (jnp.where(low_half, a, swap_halves(b)), jnp.where(low_half, swap_halves(a), b))
        for a, b in ((x[0], x[2]), (x[1], x[3]))
    ]
    out = []
    for k in range(2):
        a, b = half[0][k], half[1][k]
        out.append(jnp.where(even, a, pltpu.roll(b, 32, 1)))
        out.append(jnp.where(even, pltpu.roll(a, 96, 1), b))
    return out


def theta_step(parity_ref, c_ref, j, count):
    zero = jnp.zeros((8, LANES), f32)
    sums = [[[zero] * 4 for _ in range(4)] for _ in range(2)]
    for i in range(count):
        for odd in range(2):
            base = odd * 2 * count + 2 * i
            scales = [
                [c_ref[j + part, pl.ds(base + k, 1), :] for k in range(2)] for part in range(2)
            ]
            for f in range(4):
                v = parity_ref[f, i, odd]
                for part in range(2):
                    for k in range(2):
                        old = sums[part][2 * odd + k][f]
                        sums[part][2 * odd + k][f] = old + scales[part][k] * v
    out = []
    for part in range(2):
        for f in range(4):
            es, ex, os, ox = (sums[part][k][f] for k in range(4))
            out.append(((es + os) + swap_halves(ex + ox), swap_halves(es - os) + (ex - ox)))
    return out[:4], out[4:]


def theta_up_kernel(x_far, c_far, o_far, x_ref, c_ref, o_ref, parity_ref, x_in, c_in, o_out):
    def get_x(f):
        return pltpu.make_async_copy(x_far.at[f], x_ref.at[f], x_in.at[f])

    def get_c(z):
        two = pl.ds(2 * z, 2)
        return pltpu.make_async_copy(c_far.at[two], c_ref.at[two], c_in.at[z])

    def put(z):
        return pltpu.make_async_copy(o_ref.at[z], o_far.at[z], o_out.at[z])

    for f in range(4):
        get_x(f).start()
    for z in range(8):
        get_c(z).start()
    for f in range(4):
        get_x(f).wait()
        for i in range(8):
            v = x_ref[f, :, pl.ds(i * LANES, LANES)]
            w = swap_halves(x_ref[f, :, pl.ds((15 - i) * LANES, LANES)])
            parity_ref[f, i, 0] = v + w
            parity_ref[f, i, 1] = v - w

    def step(z, carry):
        get_c(z).wait()
        both = theta_step(parity_ref, c_ref, 2 * z, 8)
        for part, out in enumerate(both):
            for f in range(4):
                o_ref[z, f, :, pl.ds(part * LANES, LANES)] = out[f][0]
                o_ref[15 - z, f, :, pl.ds((1 - part) * LANES, LANES)] = out[f][1]
        put(z).start()
        put(15 - z).start()
        return carry

    lax.fori_loop(0, 8, step, 0)
    for z in range(16):
        put(z).wait()


def theta_down_kernel(y_ref, c_ref, o_far, o_ref, parity_ref, o_out):
    def put(j):
        block = pl.ds(pl.multiple_of(j * LANES, LANES), LANES)
        return pltpu.make_async_copy(o_ref.at[:, :, block], o_far.at[:, :, block], o_out.at[j])

    for f in range(4):
        for i in range(16):
            v = y_ref[i // 2, f, :, pl.ds(i % 2 * LANES, LANES)]
            w = swap_halves(y_ref[15 - i // 2, f, :, pl.ds((1 - i % 2) * LANES, LANES)])
            parity_ref[f, i, 0] = v + w
            parity_ref[f, i, 1] = v - w

    def step(q, carry):
        both = theta_step(parity_ref, c_ref, 2 * q, 16)
        for part, out in enumerate(both):
            j = 2 * q + part
            for f in range(4):
                o_ref[f, :, pl.ds(pl.multiple_of(j * LANES, LANES), LANES)] = out[f][0]
                o_ref[f, :, pl.ds(pl.multiple_of((15 - j) * LANES, LANES), LANES)] = out[f][1]
            put(j).start()
            put(15 - j).start()
        return carry

    for q in range(4):
        step(q, 0)
    for j in range(16):
        put(j).wait()


def channel_sign():
    row = lax.broadcasted_iota(jnp.int32, (8, 4 * LANES), 0)
    return jnp.where(row < 4, 1.0, -1.0).astype(f32)


def gather_kernel(inv_ref, x_ref, w_ref, cos_ref, sin_ref, after_ref, o_ref, raised_ref, parent_ref):
    for j in range(2):
        high, low = split(x_ref[:, :, :, pl.ds(j * LANES, LANES)].reshape(512, LANES))
        both = jnp.concatenate([high, low], 1)
        part = jnp.dot(both, w_ref[:256], preferred_element_type=f32)
        part = part + jnp.dot(high, w_ref[256:], preferred_element_type=f32)
        raised_ref[:, :, pl.ds(j * 256, 256)] = part.reshape(64, 8, 256)
    sign = channel_sign()

    def step(p, carry):
        plain = jnp.zeros((8, 512), f32)
        turned = jnp.zeros((8, 512), f32)
        for o in range(8):
            v = raised_ref[inv_ref[p * 8 + o]]
            plain = plain + v * cos_ref[pl.ds(o, 1), :]
            turned = turned + v * sin_ref[pl.ds(o, 1), :]
        parent_ref[p] = plain + sign * pltpu.roll(turned, 4, 0)
        return carry

    lax.fori_loop(0, 8, step, 0, unroll=4)
    top = lax.broadcasted_iota(jnp.int32, (8, LANES), 0) < 4
    for k in range(2):
        for block in range(4):
            lanes = pl.ds(block * LANES, LANES)
            a, b, c, d = (parent_ref[4 * k + i, :, lanes] for i in range(4))
            quarters = transpose_quarters(
                [
                    jnp.where(top, a, pltpu.roll(c, 4, 0)),
                    jnp.where(top, b, pltpu.roll(d, 4, 0)),
                    jnp.where(top, pltpu.roll(a, 4, 0), c),
                    jnp.where(top, pltpu.roll(b, 4, 0), d),
                ]
            )
            for q in range(4):
                for group in range(2):
                    dest = group * 16 + 4 * block + q
                    o_ref[pl.ds(dest * 16 + k * 8, 8), :] = quarters[q]


def matrix_kernel(
    partner_ref, kind_ref, table_ref, cos_ref, sin_ref, o_ref, token_ref, both_ref, picked_ref
):
    @pl.when(pl.program_id(0) == 0)
    def _():
        low_half = lax.broadcasted_iota(jnp.int32, (KINDS, LANES), 1) < PF
        high, low = (v.astype(f32) for v in split(table_ref[...]))
        both_ref[:, :LANES] = jnp.where(low_half, high, swap_halves(low)).astype(bf16)
        both_ref[:, LANES:] = jnp.where(low_half, swap_halves(high), low).astype(bf16)
        token_ref[...] = jnp.zeros((8, LANES), f32)

    lane_kind = lax.broadcasted_iota(jnp.int32, (SLOTS, KINDS), 1)
    row = lax.broadcasted_iota(jnp.int32, (SOURCES, SLOTS), 0)
    row_source = jnp.where(row < LANES, 2 * row, 2 * row - SOURCES + 1)
    pick_kind = []
    for p in range(8):
        kind = kind_ref[0, :, p : p + 1] % KINDS
        pick_kind.append(jnp.where(lane_kind == kind, 1.0, 0.0).astype(bf16))
    picked = jnp.dot(
        jnp.concatenate(pick_kind, 0), both_ref[...], preferred_element_type=f32
    )
    for p in range(8):
        mine = picked[p * SLOTS : (p + 1) * SLOTS]
        upper = kind_ref[0, :, p : p + 1] >= KINDS
        chosen = jnp.where(upper, mine[:, LANES:], mine[:, :LANES])
        picked_ref[pl.ds(p * SLOTS, SLOTS), :] = chosen.astype(bf16)
    quarter = lax.broadcasted_iota(jnp.int32, (LANES, LANES), 1) // 32
    for p in range(8):
        pick_source = jnp.where(row_source == partner_ref[pl.ds(p, 1), :], 1.0, 0.0).astype(bf16)
        rows = picked_ref[pl.ds(p * SLOTS, SLOTS), :]
        sums = jnp.dot(pick_source, rows, preferred_element_type=f32)
        sums = sums + swap_halves(sums)
        a, b = sums[:LANES], sums[LANES:]
        outer = jnp.where(quarter == 0, a, b)
        inner = jnp.where(quarter == 0, b, a)
        o_ref[p] = jnp.where((quarter == 0) | (quarter == 3), outer, pltpu.roll(inner, 32, 1))


def fold_rows(parts):
    row = lax.broadcasted_iota(jnp.int32, (8, LANES), 0)
    shift = 1
    while len(parts) > 1:
        first = (row & shift) == 0
        parts = [
            jnp.where(first, a, b) + pltpu.roll(jnp.where(first, b, a), shift, 0)
            for a, b in zip(parts[0::2], parts[1::2])
        ]
        shift *= 2
    return parts[0]


def translate_kernel(s_ref, m_far, o_ref, wide_ref, m_ref, arrived):
    low_half = lane_quarter() < 2
    row = lax.broadcasted_iota(jnp.int32, (8, LANES), 0)
    top = row < 4

    def fetch(g):
        eight = pl.ds(g * 8, 8)
        return pltpu.make_async_copy(m_far.at[eight], m_ref.at[eight], arrived.at[g])

    for g in range(TARGETS // 8):
        fetch(g).start()

    def spread(b, carry):
        plain = [s_ref[pl.ds(b * 32 + e, 8, stride=4), :] for e in range(4)]
        both = [v + swap_halves(v) for v in plain]
        for e in range(4):
            wide_ref[b, e] = plain[e]
        for h in range(2):
            wide_ref[b, 4 + h] = jnp.where(low_half, both[h], both[h + 2])
        return carry

    lax.fori_loop(0, 16, spread, 0, unroll=4)

    def add_pair(v):
        return v + pltpu.roll(v, 96, 1)

    def four_targets(g):
        sums = [[jnp.zeros((8, LANES), f32) for _ in range(6)] for _ in range(4)]
        for b in range(16):
            source = [wide_ref[b, k] for k in range(6)]
            for p in range(4):
                m = m_ref[g * 4 + p, pl.ds(b * 8, 8), :]
                t = m + swap_halves(m)
                for k in range(6):
                    sums[p][k] = sums[p][k] + source[k] * (m if k < 4 else t)
        plain = [fold_rows(sums[0][:4] + sums[1][:4]), fold_rows(sums[2][:4] + sums[3][:4])]
        mixed = fold_rows(sums[0][4:] + sums[2][4:] + sums[1][4:] + sums[3][4:])
        turned = swap_halves(mixed)
        first = (row & 2) == 0
        third = [
            jnp.where(first, mixed, pltpu.roll(turned, 2, 0)),
            jnp.where(first, pltpu.roll(mixed, 6, 0), turned),
        ]
        whole = []
        for k in range(2):
            other = swap_halves(plain[k])
            real = add_pair(plain[k] - other)
            imag = add_pair(third[k] - (plain[k] + other))
            whole.append(jnp.where(top, real, pltpu.roll(imag, 4, 0)))
            whole.append(jnp.where(top, pltpu.roll(real, 4, 0), imag))
        out = whole[0]
        for k in range(1, 4):
            out = jnp.where(lane_quarter() == k, pltpu.roll(whole[k], 32 * k, 1), out)
        o_ref[g // 2, g % 2] = out

    def step(q, carry):
        fetch(2 * q).wait()
        fetch(2 * q + 1).wait()
        for k in range(4):
            four_targets(4 * q + k)
        return carry

    lax.fori_loop(0, TARGETS // 16, step, 0)


def scatter_kernel(inv_ref, x_ref, w_ref, cos_ref, sin_ref, o_ref, plain_ref, child_ref):
    for block in range(4):
        for k in range(2):
            quarters = transpose_quarters([x_ref[4 * block + q, k] for q in range(4)])
            for i in range(4):
                plain_ref[4 * k + i, :, pl.ds(block * LANES, LANES)] = quarters[i]
    sign = channel_sign()

    def step(p, carry):
        plain = plain_ref[p]
        turned = -sign * pltpu.roll(plain, 4, 0)
        for o in range(8):
            child_ref[inv_ref[p * 8 + o]] = (
                plain * cos_ref[pl.ds(o, 1), :] + turned * sin_ref[pl.ds(o, 1), :]
            )
        return carry

    lax.fori_loop(0, 8, step, 0, unroll=4)
    for j in range(2):
        high, low = split(child_ref[:, :, pl.ds(j * 256, 256)].reshape(512, 256))
        part = jnp.dot(high, w_ref[...], preferred_element_type=f32)
        part = part[:, :LANES] + part[:, LANES:]
        part = part + jnp.dot(low, w_ref[:, :LANES], preferred_element_type=f32)
        o_ref[:, :, :, pl.ds(j * LANES, LANES)] = part.reshape(16, 4, 8, LANES)


def phase_tables(dir_index):
    theta_here = TP // 16
    theta_index = dir_index * theta_here + jnp.arange(theta_here, dtype=jnp.int32)
    polar = (theta_index.astype(f32) + 0.5) * (jnp.pi / TP)
    azimuth = jnp.arange(PP, dtype=f32) * (2.0 * jnp.pi / PP)
    along_x = (jnp.sin(polar)[:, None] * jnp.cos(azimuth)[None, :]).reshape(1, 512)
    along_y = (jnp.sin(polar)[:, None] * jnp.sin(azimuth)[None, :]).reshape(1, 512)
    along_z = (jnp.cos(polar)[:, None] + 0.0 * azimuth[None, :]).reshape(1, 512)
    octant = jnp.arange(8, dtype=jnp.int32)[:, None]
    sign_x = (2 * (octant % 2) - 1).astype(f32)
    sign_y = (2 * (octant // 2 % 2) - 1).astype(f32)
    sign_z = (2 * (octant // 4) - 1).astype(f32)
    angle = wave_shift * (sign_x * along_x + sign_y * along_y + sign_z * along_z)
    return jnp.cos(angle), jnp.sin(angle)


vmem = pl.BlockSpec(memory_space=pltpu.VMEM)
smem = pl.BlockSpec(memory_space=pltpu.SMEM)
hbm = pl.BlockSpec(memory_space=pltpu.HBM)


def shape(*dims):
    return jax.ShapeDtypeStruct(dims, f32)


def near(*dims):
    return pltpu.VMEM(dims, f32)


def grant(mib):
    return pltpu.CompilerParams(vmem_limit_bytes=mib << 20)


def far(x):
    return pltpu.with_memory_space_constraint(x, pltpu.HBM)


def hold(x):
    return pltpu.with_memory_space_constraint(x, pltpu.VMEM)


def body(outgoing, fine_slot, translator, list_partner, list_kind, list_count):
    box_index = lax.axis_index("box")
    dir_index = lax.axis_index("dir")
    chunk = box_index % 16
    group = box_index // 16

    theta = theta_matrix()
    up = jnp.asarray(parity_table(theta))
    down = jnp.asarray(parity_table(theta.T * (TF / TP)))
    phi = phi_matrix()
    high, low = split_constant(np.kron(np.eye(2), phi.T))
    phi_up = jnp.asarray(np.concatenate([high, high, low], 0))
    high, low = split_constant(np.kron(np.eye(2), phi) * (PF / PP))
    phi_down = jnp.asarray(np.concatenate([high, low], 1))

    sent = pl.pallas_call(
        theta_up_kernel,
        out_shape=pltpu.HBM((16, 4, 8, 256), f32),
        in_specs=[hbm, hbm],
        out_specs=hbm,
        scratch_shapes=[
            pltpu.VMEM((4, 8, TF * PF), f32),
            pltpu.VMEM((16, 32, LANES), f32),
            pltpu.VMEM((16, 4, 8, 256), f32),
            pltpu.VMEM((4, 8, 2, 8, LANES), f32),
            pltpu.SemaphoreType.DMA((4,)),
            pltpu.SemaphoreType.DMA((8,)),
            pltpu.SemaphoreType.DMA((16,)),
        ],
        compiler_params=grant(8),
    )(far(outgoing), far(up))
    spread = lax.all_to_all(sent, "dir", split_axis=0, concat_axis=0, tiled=True)

    rows = lax.dynamic_slice_in_dim(list_partner, group * TARGETS, TARGETS, 0)
    kinds = lax.dynamic_slice_in_dim(list_kind, group * TARGETS, TARGETS, 0)
    count = lax.dynamic_slice_in_dim(list_count, group * TARGETS, TARGETS, 0)
    length = rows.shape[1]
    live = jnp.arange(length, dtype=jnp.int32)[None, :] < count[:, None]
    pad = ((0, 0), (0, SLOTS - length))
    rows = jnp.pad(jnp.where(live, rows, -1), pad, constant_values=-1)
    kinds = jnp.pad(kinds, pad, constant_values=-1)
    kinds = kinds.reshape(TARGETS // 8, 8, SLOTS).transpose(0, 2, 1)
    table = lax.dynamic_slice_in_dim(translator, chunk * CHUNK, CHUNK, 2)
    table = table.reshape(table.shape[0], 2 * CHUNK)
    table = jnp.pad(table, ((0, 2 * KINDS - table.shape[0]), (0, 0)))
    table = jnp.concatenate([table[:KINDS], table[KINDS:]], 1)
    cos_table, sin_table = phase_tables(dir_index)
    place = jnp.arange(64, dtype=jnp.int32)
    found = fine_slot[None, :] % 64 == place[:, None]
    inverse = jnp.sum(jnp.where(found, place[None, :], 0), 1)
    matrix, token = pl.pallas_call(
        matrix_kernel,
        grid=(TARGETS // 8,),
        in_specs=[
            pl.BlockSpec((8, SLOTS), lambda i: (i, 0)),
            pl.BlockSpec((1, SLOTS, 8), lambda i: (i, 0, 0)),
            pl.BlockSpec((KINDS, LANES), lambda i: (0, 0)),
            vmem,
            vmem,
        ],
        out_specs=[pl.BlockSpec((8, LANES, LANES), lambda i: (i, 0, 0)), vmem],
        out_shape=[pltpu.HBM((TARGETS, LANES, LANES), f32), near(8, LANES)],
        scratch_shapes=[pltpu.VMEM((KINDS, 256), bf16), pltpu.VMEM((8 * SLOTS, LANES), bf16)],
        compiler_params=grant(16),
    )(rows, kinds, table, hold(cos_table), hold(sin_table))

    packed = pl.pallas_call(
        gather_kernel,
        out_shape=near(32 * 16, LANES),
        in_specs=[smem, vmem, vmem, vmem, vmem, vmem],
        out_specs=vmem,
        scratch_shapes=[
            pltpu.VMEM((64, 8, 512), f32),
            pltpu.VMEM((8, 8, 512), f32),
        ],
        compiler_params=grant(16),
    )(inverse, hold(spread), hold(phi_up), hold(cos_table), hold(sin_table), hold(token))
    everyone = lax.all_to_all(packed, "box", split_axis=0, concat_axis=0, tiled=True)
    incoming = pl.pallas_call(
        translate_kernel,
        in_specs=[vmem, hbm],
        out_specs=vmem,
        out_shape=near(16, 2, 8, LANES),
        scratch_shapes=[
            pltpu.VMEM((16, 6, 8, LANES), f32),
            pltpu.VMEM((TARGETS, LANES, LANES), f32),
            pltpu.SemaphoreType.DMA((TARGETS // 8,)),
        ],
        compiler_params=grant(16),
    )(hold(everyone), far(matrix))
    groups = [[16 * g + k for k in range(16)] for g in range(2)]
    fields = lax.all_to_all(
        incoming, "box", split_axis=0, concat_axis=0, axis_index_groups=groups, tiled=True
    )
    lowered = pl.pallas_call(
        scatter_kernel,
        out_shape=near(16, 4, 8, 256),
        in_specs=[smem, vmem, vmem, vmem, vmem],
        out_specs=vmem,
        scratch_shapes=[
            pltpu.VMEM((8, 8, 512), f32),
            pltpu.VMEM((64, 8, 512), f32),
        ],
        compiler_params=grant(16),
    )(inverse, hold(fields), hold(phi_down), hold(cos_table), hold(sin_table))
    back = lax.all_to_all(lowered, "dir", split_axis=0, concat_axis=0, tiled=True)
    return pl.pallas_call(
        theta_down_kernel,
        out_shape=shape(4, 8, TF * PF),
        in_specs=[vmem, vmem],
        out_specs=hbm,
        scratch_shapes=[
            pltpu.VMEM((4, 8, TF * PF), f32),
            pltpu.VMEM((4, 16, 2, 8, LANES), f32),
            pltpu.SemaphoreType.DMA((16,)),
        ],
        compiler_params=grant(8),
    )(hold(back), hold(down))


def solution(mesh):
    placed = (P(("box", "dir"), None, None), P("box"), P(None, None, "dir"), P(), P(), P())
    return jax.shard_map(
        body, mesh=mesh, in_specs=placed, out_specs=P(("box", "dir"), None, None), check_vma=False
    )
```

```python
import numpy as np

import jax
import jax.numpy as jnp
from jax import lax
from jax.experimental import pallas as pl
from jax.experimental.pallas import tpu as pltpu
from jax.sharding import PartitionSpec as P

TF = 32
PF = 64
TP = 64
PP = 128
LANES = 128
SLOTS = 192
KINDS = 256
TARGETS = 128
SOURCES = 256
CHUNK = 32

wave_shift = 5.0
f32 = jnp.float32
bf16 = jnp.bfloat16


def theta_matrix():
    a = (np.arange(TP) + 0.5) * np.pi / TP
    b = (np.arange(TF) + 0.5) * np.pi / TF
    m = np.arange(1, TF)
    series = np.cos(a[:, None, None] * m) * np.cos(b[None, :, None] * m)
    return (1.0 + 2.0 * series.sum(2)) / TF


def phi_matrix():
    e = 2 * np.pi * (np.arange(PP)[:, None] / PP - np.arange(PF)[None, :] / PF)
    k = np.arange(1, PF // 2)
    series = np.cos(e[:, :, None] * k).sum(2)
    return (1.0 + 2.0 * series + np.cos(e * (PF // 2))) / PF


def pair_table(matrix):
    n_out, n_in = matrix.shape
    m = matrix.reshape(n_out // 2, 2, n_in // 2, 2).transpose(0, 2, 1, 3)
    same = np.stack([m[:, :, 0, 0], m[:, :, 1, 1]], -1)
    cross = np.stack([m[:, :, 1, 0], m[:, :, 0, 1]], -1)
    table = np.repeat(np.stack([same, cross], 2), PF, axis=3)
    return table.reshape(n_out // 2, n_in, LANES).astype(np.float32)


def split(x):
    high = x.astype(bf16)
    return high, (x - high.astype(f32)).astype(bf16)


def split_constant(x):
    high = np.asarray(x, np.float32).astype(jnp.bfloat16)
    low = (np.asarray(x, np.float32) - high.astype(np.float32)).astype(jnp.bfloat16)
    return high, low


def swap_halves(x):
    return pltpu.roll(x, PF, x.ndim - 1)


def parity_table(matrix):
    n_out, n_in = matrix.shape
    top = matrix[: n_out // 2]
    near, far = top[:, : n_in // 2], top[:, ::-1][:, : n_in // 2]
    return np.concatenate([pair_table((near + far) / 2), pair_table((near - far) / 2)], 1)


def lane_quarter():
    return lax.broadcasted_iota(jnp.int32, (8, LANES), 1) // 32


def transpose_quarters(x):
    low_half = lane_quarter() < 2
    even = lane_quarter() % 2 == 0
    half = [
        (jnp.where(low_half, a, swap_halves(b)), jnp.where(low_half, swap_halves(a), b))
        for a, b in ((x[0], x[2]), (x[1], x[3]))
    ]
    out = []
    for k in range(2):
        a, b = half[0][k], half[1][k]
        out.append(jnp.where(even, a, pltpu.roll(b, 32, 1)))
        out.append(jnp.where(even, pltpu.roll(a, 96, 1), b))
    return out


def theta_step(parity_ref, c_ref, j, count):
    zero = jnp.zeros((8, LANES), f32)
    sums = [[[zero] * 4 for _ in range(4)] for _ in range(2)]
    for i in range(count):
        for odd in range(2):
            base = odd * 2 * count + 2 * i
            scales = [
                [c_ref[j + part, pl.ds(base + k, 1), :] for k in range(2)] for part in range(2)
            ]
            for f in range(4):
                v = parity_ref[f, i, odd]
                for part in range(2):
                    for k in range(2):
                        old = sums[part][2 * odd + k][f]
                        sums[part][2 * odd + k][f] = old + scales[part][k] * v
    out = []
    for part in range(2):
        for f in range(4):
            es, ex, os, ox = (sums[part][k][f] for k in range(4))
            out.append(((es + os) + swap_halves(ex + ox), swap_halves(es - os) + (ex - ox)))
    return out[:4], out[4:]


def theta_up_kernel(x_far, c_far, o_far, x_ref, c_ref, o_ref, parity_ref, x_in, c_in, o_out):
    def get_x(f):
        return pltpu.make_async_copy(x_far.at[f], x_ref.at[f], x_in.at[f])

    def get_c(z):
        two = pl.ds(2 * z, 2)
        return pltpu.make_async_copy(c_far.at[two], c_ref.at[two], c_in.at[z])

    def put(z):
        return pltpu.make_async_copy(o_ref.at[z], o_far.at[z], o_out.at[z])

    for f in range(4):
        get_x(f).start()
    for z in range(8):
        get_c(z).start()
    for f in range(4):
        get_x(f).wait()
        for i in range(8):
            v = x_ref[f, :, pl.ds(i * LANES, LANES)]
            w = swap_halves(x_ref[f, :, pl.ds((15 - i) * LANES, LANES)])
            parity_ref[f, i, 0] = v + w
            parity_ref[f, i, 1] = v - w

    def step(z, carry):
        get_c(z).wait()
        both = theta_step(parity_ref, c_ref, 2 * z, 8)
        for part, out in enumerate(both):
            for f in range(4):
                o_ref[z, f, :, pl.ds(part * LANES, LANES)] = out[f][0]
                o_ref[15 - z, f, :, pl.ds((1 - part) * LANES, LANES)] = out[f][1]
        put(z).start()
        put(15 - z).start()
        return carry

    lax.fori_loop(0, 8, step, 0)
    for z in range(16):
        put(z).wait()


def theta_down_kernel(y_ref, c_ref, o_far, o_ref, parity_ref, o_out):
    def put(j):
        block = pl.ds(pl.multiple_of(j * LANES, LANES), LANES)
        return pltpu.make_async_copy(o_ref.at[:, :, block], o_far.at[:, :, block], o_out.at[j])

    for f in range(4):
        for i in range(16):
            v = y_ref[i // 2, f, :, pl.ds(i % 2 * LANES, LANES)]
            w = swap_halves(y_ref[15 - i // 2, f, :, pl.ds((1 - i % 2) * LANES, LANES)])
            parity_ref[f, i, 0] = v + w
            parity_ref[f, i, 1] = v - w

    def step(q, carry):
        both = theta_step(parity_ref, c_ref, 2 * q, 16)
        for part, out in enumerate(both):
            j = 2 * q + part
            for f in range(4):
                o_ref[f, :, pl.ds(pl.multiple_of(j * LANES, LANES), LANES)] = out[f][0]
                o_ref[f, :, pl.ds(pl.multiple_of((15 - j) * LANES, LANES), LANES)] = out[f][1]
            put(j).start()
            put(15 - j).start()
        return carry

    for q in range(4):
        step(q, 0)
    for j in range(16):
        put(j).wait()


def channel_sign():
    row = lax.broadcasted_iota(jnp.int32, (8, 4 * LANES), 0)
    return jnp.where(row < 4, 1.0, -1.0).astype(f32)


def gather_kernel(inv_ref, x_ref, w_ref, cos_ref, sin_ref, after_ref, o_ref, raised_ref, parent_ref):
    for j in range(2):
        high, low = split(x_ref[:, :, :, pl.ds(j * LANES, LANES)].reshape(512, LANES))
        both = jnp.concatenate([high, low], 1)
        part = jnp.dot(both, w_ref[:256], preferred_element_type=f32)
        part = part + jnp.dot(high, w_ref[256:], preferred_element_type=f32)
        raised_ref[:, :, pl.ds(j * 256, 256)] = part.reshape(64, 8, 256)
    sign = channel_sign()

    def step(p, carry):
        plain = jnp.zeros((8, 512), f32)
        turned = jnp.zeros((8, 512), f32)
        for o in range(8):
            v = raised_ref[inv_ref[p * 8 + o]]
            plain = plain + v * cos_ref[pl.ds(o, 1), :]
            turned = turned + v * sin_ref[pl.ds(o, 1), :]
        parent_ref[p] = plain + sign * pltpu.roll(turned, 4, 0)
        return carry

    lax.fori_loop(0, 8, step, 0, unroll=4)
    top = lax.broadcasted_iota(jnp.int32, (8, LANES), 0) < 4
    for k in range(2):
        for block in range(4):
            lanes = pl.ds(block * LANES, LANES)
            a, b, c, d = (parent_ref[4 * k + i, :, lanes] for i in range(4))
            quarters = transpose_quarters(
                [
                    jnp.where(top, a, pltpu.roll(c, 4, 0)),
                    jnp.where(top, b, pltpu.roll(d, 4, 0)),
                    jnp.where(top, pltpu.roll(a, 4, 0), c),
                    jnp.where(top, pltpu.roll(b, 4, 0), d),
                ]
            )
            for q in range(4):
                for group in range(2):
                    dest = group * 16 + 4 * block + q
                    o_ref[pl.ds(dest * 16 + k * 8, 8), :] = quarters[q]


def matrix_kernel(
    partner_ref,
    kind_ref,
    place_ref,
    whole_far,
    cos_ref,
    sin_ref,
    o_ref,
    token_ref,
    both_ref,
    picked_ref,
    whole_ref,
    table_ref,
    arrived,
):
    @pl.when(pl.program_id(0) == 0)
    def _():
        chunk = place_ref[64]
        lanes = pl.ds(pl.multiple_of(chunk // 4 * LANES, LANES), LANES)
        copy = pltpu.make_async_copy(whole_far.at[:, :, lanes], whole_ref, arrived)
        copy.start()
        table_ref[...] = jnp.zeros((2 * KINDS, LANES), f32)
        copy.wait()
        count = whole_ref.shape[0]
        turn = chunk % 4 * 32
        real = pltpu.roll(whole_ref[:, 0, :], (LANES - turn) % LANES, 1)
        imag = pltpu.roll(whole_ref[:, 1, :], (LANES + 32 - turn) % LANES, 1)
        lane = lax.broadcasted_iota(jnp.int32, (count, LANES), 1)
        table_ref[pl.ds(0, count), :] = jnp.where(lane < 32, real, imag)
        low_half = lax.broadcasted_iota(jnp.int32, (KINDS, LANES), 1) < PF
        table = jnp.where(low_half, table_ref[:KINDS], swap_halves(table_ref[KINDS:]))
        high, low = (v.astype(f32) for v in split(table))
        both_ref[:, :LANES] = jnp.where(low_half, high, swap_halves(low)).astype(bf16)
        both_ref[:, LANES:] = jnp.where(low_half, swap_halves(high), low).astype(bf16)
        token_ref[...] = jnp.zeros((8, LANES), f32)

    lane_kind = lax.broadcasted_iota(jnp.int32, (SLOTS, KINDS), 1)
    row = lax.broadcasted_iota(jnp.int32, (SOURCES, SLOTS), 0)
    row_source = jnp.where(row < LANES, 2 * row, 2 * row - SOURCES + 1)
    pick_kind = []
    for p in range(8):
        kind = kind_ref[0, :, p : p + 1] % KINDS
        pick_kind.append(jnp.where(lane_kind == kind, 1.0, 0.0).astype(bf16))
    picked = jnp.dot(
        jnp.concatenate(pick_kind, 0), both_ref[...], preferred_element_type=f32
    )
    for p in range(8):
        mine = picked[p * SLOTS : (p + 1) * SLOTS]
        upper = kind_ref[0, :, p : p + 1] >= KINDS
        chosen = jnp.where(upper, mine[:, LANES:], mine[:, :LANES])
        picked_ref[pl.ds(p * SLOTS, SLOTS), :] = chosen.astype(bf16)
    quarter = lax.broadcasted_iota(jnp.int32, (LANES, LANES), 1) // 32
    for p in range(8):
        pick_source = jnp.where(row_source == partner_ref[pl.ds(p, 1), :], 1.0, 0.0).astype(bf16)
        rows = picked_ref[pl.ds(p * SLOTS, SLOTS), :]
        sums = jnp.dot(pick_source, rows, preferred_element_type=f32)
        sums = sums + swap_halves(sums)
        a, b = sums[:LANES], sums[LANES:]
        outer = jnp.where(quarter == 0, a, b)
        inner = jnp.where(quarter == 0, b, a)
        o_ref[p] = jnp.where((quarter == 0) | (quarter == 3), outer, pltpu.roll(inner, 32, 1))


def fold_rows(parts):
    row = lax.broadcasted_iota(jnp.int32, (8, LANES), 0)
    shift = 1
    while len(parts) > 1:
        first = (row & shift) == 0
        parts = [
            jnp.where(first, a, b) + pltpu.roll(jnp.where(first, b, a), shift, 0)
            for a, b in zip(parts[0::2], parts[1::2])
        ]
        shift *= 2
    return parts[0]


def translate_kernel(s_ref, m_far, o_ref, wide_ref, m_ref, arrived):
    low_half = lane_quarter() < 2
    row = lax.broadcasted_iota(jnp.int32, (8, LANES), 0)
    top = row < 4

    def fetch(g):
        eight = pl.ds(g * 8, 8)
        return pltpu.make_async_copy(m_far.at[eight], m_ref.at[eight], arrived.at[g])

    for g in range(TARGETS // 8):
        fetch(g).start()

    def spread(b, carry):
        plain = [s_ref[pl.ds(b * 32 + e, 8, stride=4), :] for e in range(4)]
        both = [v + swap_halves(v) for v in plain]
        for e in range(4):
            wide_ref[b, e] = plain[e]
        for h in range(2):
            wide_ref[b, 4 + h] = jnp.where(low_half, both[h], both[h + 2])
        return carry

    lax.fori_loop(0, 16, spread, 0, unroll=4)

    def add_pair(v):
        return v + pltpu.roll(v, 96, 1)

    def four_targets(g):
        sums = [[jnp.zeros((8, LANES), f32) for _ in range(6)] for _ in range(4)]
        for b in range(16):
            source = [wide_ref[b, k] for k in range(6)]
            for p in range(4):
                m = m_ref[g * 4 + p, pl.ds(b * 8, 8), :]
                t = m + swap_halves(m)
                for k in range(6):
                    sums[p][k] = sums[p][k] + source[k] * (m if k < 4 else t)
        plain = [fold_rows(sums[0][:4] + sums[1][:4]), fold_rows(sums[2][:4] + sums[3][:4])]
        mixed = fold_rows(sums[0][4:] + sums[2][4:] + sums[1][4:] + sums[3][4:])
        turned = swap_halves(mixed)
        first = (row & 2) == 0
        third = [
            jnp.where(first, mixed, pltpu.roll(turned, 2, 0)),
            jnp.where(first, pltpu.roll(mixed, 6, 0), turned),
        ]
        whole = []
        for k in range(2):
            other = swap_halves(plain[k])
            real = add_pair(plain[k] - other)
            imag = add_pair(third[k] - (plain[k] + other))
            whole.append(jnp.where(top, real, pltpu.roll(imag, 4, 0)))
            whole.append(jnp.where(top, pltpu.roll(real, 4, 0), imag))
        out = whole[0]
        for k in range(1, 4):
            out = jnp.where(lane_quarter() == k, pltpu.roll(whole[k], 32 * k, 1), out)
        o_ref[g // 2, g % 2] = out

    def step(q, carry):
        fetch(2 * q).wait()
        fetch(2 * q + 1).wait()
        for k in range(4):
            four_targets(4 * q + k)
        return carry

    lax.fori_loop(0, TARGETS // 16, step, 0)


def scatter_kernel(inv_ref, x_ref, w_ref, cos_ref, sin_ref, o_ref, plain_ref, child_ref):
    for block in range(4):
        for k in range(2):
            quarters = transpose_quarters([x_ref[4 * block + q, k] for q in range(4)])
            for i in range(4):
                plain_ref[4 * k + i, :, pl.ds(block * LANES, LANES)] = quarters[i]
    sign = channel_sign()

    def step(p, carry):
        plain = plain_ref[p]
        turned = -sign * pltpu.roll(plain, 4, 0)
        for o in range(8):
            child_ref[inv_ref[p * 8 + o]] = (
                plain * cos_ref[pl.ds(o, 1), :] + turned * sin_ref[pl.ds(o, 1), :]
            )
        return carry

    lax.fori_loop(0, 8, step, 0, unroll=4)
    for j in range(2):
        high, low = split(child_ref[:, :, pl.ds(j * 256, 256)].reshape(512, 256))
        part = jnp.dot(high, w_ref[...], preferred_element_type=f32)
        part = part[:, :LANES] + part[:, LANES:]
        part = part + jnp.dot(low, w_ref[:, :LANES], preferred_element_type=f32)
        o_ref[:, :, :, pl.ds(j * LANES, LANES)] = part.reshape(16, 4, 8, LANES)


def phase_tables(dir_index):
    theta_here = TP // 16
    theta_index = dir_index * theta_here + jnp.arange(theta_here, dtype=jnp.int32)
    polar = (theta_index.astype(f32) + 0.5) * (jnp.pi / TP)
    azimuth = jnp.arange(PP, dtype=f32) * (2.0 * jnp.pi / PP)
    along_x = (jnp.sin(polar)[:, None] * jnp.cos(azimuth)[None, :]).reshape(1, 512)
    along_y = (jnp.sin(polar)[:, None] * jnp.sin(azimuth)[None, :]).reshape(1, 512)
    along_z = (jnp.cos(polar)[:, None] + 0.0 * azimuth[None, :]).reshape(1, 512)
    octant = jnp.arange(8, dtype=jnp.int32)[:, None]
    sign_x = (2 * (octant % 2) - 1).astype(f32)
    sign_y = (2 * (octant // 2 % 2) - 1).astype(f32)
    sign_z = (2 * (octant // 4) - 1).astype(f32)
    angle = wave_shift * (sign_x * along_x + sign_y * along_y + sign_z * along_z)
    return jnp.cos(angle), jnp.sin(angle)


vmem = pl.BlockSpec(memory_space=pltpu.VMEM)
smem = pl.BlockSpec(memory_space=pltpu.SMEM)
hbm = pl.BlockSpec(memory_space=pltpu.HBM)


def shape(*dims):
    return jax.ShapeDtypeStruct(dims, f32)


def near(*dims):
    return pltpu.VMEM(dims, f32)


def grant(mib):
    return pltpu.CompilerParams(vmem_limit_bytes=mib << 20)


def far(x):
    return pltpu.with_memory_space_constraint(x, pltpu.HBM)


def hold(x):
    return pltpu.with_memory_space_constraint(x, pltpu.VMEM)


def body(outgoing, fine_slot, translator, list_partner, list_kind, list_count):
    box_index = lax.axis_index("box")
    dir_index = lax.axis_index("dir")
    chunk = box_index % 16
    group = box_index // 16

    theta = theta_matrix()
    up = jnp.asarray(parity_table(theta))
    down = jnp.asarray(parity_table(theta.T * (TF / TP)))
    phi = phi_matrix()
    high, low = split_constant(np.kron(np.eye(2), phi.T))
    phi_up = jnp.asarray(np.concatenate([high, high, low], 0))
    high, low = split_constant(np.kron(np.eye(2), phi) * (PF / PP))
    phi_down = jnp.asarray(np.concatenate([high, low], 1))

    sent = pl.pallas_call(
        theta_up_kernel,
        out_shape=pltpu.HBM((16, 4, 8, 256), f32),
        in_specs=[hbm, hbm],
        out_specs=hbm,
        scratch_shapes=[
            pltpu.VMEM((4, 8, TF * PF), f32),
            pltpu.VMEM((16, 32, LANES), f32),
            pltpu.VMEM((16, 4, 8, 256), f32),
            pltpu.VMEM((4, 8, 2, 8, LANES), f32),
            pltpu.SemaphoreType.DMA((4,)),
            pltpu.SemaphoreType.DMA((8,)),
            pltpu.SemaphoreType.DMA((16,)),
        ],
        compiler_params=grant(8),
    )(far(outgoing), far(up))
    spread = lax.all_to_all(sent, "dir", split_axis=0, concat_axis=0, tiled=True)

    rows = lax.dynamic_slice_in_dim(list_partner, group * TARGETS, TARGETS, 0)
    kinds = lax.dynamic_slice_in_dim(list_kind, group * TARGETS, TARGETS, 0)
    count = lax.dynamic_slice_in_dim(list_count, group * TARGETS, TARGETS, 0)
    length = rows.shape[1]
    live = jnp.arange(length, dtype=jnp.int32)[None, :] < count[:, None]
    pad = ((0, 0), (0, SLOTS - length))
    rows = jnp.pad(jnp.where(live, rows, -1), pad, constant_values=-1)
    kinds = jnp.pad(kinds, pad, constant_values=-1)
    kinds = kinds.reshape(TARGETS // 8, 8, SLOTS).transpose(0, 2, 1)
    cos_table, sin_table = phase_tables(dir_index)
    place = jnp.arange(64, dtype=jnp.int32)
    found = fine_slot[None, :] % 64 == place[:, None]
    inverse = jnp.sum(jnp.where(found, place[None, :], 0), 1)
    inverse = jnp.concatenate([inverse, jnp.full((8,), chunk, jnp.int32)])
    matrix, token = pl.pallas_call(
        matrix_kernel,
        grid=(TARGETS // 8,),
        in_specs=[
            pl.BlockSpec((8, SLOTS), lambda i: (i, 0)),
            pl.BlockSpec((1, SLOTS, 8), lambda i: (i, 0, 0)),
            smem,
            hbm,
            vmem,
            vmem,
        ],
        out_specs=[pl.BlockSpec((8, LANES, LANES), lambda i: (i, 0, 0)), vmem],
        out_shape=[pltpu.HBM((TARGETS, LANES, LANES), f32), near(8, LANES)],
        scratch_shapes=[
            pltpu.VMEM((KINDS, 256), bf16),
            pltpu.VMEM((8 * SLOTS, LANES), bf16),
            pltpu.VMEM((translator.shape[0], 2, LANES), f32),
            pltpu.VMEM((2 * KINDS, LANES), f32),
            pltpu.SemaphoreType.DMA,
        ],
        compiler_params=grant(16),
    )(rows, kinds, inverse, far(translator), hold(cos_table), hold(sin_table))

    packed = pl.pallas_call(
        gather_kernel,
        out_shape=near(32 * 16, LANES),
        in_specs=[smem, vmem, vmem, vmem, vmem, vmem],
        out_specs=vmem,
        scratch_shapes=[
            pltpu.VMEM((64, 8, 512), f32),
            pltpu.VMEM((8, 8, 512), f32),
        ],
        compiler_params=grant(16),
    )(inverse, hold(spread), hold(phi_up), hold(cos_table), hold(sin_table), hold(token))
    everyone = lax.all_to_all(packed, "box", split_axis=0, concat_axis=0, tiled=True)
    incoming = pl.pallas_call(
        translate_kernel,
        in_specs=[vmem, hbm],
        out_specs=vmem,
        out_shape=near(16, 2, 8, LANES),
        scratch_shapes=[
            pltpu.VMEM((16, 6, 8, LANES), f32),
            pltpu.VMEM((TARGETS, LANES, LANES), f32),
            pltpu.SemaphoreType.DMA((TARGETS // 8,)),
        ],
        compiler_params=grant(16),
    )(hold(everyone), far(matrix))
    groups = [[16 * g + k for k in range(16)] for g in range(2)]
    fields = lax.all_to_all(
        incoming, "box", split_axis=0, concat_axis=0, axis_index_groups=groups, tiled=True
    )
    lowered = pl.pallas_call(
        scatter_kernel,
        out_shape=near(16, 4, 8, 256),
        in_specs=[smem, vmem, vmem, vmem, vmem],
        out_specs=vmem,
        scratch_shapes=[
            pltpu.VMEM((8, 8, 512), f32),
            pltpu.VMEM((64, 8, 512), f32),
        ],
        compiler_params=grant(16),
    )(inverse, hold(fields), hold(phi_down), hold(cos_table), hold(sin_table))
    back = lax.all_to_all(lowered, "dir", split_axis=0, concat_axis=0, tiled=True)
    return pl.pallas_call(
        theta_down_kernel,
        out_shape=shape(4, 8, TF * PF),
        in_specs=[vmem, vmem],
        out_specs=hbm,
        scratch_shapes=[
            pltpu.VMEM((4, 8, TF * PF), f32),
            pltpu.VMEM((4, 16, 2, 8, LANES), f32),
            pltpu.SemaphoreType.DMA((16,)),
        ],
        compiler_params=grant(8),
    )(hold(back), hold(down))


def solution(mesh):
    placed = (P(("box", "dir"), None, None), P("box"), P(None, None, "dir"), P(), P(), P())
    return jax.shard_map(
        body, mesh=mesh, in_specs=placed, out_specs=P(("box", "dir"), None, None), check_vma=False
    )
```

```python
import numpy as np

import jax
import jax.numpy as jnp
from jax import lax
from jax.experimental import pallas as pl
from jax.experimental.pallas import tpu as pltpu
from jax.sharding import PartitionSpec as P

TF = 32
PF = 64
TP = 64
PP = 128
LANES = 128
SLOTS = 192
KINDS = 256
TARGETS = 128
SOURCES = 256
CHUNK = 32

wave_shift = 5.0
f32 = jnp.float32
bf16 = jnp.bfloat16


def theta_matrix():
    a = (np.arange(TP) + 0.5) * np.pi / TP
    b = (np.arange(TF) + 0.5) * np.pi / TF
    m = np.arange(1, TF)
    series = np.cos(a[:, None, None] * m) * np.cos(b[None, :, None] * m)
    return (1.0 + 2.0 * series.sum(2)) / TF


def phi_matrix():
    e = 2 * np.pi * (np.arange(PP)[:, None] / PP - np.arange(PF)[None, :] / PF)
    k = np.arange(1, PF // 2)
    series = np.cos(e[:, :, None] * k).sum(2)
    return (1.0 + 2.0 * series + np.cos(e * (PF // 2))) / PF


def pair_table(matrix):
    n_out, n_in = matrix.shape
    m = matrix.reshape(n_out // 2, 2, n_in // 2, 2).transpose(0, 2, 1, 3)
    same = np.stack([m[:, :, 0, 0], m[:, :, 1, 1]], -1)
    cross = np.stack([m[:, :, 1, 0], m[:, :, 0, 1]], -1)
    table = np.repeat(np.stack([same, cross], 2), PF, axis=3)
    return table.reshape(n_out // 2, n_in, LANES).astype(np.float32)


def split(x):
    high = x.astype(bf16)
    return high, (x - high.astype(f32)).astype(bf16)


def split_constant(x):
    high = np.asarray(x, np.float32).astype(jnp.bfloat16)
    low = (np.asarray(x, np.float32) - high.astype(np.float32)).astype(jnp.bfloat16)
    return high, low


def swap_halves(x):
    return pltpu.roll(x, PF, x.ndim - 1)


def parity_table(matrix):
    n_out, n_in = matrix.shape
    top = matrix[: n_out // 2]
    near, far = top[:, : n_in // 2], top[:, ::-1][:, : n_in // 2]
    return np.concatenate([pair_table((near + far) / 2), pair_table((near - far) / 2)], 1)


def lane_quarter():
    return lax.broadcasted_iota(jnp.int32, (8, LANES), 1) // 32


def transpose_quarters(x):
    low_half = lane_quarter() < 2
    even = lane_quarter() % 2 == 0
    half = [
        (jnp.where(low_half, a, swap_halves(b)), jnp.where(low_half, swap_halves(a), b))
        for a, b in ((x[0], x[2]), (x[1], x[3]))
    ]
    out = []
    for k in range(2):
        a, b = half[0][k], half[1][k]
        out.append(jnp.where(even, a, pltpu.roll(b, 32, 1)))
        out.append(jnp.where(even, pltpu.roll(a, 96, 1), b))
    return out


def theta_step(parity_ref, c_ref, j, count):
    zero = jnp.zeros((8, LANES), f32)
    sums = [[[zero] * 4 for _ in range(4)] for _ in range(2)]
    for i in range(count):
        for odd in range(2):
            base = odd * 2 * count + 2 * i
            scales = [
                [c_ref[j + part, pl.ds(base + k, 1), :] for k in range(2)] for part in range(2)
            ]
            for f in range(4):
                v = parity_ref[f, i, odd]
                for part in range(2):
                    for k in range(2):
                        old = sums[part][2 * odd + k][f]
                        sums[part][2 * odd + k][f] = old + scales[part][k] * v
    out = []
    for part in range(2):
        for f in range(4):
            es, ex, os, ox = (sums[part][k][f] for k in range(4))
            out.append(((es + os) + swap_halves(ex + ox), swap_halves(es - os) + (ex - ox)))
    return out[:4], out[4:]


def theta_up_kernel(x_far, c_far, o_far, x_ref, c_ref, o_ref, parity_ref, x_in, c_in, o_out):
    def get_x(f):
        return pltpu.make_async_copy(x_far.at[f], x_ref.at[f], x_in.at[f])

    def get_c(z):
        two = pl.ds(2 * z, 2)
        return pltpu.make_async_copy(c_far.at[two], c_ref.at[two], c_in.at[z])

    def put(z):
        return pltpu.make_async_copy(o_ref.at[z], o_far.at[z], o_out.at[z])

    for f in range(4):
        get_x(f).start()
    for z in range(8):
        get_c(z).start()
    for f in range(4):
        get_x(f).wait()
        for i in range(8):
            v = x_ref[f, :, pl.ds(i * LANES, LANES)]
            w = swap_halves(x_ref[f, :, pl.ds((15 - i) * LANES, LANES)])
            parity_ref[f, i, 0] = v + w
            parity_ref[f, i, 1] = v - w

    def step(z, carry):
        get_c(z).wait()
        both = theta_step(parity_ref, c_ref, 2 * z, 8)
        for part, out in enumerate(both):
            for f in range(4):
                o_ref[z, f, :, pl.ds(part * LANES, LANES)] = out[f][0]
                o_ref[15 - z, f, :, pl.ds((1 - part) * LANES, LANES)] = out[f][1]
        put(z).start()
        put(15 - z).start()
        return carry

    lax.fori_loop(0, 8, step, 0)
    for z in range(16):
        put(z).wait()


def theta_down_kernel(y_ref, c_ref, o_far, o_ref, parity_ref, o_out):
    def put(j):
        block = pl.ds(pl.multiple_of(j * LANES, LANES), LANES)
        return pltpu.make_async_copy(o_ref.at[:, :, block], o_far.at[:, :, block], o_out.at[j])

    for f in range(4):
        for i in range(16):
            v = y_ref[i // 2, f, :, pl.ds(i % 2 * LANES, LANES)]
            w = swap_halves(y_ref[15 - i // 2, f, :, pl.ds((1 - i % 2) * LANES, LANES)])
            parity_ref[f, i, 0] = v + w
            parity_ref[f, i, 1] = v - w

    def step(q, carry):
        both = theta_step(parity_ref, c_ref, 2 * q, 16)
        for part, out in enumerate(both):
            j = 2 * q + part
            for f in range(4):
                o_ref[f, :, pl.ds(pl.multiple_of(j * LANES, LANES), LANES)] = out[f][0]
                o_ref[f, :, pl.ds(pl.multiple_of((15 - j) * LANES, LANES), LANES)] = out[f][1]
            put(j).start()
            put(15 - j).start()
        return carry

    for q in range(4):
        step(q, 0)
    for j in range(16):
        put(j).wait()


def channel_sign():
    row = lax.broadcasted_iota(jnp.int32, (8, 4 * LANES), 0)
    return jnp.where(row < 4, 1.0, -1.0).astype(f32)


def gather_kernel(inv_ref, x_ref, w_ref, cos_ref, sin_ref, after_ref, o_ref, raised_ref, parent_ref):
    for j in range(2):
        high, low = split(x_ref[:, :, :, pl.ds(j * LANES, LANES)].reshape(512, LANES))
        both = jnp.concatenate([high, low], 1)
        part = jnp.dot(both, w_ref[:256], preferred_element_type=f32)
        part = part + jnp.dot(high, w_ref[256:], preferred_element_type=f32)
        raised_ref[:, :, pl.ds(j * 256, 256)] = part.reshape(64, 8, 256)
    sign = channel_sign()

    def step(p, carry):
        plain = jnp.zeros((8, 512), f32)
        turned = jnp.zeros((8, 512), f32)
        for o in range(8):
            v = raised_ref[inv_ref[p * 8 + o]]
            plain = plain + v * cos_ref[pl.ds(o, 1), :]
            turned = turned + v * sin_ref[pl.ds(o, 1), :]
        parent_ref[p] = plain + sign * pltpu.roll(turned, 4, 0)
        return carry

    lax.fori_loop(0, 8, step, 0, unroll=4)
    top = lax.broadcasted_iota(jnp.int32, (8, LANES), 0) < 4
    for k in range(2):
        for block in range(4):
            lanes = pl.ds(block * LANES, LANES)
            a, b, c, d = (parent_ref[4 * k + i, :, lanes] for i in range(4))
            quarters = transpose_quarters(
                [
                    jnp.where(top, a, pltpu.roll(c, 4, 0)),
                    jnp.where(top, b, pltpu.roll(d, 4, 0)),
                    jnp.where(top, pltpu.roll(a, 4, 0), c),
                    jnp.where(top, pltpu.roll(b, 4, 0), d),
                ]
            )
            for q in range(4):
                for group in range(2):
                    dest = group * 16 + 4 * block + q
                    o_ref[pl.ds(dest * 16 + k * 8, 8), :] = quarters[q]


def matrix_kernel(
    partner_ref,
    kind_ref,
    place_ref,
    whole_far,
    cos_ref,
    sin_ref,
    o_ref,
    token_ref,
    both_ref,
    picked_ref,
    whole_ref,
    table_ref,
    arrived,
):
    @pl.when(pl.program_id(0) == 0)
    def _():
        chunk = place_ref[64]
        lanes = pl.ds(pl.multiple_of(chunk // 4 * LANES, LANES), LANES)
        copy = pltpu.make_async_copy(whole_far.at[:, :, lanes], whole_ref, arrived)
        copy.start()
        table_ref[...] = jnp.zeros((2 * KINDS, LANES), f32)
        copy.wait()
        count = whole_ref.shape[0]
        turn = chunk % 4 * 32
        real = pltpu.roll(whole_ref[:, 0, :], (LANES - turn) % LANES, 1)
        imag = pltpu.roll(whole_ref[:, 1, :], (LANES + 32 - turn) % LANES, 1)
        lane = lax.broadcasted_iota(jnp.int32, (count, LANES), 1)
        table_ref[pl.ds(0, count), :] = jnp.where(lane < 32, real, imag)
        low_half = lax.broadcasted_iota(jnp.int32, (KINDS, LANES), 1) < PF
        table = jnp.where(low_half, table_ref[:KINDS], swap_halves(table_ref[KINDS:]))
        high, low = (v.astype(f32) for v in split(table))
        both_ref[:, :LANES] = jnp.where(low_half, high, swap_halves(low)).astype(bf16)
        both_ref[:, LANES:] = jnp.where(low_half, swap_halves(high), low).astype(bf16)
        token_ref[...] = jnp.zeros((8, LANES), f32)

    lane_kind = lax.broadcasted_iota(jnp.int32, (SLOTS, KINDS), 1)
    row = lax.broadcasted_iota(jnp.int32, (SOURCES, SLOTS), 0)
    row_source = jnp.where(row < LANES, 2 * row, 2 * row - SOURCES + 1)
    pick_kind = []
    for p in range(8):
        kind = kind_ref[0, :, p : p + 1] % KINDS
        pick_kind.append(jnp.where(lane_kind == kind, 1.0, 0.0).astype(bf16))
    picked = jnp.dot(
        jnp.concatenate(pick_kind, 0), both_ref[...], preferred_element_type=f32
    )
    for p in range(8):
        mine = picked[p * SLOTS : (p + 1) * SLOTS]
        upper = kind_ref[0, :, p : p + 1] >= KINDS
        chosen = jnp.where(upper, mine[:, LANES:], mine[:, :LANES])
        picked_ref[pl.ds(p * SLOTS, SLOTS), :] = chosen.astype(bf16)
    quarter = lax.broadcasted_iota(jnp.int32, (LANES, LANES), 1) // 32
    for p in range(8):
        pick_source = jnp.where(row_source == partner_ref[pl.ds(p, 1), :], 1.0, 0.0).astype(bf16)
        rows = picked_ref[pl.ds(p * SLOTS, SLOTS), :]
        sums = jnp.dot(pick_source, rows, preferred_element_type=f32)
        sums = sums + swap_halves(sums)
        a, b = sums[:LANES], sums[LANES:]
        outer = jnp.where(quarter == 0, a, b)
        inner = jnp.where(quarter == 0, b, a)
        o_ref[p] = jnp.where((quarter == 0) | (quarter == 3), outer, pltpu.roll(inner, 32, 1))


def fold_rows(parts):
    row = lax.broadcasted_iota(jnp.int32, (8, LANES), 0)
    shift = 1
    while len(parts) > 1:
        first = (row & shift) == 0
        parts = [
            jnp.where(first, a, b) + pltpu.roll(jnp.where(first, b, a), shift, 0)
            for a, b in zip(parts[0::2], parts[1::2])
        ]
        shift *= 2
    return parts[0]


def translate_kernel(s_ref, m_far, o_ref, wide_ref, m_ref, sums_ref, arrived):
    low_half = lane_quarter() < 2
    row = lax.broadcasted_iota(jnp.int32, (8, LANES), 0)
    top = row < 4

    def fetch(g):
        eight = pl.ds(g * 8, 8)
        return pltpu.make_async_copy(m_far.at[eight], m_ref.at[eight], arrived.at[g])

    for g in range(TARGETS // 8):
        fetch(g).start()

    def spread(b, carry):
        plain = [s_ref[pl.ds(b * 32 + e, 8, stride=4), :] for e in range(4)]
        both = [v + swap_halves(v) for v in plain]
        for e in range(4):
            wide_ref[b, e] = plain[e]
        for h in range(2):
            wide_ref[b, 4 + h] = jnp.where(low_half, both[h], both[h + 2])
        return carry

    lax.fori_loop(0, 16, spread, 0, unroll=4)

    def add_pair(v):
        return v + pltpu.roll(v, 96, 1)

    def four_targets(g):
        sums = [[jnp.zeros((8, LANES), f32) for _ in range(6)] for _ in range(4)]
        for b in range(16):
            source = [wide_ref[b, k] for k in range(6)]
            for p in range(4):
                m = m_ref[g * 4 + p, pl.ds(b * 8, 8), :]
                t = m + swap_halves(m)
                for k in range(6):
                    sums[p][k] = sums[p][k] + source[k] * (m if k < 4 else t)
        for p in range(4):
            for k in range(6):
                sums_ref[g, p, k] = sums[p][k]

    def finish(g):
        sums = [[sums_ref[g, p, k] for k in range(6)] for p in range(4)]
        plain = [fold_rows(sums[0][:4] + sums[1][:4]), fold_rows(sums[2][:4] + sums[3][:4])]
        mixed = fold_rows(sums[0][4:] + sums[2][4:] + sums[1][4:] + sums[3][4:])
        turned = swap_halves(mixed)
        first = (row & 2) == 0
        third = [
            jnp.where(first, mixed, pltpu.roll(turned, 2, 0)),
            jnp.where(first, pltpu.roll(mixed, 6, 0), turned),
        ]
        whole = []
        for k in range(2):
            other = swap_halves(plain[k])
            real = add_pair(plain[k] - other)
            imag = add_pair(third[k] - (plain[k] + other))
            whole.append(jnp.where(top, real, pltpu.roll(imag, 4, 0)))
            whole.append(jnp.where(top, pltpu.roll(real, 4, 0), imag))
        out = whole[0]
        for k in range(1, 4):
            out = jnp.where(lane_quarter() == k, pltpu.roll(whole[k], 32 * k, 1), out)
        o_ref[g // 2, g % 2] = out

    def step(q, carry):
        fetch(q).wait()
        for k in range(2):
            four_targets(2 * q + k)
        return carry

    lax.fori_loop(0, TARGETS // 8, step, 0)

    def last(q, carry):
        for k in range(16):
            finish(16 * q + k)
        return carry

    lax.fori_loop(0, TARGETS // 64, last, 0)


def scatter_kernel(inv_ref, x_ref, w_ref, cos_ref, sin_ref, o_ref, plain_ref, child_ref):
    for block in range(4):
        for k in range(2):
            quarters = transpose_quarters([x_ref[4 * block + q, k] for q in range(4)])
            for i in range(4):
                plain_ref[4 * k + i, :, pl.ds(block * LANES, LANES)] = quarters[i]
    sign = channel_sign()

    def step(p, carry):
        plain = plain_ref[p]
        turned = -sign * pltpu.roll(plain, 4, 0)
        for o in range(8):
            child_ref[inv_ref[p * 8 + o]] = (
                plain * cos_ref[pl.ds(o, 1), :] + turned * sin_ref[pl.ds(o, 1), :]
            )
        return carry

    lax.fori_loop(0, 8, step, 0, unroll=4)
    for j in range(2):
        high, low = split(child_ref[:, :, pl.ds(j * 256, 256)].reshape(512, 256))
        part = jnp.dot(high, w_ref[...], preferred_element_type=f32)
        part = part[:, :LANES] + part[:, LANES:]
        part = part + jnp.dot(low, w_ref[:, :LANES], preferred_element_type=f32)
        o_ref[:, :, :, pl.ds(j * LANES, LANES)] = part.reshape(16, 4, 8, LANES)


def phase_tables(dir_index):
    theta_here = TP // 16
    theta_index = dir_index * theta_here + jnp.arange(theta_here, dtype=jnp.int32)
    polar = (theta_index.astype(f32) + 0.5) * (jnp.pi / TP)
    azimuth = jnp.arange(PP, dtype=f32) * (2.0 * jnp.pi / PP)
    along_x = (jnp.sin(polar)[:, None] * jnp.cos(azimuth)[None, :]).reshape(1, 512)
    along_y = (jnp.sin(polar)[:, None] * jnp.sin(azimuth)[None, :]).reshape(1, 512)
    along_z = (jnp.cos(polar)[:, None] + 0.0 * azimuth[None, :]).reshape(1, 512)
    octant = jnp.arange(8, dtype=jnp.int32)[:, None]
    sign_x = (2 * (octant % 2) - 1).astype(f32)
    sign_y = (2 * (octant // 2 % 2) - 1).astype(f32)
    sign_z = (2 * (octant // 4) - 1).astype(f32)
    angle = wave_shift * (sign_x * along_x + sign_y * along_y + sign_z * along_z)
    return jnp.cos(angle), jnp.sin(angle)


vmem = pl.BlockSpec(memory_space=pltpu.VMEM)
smem = pl.BlockSpec(memory_space=pltpu.SMEM)
hbm = pl.BlockSpec(memory_space=pltpu.HBM)


def shape(*dims):
    return jax.ShapeDtypeStruct(dims, f32)


def near(*dims):
    return pltpu.VMEM(dims, f32)


def grant(mib):
    return pltpu.CompilerParams(vmem_limit_bytes=mib << 20)


def far(x):
    return pltpu.with_memory_space_constraint(x, pltpu.HBM)


def hold(x):
    return pltpu.with_memory_space_constraint(x, pltpu.VMEM)


def body(outgoing, fine_slot, translator, list_partner, list_kind, list_count):
    box_index = lax.axis_index("box")
    dir_index = lax.axis_index("dir")
    chunk = box_index % 16
    group = box_index // 16

    theta = theta_matrix()
    up = jnp.asarray(parity_table(theta))
    down = jnp.asarray(parity_table(theta.T * (TF / TP)))
    phi = phi_matrix()
    high, low = split_constant(np.kron(np.eye(2), phi.T))
    phi_up = jnp.asarray(np.concatenate([high, high, low], 0))
    high, low = split_constant(np.kron(np.eye(2), phi) * (PF / PP))
    phi_down = jnp.asarray(np.concatenate([high, low], 1))

    sent = pl.pallas_call(
        theta_up_kernel,
        out_shape=pltpu.HBM((16, 4, 8, 256), f32),
        in_specs=[hbm, hbm],
        out_specs=hbm,
        scratch_shapes=[
            pltpu.VMEM((4, 8, TF * PF), f32),
            pltpu.VMEM((16, 32, LANES), f32),
            pltpu.VMEM((16, 4, 8, 256), f32),
            pltpu.VMEM((4, 8, 2, 8, LANES), f32),
            pltpu.SemaphoreType.DMA((4,)),
            pltpu.SemaphoreType.DMA((8,)),
            pltpu.SemaphoreType.DMA((16,)),
        ],
        compiler_params=grant(8),
    )(far(outgoing), far(up))
    spread = lax.all_to_all(sent, "dir", split_axis=0, concat_axis=0, tiled=True)

    rows = lax.dynamic_slice_in_dim(list_partner, group * TARGETS, TARGETS, 0)
    kinds = lax.dynamic_slice_in_dim(list_kind, group * TARGETS, TARGETS, 0)
    count = lax.dynamic_slice_in_dim(list_count, group * TARGETS, TARGETS, 0)
    length = rows.shape[1]
    live = jnp.arange(length, dtype=jnp.int32)[None, :] < count[:, None]
    pad = ((0, 0), (0, SLOTS - length))
    rows = jnp.pad(jnp.where(live, rows, -1), pad, constant_values=-1)
    kinds = jnp.pad(kinds, pad, constant_values=-1)
    kinds = kinds.reshape(TARGETS // 8, 8, SLOTS).transpose(0, 2, 1)
    cos_table, sin_table = phase_tables(dir_index)
    place = jnp.arange(64, dtype=jnp.int32)
    found = fine_slot[None, :] % 64 == place[:, None]
    inverse = jnp.sum(jnp.where(found, place[None, :], 0), 1)
    inverse = jnp.concatenate([inverse, jnp.full((8,), chunk, jnp.int32)])
    matrix, token = pl.pallas_call(
        matrix_kernel,
        grid=(TARGETS // 8,),
        in_specs=[
            pl.BlockSpec((8, SLOTS), lambda i: (i, 0)),
            pl.BlockSpec((1, SLOTS, 8), lambda i: (i, 0, 0)),
            smem,
            hbm,
            vmem,
            vmem,
        ],
        out_specs=[pl.BlockSpec((8, LANES, LANES), lambda i: (i, 0, 0)), vmem],
        out_shape=[pltpu.HBM((TARGETS, LANES, LANES), f32), near(8, LANES)],
        scratch_shapes=[
            pltpu.VMEM((KINDS, 256), bf16),
            pltpu.VMEM((8 * SLOTS, LANES), bf16),
            pltpu.VMEM((translator.shape[0], 2, LANES), f32),
            pltpu.VMEM((2 * KINDS, LANES), f32),
            pltpu.SemaphoreType.DMA,
        ],
        compiler_params=grant(16),
    )(rows, kinds, inverse, far(translator), hold(cos_table), hold(sin_table))

    packed = pl.pallas_call(
        gather_kernel,
        out_shape=near(32 * 16, LANES),
        in_specs=[smem, vmem, vmem, vmem, vmem, vmem],
        out_specs=vmem,
        scratch_shapes=[
            pltpu.VMEM((64, 8, 512), f32),
            pltpu.VMEM((8, 8, 512), f32),
        ],
        compiler_params=grant(16),
    )(inverse, hold(spread), hold(phi_up), hold(cos_table), hold(sin_table), hold(token))
    everyone = lax.all_to_all(packed, "box", split_axis=0, concat_axis=0, tiled=True)
    incoming = pl.pallas_call(
        translate_kernel,
        in_specs=[vmem, hbm],
        out_specs=vmem,
        out_shape=near(16, 2, 8, LANES),
        scratch_shapes=[
            pltpu.VMEM((16, 6, 8, LANES), f32),
            pltpu.VMEM((TARGETS, LANES, LANES), f32),
            pltpu.VMEM((TARGETS // 4, 4, 6, 8, LANES), f32),
            pltpu.SemaphoreType.DMA((TARGETS // 8,)),
        ],
        compiler_params=grant(16),
    )(hold(everyone), far(matrix))
    groups = [[16 * g + k for k in range(16)] for g in range(2)]
    fields = lax.all_to_all(
        incoming, "box", split_axis=0, concat_axis=0, axis_index_groups=groups, tiled=True
    )
    lowered = pl.pallas_call(
        scatter_kernel,
        out_shape=near(16, 4, 8, 256),
        in_specs=[smem, vmem, vmem, vmem, vmem],
        out_specs=vmem,
        scratch_shapes=[
            pltpu.VMEM((8, 8, 512), f32),
            pltpu.VMEM((64, 8, 512), f32),
        ],
        compiler_params=grant(16),
    )(inverse, hold(fields), hold(phi_down), hold(cos_table), hold(sin_table))
    back = lax.all_to_all(lowered, "dir", split_axis=0, concat_axis=0, tiled=True)
    return pl.pallas_call(
        theta_down_kernel,
        out_shape=shape(4, 8, TF * PF),
        in_specs=[vmem, vmem],
        out_specs=hbm,
        scratch_shapes=[
            pltpu.VMEM((4, 8, TF * PF), f32),
            pltpu.VMEM((4, 16, 2, 8, LANES), f32),
            pltpu.SemaphoreType.DMA((16,)),
        ],
        compiler_params=grant(8),
    )(hold(back), hold(down))


def solution(mesh):
    placed = (P(("box", "dir"), None, None), P("box"), P(None, None, "dir"), P(), P(), P())
    return jax.shard_map(
        body, mesh=mesh, in_specs=placed, out_specs=P(("box", "dir"), None, None), check_vma=False
    )
```

```python
import numpy as np

import jax
import jax.numpy as jnp
from jax import lax
from jax.experimental import pallas as pl
from jax.experimental.pallas import tpu as pltpu
from jax.sharding import PartitionSpec as P

TF = 32
PF = 64
TP = 64
PP = 128
LANES = 128
SLOTS = 192
KINDS = 256
TABLE_ROWS = 320
TARGETS = 128
SOURCES = 256
CHUNK = 32

wave_shift = 5.0
f32 = jnp.float32
bf16 = jnp.bfloat16


def theta_matrix():
    a = (np.arange(TP) + 0.5) * np.pi / TP
    b = (np.arange(TF) + 0.5) * np.pi / TF
    m = np.arange(1, TF)
    series = np.cos(a[:, None, None] * m) * np.cos(b[None, :, None] * m)
    return (1.0 + 2.0 * series.sum(2)) / TF


def phi_matrix():
    e = 2 * np.pi * (np.arange(PP)[:, None] / PP - np.arange(PF)[None, :] / PF)
    k = np.arange(1, PF // 2)
    series = np.cos(e[:, :, None] * k).sum(2)
    return (1.0 + 2.0 * series + np.cos(e * (PF // 2))) / PF


def pair_table(matrix):
    n_out, n_in = matrix.shape
    m = matrix.reshape(n_out // 2, 2, n_in // 2, 2).transpose(0, 2, 1, 3)
    same = np.stack([m[:, :, 0, 0], m[:, :, 1, 1]], -1)
    cross = np.stack([m[:, :, 1, 0], m[:, :, 0, 1]], -1)
    table = np.repeat(np.stack([same, cross], 2), PF, axis=3)
    return table.reshape(n_out // 2, n_in, LANES).astype(np.float32)


def split(x):
    high = x.astype(bf16)
    return high, (x - high.astype(f32)).astype(bf16)


def split_constant(x):
    high = np.asarray(x, np.float32).astype(jnp.bfloat16)
    low = (np.asarray(x, np.float32) - high.astype(np.float32)).astype(jnp.bfloat16)
    return high, low


def swap_halves(x):
    return pltpu.roll(x, PF, x.ndim - 1)


def parity_table(matrix):
    n_out, n_in = matrix.shape
    top = matrix[: n_out // 2]
    near, far = top[:, : n_in // 2], top[:, ::-1][:, : n_in // 2]
    return np.concatenate([pair_table((near + far) / 2), pair_table((near - far) / 2)], 1)


def lane_quarter():
    return lax.broadcasted_iota(jnp.int32, (8, LANES), 1) // 32


def transpose_quarters(x):
    low_half = lane_quarter() < 2
    even = lane_quarter() % 2 == 0
    half = [
        (jnp.where(low_half, a, swap_halves(b)), jnp.where(low_half, swap_halves(a), b))
        for a, b in ((x[0], x[2]), (x[1], x[3]))
    ]
    out = []
    for k in range(2):
        a, b = half[0][k], half[1][k]
        out.append(jnp.where(even, a, pltpu.roll(b, 32, 1)))
        out.append(jnp.where(even, pltpu.roll(a, 96, 1), b))
    return out


def theta_step(parity_ref, c_ref, j, count):
    zero = jnp.zeros((8, LANES), f32)
    sums = [[[zero] * 4 for _ in range(4)] for _ in range(2)]
    for i in range(count):
        for odd in range(2):
            base = odd * 2 * count + 2 * i
            scales = [
                [c_ref[j + part, pl.ds(base + k, 1), :] for k in range(2)] for part in range(2)
            ]
            for f in range(4):
                v = parity_ref[f, i, odd]
                for part in range(2):
                    for k in range(2):
                        old = sums[part][2 * odd + k][f]
                        sums[part][2 * odd + k][f] = old + scales[part][k] * v
    out = []
    for part in range(2):
        for f in range(4):
            es, ex, os, ox = (sums[part][k][f] for k in range(4))
            out.append(((es + os) + swap_halves(ex + ox), swap_halves(es - os) + (ex - ox)))
    return out[:4], out[4:]


def theta_up_kernel(x_far, c_far, o_far, x_ref, c_ref, o_ref, parity_ref, x_in, c_in, o_out):
    def get_x(f):
        return pltpu.make_async_copy(x_far.at[f], x_ref.at[f], x_in.at[f])

    def get_c(z):
        two = pl.ds(2 * z, 2)
        return pltpu.make_async_copy(c_far.at[two], c_ref.at[two], c_in.at[z])

    def put(z):
        return pltpu.make_async_copy(o_ref.at[z], o_far.at[z], o_out.at[z])

    for f in range(4):
        get_x(f).start()
    for z in range(8):
        get_c(z).start()
    for f in range(4):
        get_x(f).wait()
        for i in range(8):
            v = x_ref[f, :, pl.ds(i * LANES, LANES)]
            w = swap_halves(x_ref[f, :, pl.ds((15 - i) * LANES, LANES)])
            parity_ref[f, i, 0] = v + w
            parity_ref[f, i, 1] = v - w

    def step(z, carry):
        get_c(z).wait()
        both = theta_step(parity_ref, c_ref, 2 * z, 8)
        for part, out in enumerate(both):
            for f in range(4):
                o_ref[z, f, :, pl.ds(part * LANES, LANES)] = out[f][0]
                o_ref[15 - z, f, :, pl.ds((1 - part) * LANES, LANES)] = out[f][1]
        put(z).start()
        put(15 - z).start()
        return carry

    lax.fori_loop(0, 8, step, 0)
    for z in range(16):
        put(z).wait()


def theta_down_kernel(y_ref, c_ref, o_far, o_ref, parity_ref, o_out):
    def put(j):
        block = pl.ds(pl.multiple_of(j * LANES, LANES), LANES)
        return pltpu.make_async_copy(o_ref.at[:, :, block], o_far.at[:, :, block], o_out.at[j])

    for f in range(4):
        for i in range(16):
            v = y_ref[i // 2, f, :, pl.ds(i % 2 * LANES, LANES)]
            w = swap_halves(y_ref[15 - i // 2, f, :, pl.ds((1 - i % 2) * LANES, LANES)])
            parity_ref[f, i, 0] = v + w
            parity_ref[f, i, 1] = v - w

    def step(q, carry):
        both = theta_step(parity_ref, c_ref, 2 * q, 16)
        for part, out in enumerate(both):
            j = 2 * q + part
            for f in range(4):
                o_ref[f, :, pl.ds(pl.multiple_of(j * LANES, LANES), LANES)] = out[f][0]
                o_ref[f, :, pl.ds(pl.multiple_of((15 - j) * LANES, LANES), LANES)] = out[f][1]
            put(j).start()
            put(15 - j).start()
        return carry

    for q in range(4):
        step(q, 0)
    for j in range(16):
        put(j).wait()


def channel_sign():
    row = lax.broadcasted_iota(jnp.int32, (8, 4 * LANES), 0)
    return jnp.where(row < 4, 1.0, -1.0).astype(f32)


def gather_kernel(inv_ref, x_ref, w_ref, cos_ref, sin_ref, after_ref, o_ref, raised_ref, parent_ref):
    for j in range(2):
        high, low = split(x_ref[:, :, :, pl.ds(j * LANES, LANES)].reshape(512, LANES))
        both = jnp.concatenate([high, low], 1)
        part = jnp.dot(both, w_ref[:256], preferred_element_type=f32)
        part = part + jnp.dot(high, w_ref[256:], preferred_element_type=f32)
        raised_ref[:, :, pl.ds(j * 256, 256)] = part.reshape(64, 8, 256)
    sign = channel_sign()

    def step(p, carry):
        plain = jnp.zeros((8, 512), f32)
        turned = jnp.zeros((8, 512), f32)
        for o in range(8):
            v = raised_ref[inv_ref[p * 8 + o]]
            plain = plain + v * cos_ref[pl.ds(o, 1), :]
            turned = turned + v * sin_ref[pl.ds(o, 1), :]
        parent_ref[p] = plain + sign * pltpu.roll(turned, 4, 0)
        return carry

    lax.fori_loop(0, 8, step, 0, unroll=True)
    top = lax.broadcasted_iota(jnp.int32, (8, LANES), 0) < 4
    for k in range(2):
        for block in range(4):
            lanes = pl.ds(block * LANES, LANES)
            a, b, c, d = (parent_ref[4 * k + i, :, lanes] for i in range(4))
            quarters = transpose_quarters(
                [
                    jnp.where(top, a, pltpu.roll(c, 4, 0)),
                    jnp.where(top, b, pltpu.roll(d, 4, 0)),
                    jnp.where(top, pltpu.roll(a, 4, 0), c),
                    jnp.where(top, pltpu.roll(b, 4, 0), d),
                ]
            )
            for q in range(4):
                for group in range(2):
                    dest = group * 16 + 4 * block + q
                    o_ref[pl.ds(dest * 16 + k * 8, 8), :] = quarters[q]


def matrix_kernel(
    partner_ref,
    kind_ref,
    place_ref,
    whole_far,
    cos_ref,
    sin_ref,
    o_ref,
    token_ref,
    both_ref,
    picked_ref,
    whole_ref,
    table_ref,
    arrived,
):
    @pl.when(pl.program_id(0) == 0)
    def _():
        chunk = place_ref[64]
        lanes = pl.ds(pl.multiple_of(chunk // 4 * LANES, LANES), LANES)
        kinds = whole_far.shape[0]
        count = whole_ref.shape[0]
        copy = pltpu.make_async_copy(
            whole_far.at[:, :, lanes], whole_ref.at[pl.ds(0, kinds)], arrived
        )
        copy.start()
        whole_ref[pl.ds(kinds, count - kinds)] = jnp.zeros((count - kinds, 2, LANES), f32)
        table_ref[...] = jnp.zeros((2 * KINDS, LANES), f32)
        copy.wait()
        turn = chunk % 4 * 32
        real = pltpu.roll(whole_ref[:, 0, :], (LANES - turn) % LANES, 1)
        imag = pltpu.roll(whole_ref[:, 1, :], (LANES + 32 - turn) % LANES, 1)
        lane = lax.broadcasted_iota(jnp.int32, (count, LANES), 1)
        table_ref[pl.ds(0, count), :] = jnp.where(lane < 32, real, imag)
        low_half = lax.broadcasted_iota(jnp.int32, (KINDS, LANES), 1) < PF
        table = jnp.where(low_half, table_ref[:KINDS], swap_halves(table_ref[KINDS:]))
        high, low = (v.astype(f32) for v in split(table))
        both_ref[:, :LANES] = jnp.where(low_half, high, swap_halves(low)).astype(bf16)
        both_ref[:, LANES:] = jnp.where(low_half, swap_halves(high), low).astype(bf16)
        token_ref[...] = jnp.zeros((8, LANES), f32)

    lane_kind = lax.broadcasted_iota(jnp.int32, (SLOTS, KINDS), 1)
    row = lax.broadcasted_iota(jnp.int32, (SOURCES, SLOTS), 0)
    row_source = jnp.where(row < LANES, 2 * row, 2 * row - SOURCES + 1)
    pick_kind = []
    for p in range(8):
        kind = kind_ref[0, :, p : p + 1] % KINDS
        pick_kind.append(jnp.where(lane_kind == kind, 1.0, 0.0).astype(bf16))
    picked = jnp.dot(
        jnp.concatenate(pick_kind, 0), both_ref[...], preferred_element_type=f32
    )
    for p in range(8):
        mine = picked[p * SLOTS : (p + 1) * SLOTS]
        upper = kind_ref[0, :, p : p + 1] >= KINDS
        chosen = jnp.where(upper, mine[:, LANES:], mine[:, :LANES])
        picked_ref[pl.ds(p * SLOTS, SLOTS), :] = chosen.astype(bf16)
    quarter = lax.broadcasted_iota(jnp.int32, (LANES, LANES), 1) // 32
    for p in range(8):
        pick_source = jnp.where(row_source == partner_ref[pl.ds(p, 1), :], 1.0, 0.0).astype(bf16)
        rows = picked_ref[pl.ds(p * SLOTS, SLOTS), :]
        sums = jnp.dot(pick_source, rows, preferred_element_type=f32)
        sums = sums + swap_halves(sums)
        a, b = sums[:LANES], sums[LANES:]
        outer = jnp.where(quarter == 0, a, b)
        inner = jnp.where(quarter == 0, b, a)
        o_ref[p] = jnp.where((quarter == 0) | (quarter == 3), outer, pltpu.roll(inner, 32, 1))


def fold_rows(parts):
    row = lax.broadcasted_iota(jnp.int32, (8, LANES), 0)
    shift = 1
    while len(parts) > 1:
        first = (row & shift) == 0
        parts = [
            jnp.where(first, a, b) + pltpu.roll(jnp.where(first, b, a), shift, 0)
            for a, b in zip(parts[0::2], parts[1::2])
        ]
        shift *= 2
    return parts[0]


def translate_kernel(s_ref, m_far, o_ref, wide_ref, m_ref, sums_ref, arrived):
    low_half = lane_quarter() < 2
    row = lax.broadcasted_iota(jnp.int32, (8, LANES), 0)
    top = row < 4

    def fetch(g):
        eight = pl.ds(g * 8, 8)
        return pltpu.make_async_copy(m_far.at[eight], m_ref.at[eight], arrived.at[g])

    for g in range(TARGETS // 8):
        fetch(g).start()

    def spread(b, carry):
        plain = [s_ref[pl.ds(b * 32 + e, 8, stride=4), :] for e in range(4)]
        both = [v + swap_halves(v) for v in plain]
        for e in range(4):
            wide_ref[b, e] = plain[e]
        for h in range(2):
            wide_ref[b, 4 + h] = jnp.where(low_half, both[h], both[h + 2])
        return carry

    lax.fori_loop(0, 16, spread, 0, unroll=4)

    def add_pair(v):
        return v + pltpu.roll(v, 96, 1)

    def four_targets(g):
        sums = [[jnp.zeros((8, LANES), f32) for _ in range(6)] for _ in range(4)]
        for b in range(16):
            source = [wide_ref[b, k] for k in range(6)]
            for p in range(4):
                m = m_ref[g * 4 + p, pl.ds(b * 8, 8), :]
                t = m + swap_halves(m)
                for k in range(6):
                    sums[p][k] = sums[p][k] + source[k] * (m if k < 4 else t)
        for p in range(4):
            for k in range(6):
                sums_ref[g, p, k] = sums[p][k]

    def finish(g):
        sums = [[sums_ref[g, p, k] for k in range(6)] for p in range(4)]
        plain = [fold_rows(sums[0][:4] + sums[1][:4]), fold_rows(sums[2][:4] + sums[3][:4])]
        mixed = fold_rows(sums[0][4:] + sums[2][4:] + sums[1][4:] + sums[3][4:])
        turned = swap_halves(mixed)
        first = (row & 2) == 0
        third = [
            jnp.where(first, mixed, pltpu.roll(turned, 2, 0)),
            jnp.where(first, pltpu.roll(mixed, 6, 0), turned),
        ]
        whole = []
        for k in range(2):
            other = swap_halves(plain[k])
            real = add_pair(plain[k] - other)
            imag = add_pair(third[k] - (plain[k] + other))
            whole.append(jnp.where(top, real, pltpu.roll(imag, 4, 0)))
            whole.append(jnp.where(top, pltpu.roll(real, 4, 0), imag))
        out = whole[0]
        for k in range(1, 4):
            out = jnp.where(lane_quarter() == k, pltpu.roll(whole[k], 32 * k, 1), out)
        o_ref[g // 2, g % 2] = out

    def step(q, carry):
        fetch(q).wait()
        for k in range(2):
            four_targets(2 * q + k)
        return carry

    lax.fori_loop(0, TARGETS // 8, step, 0)

    def last(q, carry):
        for k in range(16):
            finish(16 * q + k)
        return carry

    lax.fori_loop(0, TARGETS // 64, last, 0)


def scatter_kernel(inv_ref, x_ref, w_ref, cos_ref, sin_ref, o_ref, plain_ref, child_ref):
    for block in range(4):
        for k in range(2):
            quarters = transpose_quarters([x_ref[4 * block + q, k] for q in range(4)])
            for i in range(4):
                plain_ref[4 * k + i, :, pl.ds(block * LANES, LANES)] = quarters[i]
    sign = channel_sign()

    def step(p, carry):
        plain = plain_ref[p]
        turned = -sign * pltpu.roll(plain, 4, 0)
        for o in range(8):
            child_ref[inv_ref[p * 8 + o]] = (
                plain * cos_ref[pl.ds(o, 1), :] + turned * sin_ref[pl.ds(o, 1), :]
            )
        return carry

    lax.fori_loop(0, 8, step, 0, unroll=True)
    for j in range(2):
        high, low = split(child_ref[:, :, pl.ds(j * 256, 256)].reshape(512, 256))
        part = jnp.dot(high, w_ref[...], preferred_element_type=f32)
        part = part[:, :LANES] + part[:, LANES:]
        part = part + jnp.dot(low, w_ref[:, :LANES], preferred_element_type=f32)
        o_ref[:, :, :, pl.ds(j * LANES, LANES)] = part.reshape(16, 4, 8, LANES)


def phase_tables(dir_index):
    theta_here = TP // 16
    theta_index = dir_index * theta_here + jnp.arange(theta_here, dtype=jnp.int32)
    polar = (theta_index.astype(f32) + 0.5) * (jnp.pi / TP)
    azimuth = jnp.arange(PP, dtype=f32) * (2.0 * jnp.pi / PP)
    along_x = (jnp.sin(polar)[:, None] * jnp.cos(azimuth)[None, :]).reshape(1, 512)
    along_y = (jnp.sin(polar)[:, None] * jnp.sin(azimuth)[None, :]).reshape(1, 512)
    along_z = (jnp.cos(polar)[:, None] + 0.0 * azimuth[None, :]).reshape(1, 512)
    octant = jnp.arange(8, dtype=jnp.int32)[:, None]
    sign_x = (2 * (octant % 2) - 1).astype(f32)
    sign_y = (2 * (octant // 2 % 2) - 1).astype(f32)
    sign_z = (2 * (octant // 4) - 1).astype(f32)
    angle = wave_shift * (sign_x * along_x + sign_y * along_y + sign_z * along_z)
    return jnp.cos(angle), jnp.sin(angle)


vmem = pl.BlockSpec(memory_space=pltpu.VMEM)
smem = pl.BlockSpec(memory_space=pltpu.SMEM)
hbm = pl.BlockSpec(memory_space=pltpu.HBM)


def shape(*dims):
    return jax.ShapeDtypeStruct(dims, f32)


def near(*dims):
    return pltpu.VMEM(dims, f32)


def grant(mib):
    return pltpu.CompilerParams(vmem_limit_bytes=mib << 20)


def far(x):
    return pltpu.with_memory_space_constraint(x, pltpu.HBM)


def hold(x):
    return pltpu.with_memory_space_constraint(x, pltpu.VMEM)


def body(outgoing, fine_slot, translator, list_partner, list_kind, list_count):
    box_index = lax.axis_index("box")
    dir_index = lax.axis_index("dir")
    chunk = box_index % 16
    group = box_index // 16

    theta = theta_matrix()
    up = jnp.asarray(parity_table(theta))
    down = jnp.asarray(parity_table(theta.T * (TF / TP)))
    phi = phi_matrix()
    high, low = split_constant(np.kron(np.eye(2), phi.T))
    phi_up = jnp.asarray(np.concatenate([high, high, low], 0))
    high, low = split_constant(np.kron(np.eye(2), phi) * (PF / PP))
    phi_down = jnp.asarray(np.concatenate([high, low], 1))

    sent = pl.pallas_call(
        theta_up_kernel,
        out_shape=pltpu.HBM((16, 4, 8, 256), f32),
        in_specs=[hbm, hbm],
        out_specs=hbm,
        scratch_shapes=[
            pltpu.VMEM((4, 8, TF * PF), f32),
            pltpu.VMEM((16, 32, LANES), f32),
            pltpu.VMEM((16, 4, 8, 256), f32),
            pltpu.VMEM((4, 8, 2, 8, LANES), f32),
            pltpu.SemaphoreType.DMA((4,)),
            pltpu.SemaphoreType.DMA((8,)),
            pltpu.SemaphoreType.DMA((16,)),
        ],
        compiler_params=grant(8),
    )(far(outgoing), far(up))
    spread = lax.all_to_all(sent, "dir", split_axis=0, concat_axis=0, tiled=True)

    rows = lax.dynamic_slice_in_dim(list_partner, group * TARGETS, TARGETS, 0)
    kinds = lax.dynamic_slice_in_dim(list_kind, group * TARGETS, TARGETS, 0)
    count = lax.dynamic_slice_in_dim(list_count, group * TARGETS, TARGETS, 0)
    length = rows.shape[1]
    live = jnp.arange(length, dtype=jnp.int32)[None, :] < count[:, None]
    pad = ((0, 0), (0, SLOTS - length))
    rows = jnp.pad(jnp.where(live, rows, -1), pad, constant_values=-1)
    kinds = jnp.pad(kinds, pad, constant_values=-1)
    kinds = kinds.reshape(TARGETS // 8, 8, SLOTS).transpose(0, 2, 1)
    cos_table, sin_table = phase_tables(dir_index)
    place = jnp.arange(64, dtype=jnp.int32)
    found = fine_slot[None, :] % 64 == place[:, None]
    inverse = jnp.sum(jnp.where(found, place[None, :], 0), 1)
    inverse = jnp.concatenate([inverse, jnp.full((8,), chunk, jnp.int32)])
    matrix, token = pl.pallas_call(
        matrix_kernel,
        grid=(TARGETS // 8,),
        in_specs=[
            pl.BlockSpec((8, SLOTS), lambda i: (i, 0)),
            pl.BlockSpec((1, SLOTS, 8), lambda i: (i, 0, 0)),
            smem,
            hbm,
            vmem,
            vmem,
        ],
        out_specs=[pl.BlockSpec((8, LANES, LANES), lambda i: (i, 0, 0)), vmem],
        out_shape=[pltpu.HBM((TARGETS, LANES, LANES), f32), near(8, LANES)],
        scratch_shapes=[
            pltpu.VMEM((KINDS, 256), bf16),
            pltpu.VMEM((8 * SLOTS, LANES), bf16),
            pltpu.VMEM((TABLE_ROWS, 2, LANES), f32),
            pltpu.VMEM((2 * KINDS, LANES), f32),
            pltpu.SemaphoreType.DMA,
        ],
        compiler_params=grant(16),
    )(rows, kinds, inverse, far(translator), hold(cos_table), hold(sin_table))

    packed = pl.pallas_call(
        gather_kernel,
        out_shape=near(32 * 16, LANES),
        in_specs=[smem, vmem, vmem, vmem, vmem, vmem],
        out_specs=vmem,
        scratch_shapes=[
            pltpu.VMEM((64, 8, 512), f32),
            pltpu.VMEM((8, 8, 512), f32),
        ],
        compiler_params=grant(16),
    )(inverse, hold(spread), hold(phi_up), hold(cos_table), hold(sin_table), hold(token))
    everyone = lax.all_to_all(packed, "box", split_axis=0, concat_axis=0, tiled=True)
    incoming = pl.pallas_call(
        translate_kernel,
        in_specs=[vmem, hbm],
        out_specs=vmem,
        out_shape=near(16, 2, 8, LANES),
        scratch_shapes=[
            pltpu.VMEM((16, 6, 8, LANES), f32),
            pltpu.VMEM((TARGETS, LANES, LANES), f32),
            pltpu.VMEM((TARGETS // 4, 4, 6, 8, LANES), f32),
            pltpu.SemaphoreType.DMA((TARGETS // 8,)),
        ],
        compiler_params=grant(16),
    )(hold(everyone), far(matrix))
    groups = [[16 * g + k for k in range(16)] for g in range(2)]
    fields = lax.all_to_all(
        incoming, "box", split_axis=0, concat_axis=0, axis_index_groups=groups, tiled=True
    )
    lowered = pl.pallas_call(
        scatter_kernel,
        out_shape=near(16, 4, 8, 256),
        in_specs=[smem, vmem, vmem, vmem, vmem],
        out_specs=vmem,
        scratch_shapes=[
            pltpu.VMEM((8, 8, 512), f32),
            pltpu.VMEM((64, 8, 512), f32),
        ],
        compiler_params=grant(16),
    )(inverse, hold(fields), hold(phi_down), hold(cos_table), hold(sin_table))
    back = lax.all_to_all(lowered, "dir", split_axis=0, concat_axis=0, tiled=True)
    return pl.pallas_call(
        theta_down_kernel,
        out_shape=shape(4, 8, TF * PF),
        in_specs=[vmem, vmem],
        out_specs=hbm,
        scratch_shapes=[
            pltpu.VMEM((4, 8, TF * PF), f32),
            pltpu.VMEM((4, 16, 2, 8, LANES), f32),
            pltpu.SemaphoreType.DMA((16,)),
        ],
        compiler_params=grant(8),
    )(hold(back), hold(down))


def solution(mesh):
    placed = (P(("box", "dir"), None, None), P("box"), P(None, None, "dir"), P(), P(), P())
    return jax.shard_map(
        body, mesh=mesh, in_specs=placed, out_specs=P(("box", "dir"), None, None), check_vma=False
    )
```

```python
import numpy as np

import jax
import jax.numpy as jnp
from jax import lax
from jax.experimental import pallas as pl
from jax.experimental.pallas import tpu as pltpu
from jax.sharding import PartitionSpec as P

TF = 32
PF = 64
TP = 64
PP = 128
LANES = 128
SLOTS = 192
KINDS = 256
TABLE_ROWS = 320
TARGETS = 128
SOURCES = 256
CHUNK = 32

wave_shift = 5.0
f32 = jnp.float32
bf16 = jnp.bfloat16


def theta_matrix():
    a = (np.arange(TP) + 0.5) * np.pi / TP
    b = (np.arange(TF) + 0.5) * np.pi / TF
    m = np.arange(1, TF)
    series = np.cos(a[:, None, None] * m) * np.cos(b[None, :, None] * m)
    return (1.0 + 2.0 * series.sum(2)) / TF


def phi_matrix():
    e = 2 * np.pi * (np.arange(PP)[:, None] / PP - np.arange(PF)[None, :] / PF)
    k = np.arange(1, PF // 2)
    series = np.cos(e[:, :, None] * k).sum(2)
    return (1.0 + 2.0 * series + np.cos(e * (PF // 2))) / PF


def pair_table(matrix):
    n_out, n_in = matrix.shape
    m = matrix.reshape(n_out // 2, 2, n_in // 2, 2).transpose(0, 2, 1, 3)
    same = np.stack([m[:, :, 0, 0], m[:, :, 1, 1]], -1)
    cross = np.stack([m[:, :, 1, 0], m[:, :, 0, 1]], -1)
    table = np.repeat(np.stack([same, cross], 2), PF, axis=3)
    return table.reshape(n_out // 2, n_in, LANES).astype(np.float32)


def split(x):
    high = x.astype(bf16)
    return high, (x - high.astype(f32)).astype(bf16)


def split_constant(x):
    high = np.asarray(x, np.float32).astype(jnp.bfloat16)
    low = (np.asarray(x, np.float32) - high.astype(np.float32)).astype(jnp.bfloat16)
    return high, low


def swap_halves(x):
    return pltpu.roll(x, PF, x.ndim - 1)


def parity_table(matrix):
    n_out, n_in = matrix.shape
    top = matrix[: n_out // 2]
    near, far = top[:, : n_in // 2], top[:, ::-1][:, : n_in // 2]
    return np.concatenate([pair_table((near + far) / 2), pair_table((near - far) / 2)], 1)


def lane_quarter():
    return lax.broadcasted_iota(jnp.int32, (8, LANES), 1) // 32


def transpose_quarters(x):
    low_half = lane_quarter() < 2
    even = lane_quarter() % 2 == 0
    half = [
        (jnp.where(low_half, a, swap_halves(b)), jnp.where(low_half, swap_halves(a), b))
        for a, b in ((x[0], x[2]), (x[1], x[3]))
    ]
    out = []
    for k in range(2):
        a, b = half[0][k], half[1][k]
        out.append(jnp.where(even, a, pltpu.roll(b, 32, 1)))
        out.append(jnp.where(even, pltpu.roll(a, 96, 1), b))
    return out


def theta_step(parity_ref, c_ref, j, count):
    zero = jnp.zeros((8, LANES), f32)
    sums = [[[zero] * 4 for _ in range(4)] for _ in range(2)]
    for i in range(count):
        for odd in range(2):
            base = odd * 2 * count + 2 * i
            scales = [
                [c_ref[j + part, pl.ds(base + k, 1), :] for k in range(2)] for part in range(2)
            ]
            for f in range(4):
                v = parity_ref[f, i, odd]
                for part in range(2):
                    for k in range(2):
                        old = sums[part][2 * odd + k][f]
                        sums[part][2 * odd + k][f] = old + scales[part][k] * v
    out = []
    for part in range(2):
        for f in range(4):
            es, ex, os, ox = (sums[part][k][f] for k in range(4))
            out.append(((es + os) + swap_halves(ex + ox), swap_halves(es - os) + (ex - ox)))
    return out[:4], out[4:]


def theta_up_kernel(x_far, c_far, o_far, x_ref, c_ref, o_ref, parity_ref, x_in, c_in, o_out):
    def get_x(f):
        return pltpu.make_async_copy(x_far.at[f], x_ref.at[f], x_in.at[f])

    def get_c(z):
        two = pl.ds(2 * z, 2)
        return pltpu.make_async_copy(c_far.at[two], c_ref.at[two], c_in.at[z])

    def put(z):
        return pltpu.make_async_copy(o_ref.at[z], o_far.at[z], o_out.at[z])

    for f in range(4):
        get_x(f).start()
    for z in range(8):
        get_c(z).start()
    for f in range(4):
        get_x(f).wait()
        for i in range(8):
            v = x_ref[f, :, pl.ds(i * LANES, LANES)]
            w = swap_halves(x_ref[f, :, pl.ds((15 - i) * LANES, LANES)])
            parity_ref[f, i, 0] = v + w
            parity_ref[f, i, 1] = v - w

    def step(z, carry):
        get_c(z).wait()
        both = theta_step(parity_ref, c_ref, 2 * z, 8)
        for part, out in enumerate(both):
            for f in range(4):
                o_ref[z, f, :, pl.ds(part * LANES, LANES)] = out[f][0]
                o_ref[15 - z, f, :, pl.ds((1 - part) * LANES, LANES)] = out[f][1]
        put(z).start()
        put(15 - z).start()
        return carry

    lax.fori_loop(0, 8, step, 0)
    for z in range(16):
        put(z).wait()


def theta_down_kernel(y_ref, c_ref, o_far, o_ref, parity_ref, o_out):
    def put(j):
        block = pl.ds(pl.multiple_of(j * LANES, LANES), LANES)
        return pltpu.make_async_copy(o_ref.at[:, :, block], o_far.at[:, :, block], o_out.at[j])

    for f in range(4):
        for i in range(16):
            v = y_ref[i // 2, f, :, pl.ds(i % 2 * LANES, LANES)]
            w = swap_halves(y_ref[15 - i // 2, f, :, pl.ds((1 - i % 2) * LANES, LANES)])
            parity_ref[f, i, 0] = v + w
            parity_ref[f, i, 1] = v - w

    def step(q, carry):
        both = theta_step(parity_ref, c_ref, 2 * q, 16)
        for part, out in enumerate(both):
            j = 2 * q + part
            for f in range(4):
                o_ref[f, :, pl.ds(pl.multiple_of(j * LANES, LANES), LANES)] = out[f][0]
                o_ref[f, :, pl.ds(pl.multiple_of((15 - j) * LANES, LANES), LANES)] = out[f][1]
            put(j).start()
            put(15 - j).start()
        return carry

    for q in range(4):
        step(q, 0)
    for j in range(16):
        put(j).wait()


def channel_sign():
    row = lax.broadcasted_iota(jnp.int32, (8, 4 * LANES), 0)
    return jnp.where(row < 4, 1.0, -1.0).astype(f32)


def gather_kernel(inv_ref, x_ref, w_ref, cos_ref, sin_ref, after_ref, o_ref, raised_ref, parent_ref):
    for j in range(2):
        high, low = split(x_ref[:, :, :, pl.ds(j * LANES, LANES)].reshape(512, LANES))
        both = jnp.concatenate([high, low], 1)
        part = jnp.dot(both, w_ref[:256], preferred_element_type=f32)
        part = part + jnp.dot(high, w_ref[256:], preferred_element_type=f32)
        raised_ref[:, :, pl.ds(j * 256, 256)] = part.reshape(64, 8, 256)
    sign = channel_sign()

    def step(p, carry):
        plain = jnp.zeros((8, 512), f32)
        turned = jnp.zeros((8, 512), f32)
        for o in range(8):
            v = raised_ref[inv_ref[p * 8 + o]]
            plain = plain + v * cos_ref[pl.ds(o, 1), :]
            turned = turned + v * sin_ref[pl.ds(o, 1), :]
        parent_ref[p] = plain + sign * pltpu.roll(turned, 4, 0)
        return carry

    lax.fori_loop(0, 8, step, 0, unroll=True)
    top = lax.broadcasted_iota(jnp.int32, (8, LANES), 0) < 4
    for k in range(2):
        for block in range(4):
            lanes = pl.ds(block * LANES, LANES)
            a, b, c, d = (parent_ref[4 * k + i, :, lanes] for i in range(4))
            quarters = transpose_quarters(
                [
                    jnp.where(top, a, pltpu.roll(c, 4, 0)),
                    jnp.where(top, b, pltpu.roll(d, 4, 0)),
                    jnp.where(top, pltpu.roll(a, 4, 0), c),
                    jnp.where(top, pltpu.roll(b, 4, 0), d),
                ]
            )
            for q in range(4):
                for group in range(2):
                    dest = group * 16 + 4 * block + q
                    o_ref[pl.ds(dest * 16 + k * 8, 8), :] = quarters[q]


def matrix_kernel(
    partner_ref,
    kind_ref,
    place_ref,
    whole_far,
    cos_ref,
    sin_ref,
    o_ref,
    token_ref,
    both_ref,
    picked_ref,
    whole_ref,
    table_ref,
    arrived,
):
    @pl.when(pl.program_id(0) == 0)
    def _():
        chunk = place_ref[64]
        lanes = pl.ds(pl.multiple_of(chunk // 4 * LANES, LANES), LANES)
        kinds = whole_far.shape[0]
        count = whole_ref.shape[0]
        copy = pltpu.make_async_copy(
            whole_far.at[:, :, lanes], whole_ref.at[pl.ds(0, kinds)], arrived
        )
        copy.start()
        whole_ref[pl.ds(kinds, count - kinds)] = jnp.zeros((count - kinds, 2, LANES), f32)
        table_ref[...] = jnp.zeros((2 * KINDS, LANES), f32)
        copy.wait()
        turn = chunk % 4 * 32
        real = pltpu.roll(whole_ref[:, 0, :], (LANES - turn) % LANES, 1)
        imag = pltpu.roll(whole_ref[:, 1, :], (LANES + 32 - turn) % LANES, 1)
        lane = lax.broadcasted_iota(jnp.int32, (count, LANES), 1)
        table_ref[pl.ds(0, count), :] = jnp.where(lane < 32, real, imag)
        low_half = lax.broadcasted_iota(jnp.int32, (KINDS, LANES), 1) < PF
        table = jnp.where(low_half, table_ref[:KINDS], swap_halves(table_ref[KINDS:]))
        high, low = (v.astype(f32) for v in split(table))
        both_ref[:, :LANES] = jnp.where(low_half, high, swap_halves(low)).astype(bf16)
        both_ref[:, LANES:] = jnp.where(low_half, swap_halves(high), low).astype(bf16)
        token_ref[...] = jnp.zeros((8, LANES), f32)

    lane_kind = lax.broadcasted_iota(jnp.int32, (SLOTS, KINDS), 1)
    row = lax.broadcasted_iota(jnp.int32, (SOURCES, SLOTS), 0)
    row_source = jnp.where(row < LANES, 2 * row, 2 * row - SOURCES + 1)
    pick_kind = []
    for p in range(8):
        kind = kind_ref[0, :, p : p + 1] % KINDS
        pick_kind.append(jnp.where(lane_kind == kind, 1.0, 0.0).astype(bf16))
    picked = jnp.dot(
        jnp.concatenate(pick_kind, 0), both_ref[...], preferred_element_type=f32
    )
    for p in range(8):
        mine = picked[p * SLOTS : (p + 1) * SLOTS]
        upper = kind_ref[0, :, p : p + 1] >= KINDS
        chosen = jnp.where(upper, mine[:, LANES:], mine[:, :LANES])
        picked_ref[pl.ds(p * SLOTS, SLOTS), :] = chosen.astype(bf16)
    quarter = lax.broadcasted_iota(jnp.int32, (LANES, LANES), 1) // 32
    for p in range(8):
        pick_source = jnp.where(row_source == partner_ref[pl.ds(p, 1), :], 1.0, 0.0).astype(bf16)
        rows = picked_ref[pl.ds(p * SLOTS, SLOTS), :]
        sums = jnp.dot(pick_source, rows, preferred_element_type=f32)
        sums = sums + swap_halves(sums)
        a, b = sums[:LANES], sums[LANES:]
        outer = jnp.where(quarter == 0, a, b)
        inner = jnp.where(quarter == 0, b, a)
        o_ref[p] = jnp.where((quarter == 0) | (quarter == 3), outer, pltpu.roll(inner, 32, 1))


def fold_rows(parts):
    row = lax.broadcasted_iota(jnp.int32, (8, LANES), 0)
    shift = 1
    while len(parts) > 1:
        first = (row & shift) == 0
        parts = [
            jnp.where(first, a, b) + pltpu.roll(jnp.where(first, b, a), shift, 0)
            for a, b in zip(parts[0::2], parts[1::2])
        ]
        shift *= 2
    return parts[0]


def translate_kernel(s_ref, m_far, o_ref, wide_ref, m_ref, sums_ref, arrived):
    low_half = lane_quarter() < 2
    row = lax.broadcasted_iota(jnp.int32, (8, LANES), 0)
    top = row < 4

    def fetch(g):
        eight = pl.ds(g * 8, 8)
        return pltpu.make_async_copy(m_far.at[eight], m_ref.at[eight], arrived.at[g])

    for g in range(TARGETS // 8):
        fetch(g).start()

    def spread(b, carry):
        plain = [s_ref[pl.ds(b * 32 + e, 8, stride=4), :] for e in range(4)]
        both = [v + swap_halves(v) for v in plain]
        for e in range(4):
            wide_ref[b, e] = plain[e]
        for h in range(2):
            wide_ref[b, 4 + h] = jnp.where(low_half, both[h], both[h + 2])
        return carry

    lax.fori_loop(0, 16, spread, 0, unroll=True)

    def add_pair(v):
        return v + pltpu.roll(v, 96, 1)

    def four_targets(g):
        sums = [[jnp.zeros((8, LANES), f32) for _ in range(6)] for _ in range(4)]
        for b in range(16):
            source = [wide_ref[b, k] for k in range(6)]
            for p in range(4):
                m = m_ref[g * 4 + p, pl.ds(b * 8, 8), :]
                t = m + swap_halves(m)
                for k in range(6):
                    sums[p][k] = sums[p][k] + source[k] * (m if k < 4 else t)
        for p in range(4):
            for k in range(6):
                sums_ref[g, p, k] = sums[p][k]

    def finish(g):
        sums = [[sums_ref[g, p, k] for k in range(6)] for p in range(4)]
        plain = [fold_rows(sums[0][:4] + sums[1][:4]), fold_rows(sums[2][:4] + sums[3][:4])]
        mixed = fold_rows(sums[0][4:] + sums[2][4:] + sums[1][4:] + sums[3][4:])
        turned = swap_halves(mixed)
        first = (row & 2) == 0
        third = [
            jnp.where(first, mixed, pltpu.roll(turned, 2, 0)),
            jnp.where(first, pltpu.roll(mixed, 6, 0), turned),
        ]
        whole = []
        for k in range(2):
            other = swap_halves(plain[k])
            real = add_pair(plain[k] - other)
            imag = add_pair(third[k] - (plain[k] + other))
            whole.append(jnp.where(top, real, pltpu.roll(imag, 4, 0)))
            whole.append(jnp.where(top, pltpu.roll(real, 4, 0), imag))
        out = whole[0]
        for k in range(1, 4):
            out = jnp.where(lane_quarter() == k, pltpu.roll(whole[k], 32 * k, 1), out)
        o_ref[g // 2, g % 2] = out

    def step(q, carry):
        fetch(q).wait()
        for k in range(2):
            four_targets(2 * q + k)
        return carry

    lax.fori_loop(0, TARGETS // 8, step, 0)

    def last(q, carry):
        for k in range(16):
            finish(16 * q + k)
        return carry

    lax.fori_loop(0, TARGETS // 64, last, 0)


def scatter_kernel(inv_ref, x_ref, w_ref, cos_ref, sin_ref, o_ref, plain_ref, child_ref):
    for block in range(4):
        for k in range(2):
            quarters = transpose_quarters([x_ref[4 * block + q, k] for q in range(4)])
            for i in range(4):
                plain_ref[4 * k + i, :, pl.ds(block * LANES, LANES)] = quarters[i]
    sign = channel_sign()

    def step(p, carry):
        plain = plain_ref[p]
        turned = -sign * pltpu.roll(plain, 4, 0)
        for o in range(8):
            child_ref[inv_ref[p * 8 + o]] = (
                plain * cos_ref[pl.ds(o, 1), :] + turned * sin_ref[pl.ds(o, 1), :]
            )
        return carry

    lax.fori_loop(0, 8, step, 0, unroll=True)
    for j in range(2):
        high, low = split(child_ref[:, :, pl.ds(j * 256, 256)].reshape(512, 256))
        part = jnp.dot(high, w_ref[...], preferred_element_type=f32)
        part = part[:, :LANES] + part[:, LANES:]
        part = part + jnp.dot(low, w_ref[:, :LANES], preferred_element_type=f32)
        o_ref[:, :, :, pl.ds(j * LANES, LANES)] = part.reshape(16, 4, 8, LANES)


def phase_tables(dir_index):
    theta_here = TP // 16
    theta_index = dir_index * theta_here + jnp.arange(theta_here, dtype=jnp.int32)
    polar = (theta_index.astype(f32) + 0.5) * (jnp.pi / TP)
    azimuth = jnp.arange(PP, dtype=f32) * (2.0 * jnp.pi / PP)
    along_x = (jnp.sin(polar)[:, None] * jnp.cos(azimuth)[None, :]).reshape(1, 512)
    along_y = (jnp.sin(polar)[:, None] * jnp.sin(azimuth)[None, :]).reshape(1, 512)
    along_z = (jnp.cos(polar)[:, None] + 0.0 * azimuth[None, :]).reshape(1, 512)
    octant = jnp.arange(8, dtype=jnp.int32)[:, None]
    sign_x = (2 * (octant % 2) - 1).astype(f32)
    sign_y = (2 * (octant // 2 % 2) - 1).astype(f32)
    sign_z = (2 * (octant // 4) - 1).astype(f32)
    angle = wave_shift * (sign_x * along_x + sign_y * along_y + sign_z * along_z)
    return jnp.cos(angle), jnp.sin(angle)


vmem = pl.BlockSpec(memory_space=pltpu.VMEM)
smem = pl.BlockSpec(memory_space=pltpu.SMEM)
hbm = pl.BlockSpec(memory_space=pltpu.HBM)


def shape(*dims):
    return jax.ShapeDtypeStruct(dims, f32)


def near(*dims):
    return pltpu.VMEM(dims, f32)


def grant(mib):
    return pltpu.CompilerParams(vmem_limit_bytes=mib << 20)


def far(x):
    return pltpu.with_memory_space_constraint(x, pltpu.HBM)


def hold(x):
    return pltpu.with_memory_space_constraint(x, pltpu.VMEM)


def body(outgoing, fine_slot, translator, list_partner, list_kind, list_count):
    box_index = lax.axis_index("box")
    dir_index = lax.axis_index("dir")
    chunk = box_index % 16
    group = box_index // 16

    theta = theta_matrix()
    up = jnp.asarray(parity_table(theta))
    down = jnp.asarray(parity_table(theta.T * (TF / TP)))
    phi = phi_matrix()
    high, low = split_constant(np.kron(np.eye(2), phi.T))
    phi_up = jnp.asarray(np.concatenate([high, high, low], 0))
    high, low = split_constant(np.kron(np.eye(2), phi) * (PF / PP))
    phi_down = jnp.asarray(np.concatenate([high, low], 1))

    sent = pl.pallas_call(
        theta_up_kernel,
        out_shape=pltpu.HBM((16, 4, 8, 256), f32),
        in_specs=[hbm, hbm],
        out_specs=hbm,
        scratch_shapes=[
            pltpu.VMEM((4, 8, TF * PF), f32),
            pltpu.VMEM((16, 32, LANES), f32),
            pltpu.VMEM((16, 4, 8, 256), f32),
            pltpu.VMEM((4, 8, 2, 8, LANES), f32),
            pltpu.SemaphoreType.DMA((4,)),
            pltpu.SemaphoreType.DMA((8,)),
            pltpu.SemaphoreType.DMA((16,)),
        ],
        compiler_params=grant(8),
    )(far(outgoing), far(up))
    spread = lax.all_to_all(sent, "dir", split_axis=0, concat_axis=0, tiled=True)

    rows = lax.dynamic_slice_in_dim(list_partner, group * TARGETS, TARGETS, 0)
    kinds = lax.dynamic_slice_in_dim(list_kind, group * TARGETS, TARGETS, 0)
    count = lax.dynamic_slice_in_dim(list_count, group * TARGETS, TARGETS, 0)
    length = rows.shape[1]
    live = jnp.arange(length, dtype=jnp.int32)[None, :] < count[:, None]
    pad = ((0, 0), (0, SLOTS - length))
    rows = jnp.pad(jnp.where(live, rows, -1), pad, constant_values=-1)
    kinds = jnp.pad(kinds, pad, constant_values=-1)
    kinds = kinds.reshape(TARGETS // 8, 8, SLOTS).transpose(0, 2, 1)
    cos_table, sin_table = phase_tables(dir_index)
    place = jnp.arange(64, dtype=jnp.int32)
    found = fine_slot[None, :] % 64 == place[:, None]
    inverse = jnp.sum(jnp.where(found, place[None, :], 0), 1)
    inverse = jnp.concatenate([inverse, jnp.full((8,), chunk, jnp.int32)])
    matrix, token = pl.pallas_call(
        matrix_kernel,
        grid=(TARGETS // 8,),
        in_specs=[
            pl.BlockSpec((8, SLOTS), lambda i: (i, 0)),
            pl.BlockSpec((1, SLOTS, 8), lambda i: (i, 0, 0)),
            smem,
            hbm,
            vmem,
            vmem,
        ],
        out_specs=[pl.BlockSpec((8, LANES, LANES), lambda i: (i, 0, 0)), vmem],
        out_shape=[pltpu.HBM((TARGETS, LANES, LANES), f32), near(8, LANES)],
        scratch_shapes=[
            pltpu.VMEM((KINDS, 256), bf16),
            pltpu.VMEM((8 * SLOTS, LANES), bf16),
            pltpu.VMEM((TABLE_ROWS, 2, LANES), f32),
            pltpu.VMEM((2 * KINDS, LANES), f32),
            pltpu.SemaphoreType.DMA,
        ],
        compiler_params=grant(16),
    )(rows, kinds, inverse, far(translator), hold(cos_table), hold(sin_table))

    packed = pl.pallas_call(
        gather_kernel,
        out_shape=near(32 * 16, LANES),
        in_specs=[smem, vmem, vmem, vmem, vmem, vmem],
        out_specs=vmem,
        scratch_shapes=[
            pltpu.VMEM((64, 8, 512), f32),
            pltpu.VMEM((8, 8, 512), f32),
        ],
        compiler_params=grant(16),
    )(inverse, hold(spread), hold(phi_up), hold(cos_table), hold(sin_table), hold(token))
    everyone = lax.all_to_all(packed, "box", split_axis=0, concat_axis=0, tiled=True)
    incoming = pl.pallas_call(
        translate_kernel,
        in_specs=[vmem, hbm],
        out_specs=vmem,
        out_shape=near(16, 2, 8, LANES),
        scratch_shapes=[
            pltpu.VMEM((16, 6, 8, LANES), f32),
            pltpu.VMEM((TARGETS, LANES, LANES), f32),
            pltpu.VMEM((TARGETS // 4, 4, 6, 8, LANES), f32),
            pltpu.SemaphoreType.DMA((TARGETS // 8,)),
        ],
        compiler_params=grant(16),
    )(hold(everyone), far(matrix))
    groups = [[16 * g + k for k in range(16)] for g in range(2)]
    fields = lax.all_to_all(
        incoming, "box", split_axis=0, concat_axis=0, axis_index_groups=groups, tiled=True
    )
    lowered = pl.pallas_call(
        scatter_kernel,
        out_shape=near(16, 4, 8, 256),
        in_specs=[smem, vmem, vmem, vmem, vmem],
        out_specs=vmem,
        scratch_shapes=[
            pltpu.VMEM((8, 8, 512), f32),
            pltpu.VMEM((64, 8, 512), f32),
        ],
        compiler_params=grant(16),
    )(inverse, hold(fields), hold(phi_down), hold(cos_table), hold(sin_table))
    back = lax.all_to_all(lowered, "dir", split_axis=0, concat_axis=0, tiled=True)
    return pl.pallas_call(
        theta_down_kernel,
        out_shape=shape(4, 8, TF * PF),
        in_specs=[vmem, vmem],
        out_specs=hbm,
        scratch_shapes=[
            pltpu.VMEM((4, 8, TF * PF), f32),
            pltpu.VMEM((4, 16, 2, 8, LANES), f32),
            pltpu.SemaphoreType.DMA((16,)),
        ],
        compiler_params=grant(8),
    )(hold(back), hold(down))


def solution(mesh):
    placed = (P(("box", "dir"), None, None), P("box"), P(None, None, "dir"), P(), P(), P())
    return jax.shard_map(
        body, mesh=mesh, in_specs=placed, out_specs=P(("box", "dir"), None, None), check_vma=False
    )
```
